32 devices in a mesh: fsdp: 16 (over z, y, x), dp: 2 (over core).
Axes of the slice: x: 2, y: 2, z: 4, core: 2. Of those that a mesh axis runs over, the one named last changes fastest.
Arguments:
- tokens: bfloat16 [32768, 768], P(('fsdp', 'dp')), may hold values from -6 to 6
- cotangent: bfloat16 [32768, 768], P(('fsdp', 'dp')), may hold values from -6 to 6
- lengths: int32 [64], P(('fsdp', 'dp')), may hold values from 32 to 512, as said below
- adam_step: int32 [1], replicated, may hold values from 1 to 64
- learn_rate: float32 [1], replicated, may hold values from 0.1 to 0.4
- attn_w: float32 [768, 3072], P('fsdp')
- attn_m: float32 [768, 3072], P('fsdp'), may hold values from -6 to 6
- attn_v: float32 [768, 3072], P('fsdp'), may hold values from 0.5 to 5
- ffn_w: float32 [768, 6144], P('fsdp')
- ffn_m: float32 [768, 6144], P('fsdp'), may hold values from -6 to 6
- ffn_v: float32 [768, 6144], P('fsdp'), may hold values from 0.5 to 5
- vecs: float32 [768, 8], P('fsdp')
- vecs_m: float32 [768, 8], P('fsdp'), may hold values from -6 to 6
- vecs_v: float32 [768, 8], P('fsdp'), may hold values from 0.5 to 5
- b_ff: float32 [3072], P('fsdp'), may hold values from -2 to 2
- bff_m: float32 [3072], P('fsdp'), may hold values from -6 to 6
- bff_v: float32 [3072], P('fsdp'), may hold values from 0.5 to 5
Outputs:
- outputs: bfloat16 [32768, 768], P(('fsdp', 'dp'))
- input_grad: float32 [32768, 768], P(('fsdp', 'dp'))
- attn_grad: float32 [768, 3072], P('fsdp')
- attn_m_new: float32 [768, 3072], P('fsdp')
- attn_v_new: float32 [768, 3072], P('fsdp')
- attn_w_new: float32 [768, 3072], P('fsdp')
- attn_w_copy: bfloat16 [768, 3072], P('fsdp')
- ffn_grad: float32 [768, 6144], P('fsdp')
- ffn_m_new: float32 [768, 6144], P('fsdp')
- ffn_v_new: float32 [768, 6144], P('fsdp')
- ffn_w_new: float32 [768, 6144], P('fsdp')
- ffn_w_copy: bfloat16 [768, 6144], P('fsdp')
- vecs_grad: float32 [768, 8], P('fsdp')
- vecs_m_new: float32 [768, 8], P('fsdp')
- vecs_v_new: float32 [768, 8], P('fsdp')
- vecs_new: float32 [768, 8], P('fsdp')
- vecs_copy: bfloat16 [768, 8], P('fsdp')
- bff_grad: float32 [3072], P('fsdp')
- bff_m_new: float32 [3072], P('fsdp')
- bff_v_new: float32 [3072], P('fsdp')
- bff_new: float32 [3072], P('fsdp')
- bff_copy: bfloat16 [3072], P('fsdp')
The draws below stay inside these ranges and needn't reach their ends.
Inputs may be any that keep to these rules, and one draw needn't show every extreme that they name: A slot's sequence fills its first lengths tokens; the first slot of all holds 512 tokens; lengths vary from slot to slot (some may repeat), so devices generally hold differing token counts.
All inputs are finite; a program needn't handle non-finite values.
Results may differ from the reference program's by a relative error of at most 0.025.
The reference program's roundings to bfloat16 on the way count: a program that leaves them out, or rounds other values in their place, can miss the bound.
Values may be sent and summed in bfloat16 or wider, within the bound.
A program may use at most 192 MiB of HBM per device.

```python
import math
import jax
import jax.numpy as jnp
from jax import lax

D = 768
HEADS = 12
HEAD = 64
FF = 3072
LMAX = 512
LMIN = 32
SLOTS = 64
ROWS = 32768


def draw_lengths(key, part):
    span_len = LMAX - LMIN
    first_key, second_key = jax.random.split(jax.random.fold_in(key, 11))
    first_pick = jax.random.randint(first_key, (SLOTS,), 0, span_len + 1)
    second_pick = jax.random.randint(second_key, (SLOTS,), span_len // 2, span_len + 1)
    drawn = LMIN + first_pick * second_pick // span_len
    return drawn.at[0].set(LMAX).astype(jnp.int32)


def draw_attn_w(key, part):
    values_drawn = jax.random.normal(jax.random.fold_in(key, 21), (D, 4 * D), jnp.float32)
    column_scale = jnp.where(jnp.arange(4 * D) < 3 * D, 1.0, 6.0) * D ** (-0.5)
    return values_drawn * column_scale[None, :]


def draw_ffn_w(key, part):
    values_drawn = jax.random.normal(jax.random.fold_in(key, 31), (D, 2 * FF), jnp.float32)
    column_scale = jnp.where(jnp.arange(2 * FF) < FF, D ** (-0.5), FF ** (-0.5))
    return values_drawn * column_scale[None, :]


def draw_vecs(key, part):
    bias_key, gain_key = jax.random.split(jax.random.fold_in(key, 41))
    biases = 0.3 * jax.random.normal(bias_key, (D, 8), jnp.float32)
    gains = jax.random.uniform(gain_key, (D, 8), jnp.float32, 0.6, 1.4)
    column_ids = jnp.arange(8)
    is_gain = (column_ids == 3) | (column_ids == 6)
    return jnp.where(is_gain[None, :], gains, biases)


def block_scale(stream_key, shape, cuts, smallest, largest):
    def one(dim, shards_of):
        draws = jax.random.uniform(jax.random.fold_in(jax.random.fold_in(stream_key, 6), dim), (shards_of,), jnp.float32, smallest / len(cuts), largest / len(cuts))
        return jnp.repeat(jnp.exp(draws), shape[dim] // shards_of).reshape((-1,) + (1,) * (len(shape) - dim - 1))

    level = one(*cuts[0])
    for cut in cuts[1:]:
        level = level * one(*cut)
    return level


def bell_draw(key, extent, width, most, cuts=(), kind=jnp.bfloat16):
    values = jax.random.normal(key, extent, jnp.float32) * width
    if len(cuts) > 0:
        values = block_scale(key, extent, cuts, -0.22, 0.18) * values
    return jnp.clip(values, min=-most, max=most).astype(kind)


def setup_inputs(seed: int = 0) -> dict:
    arg_keys = jax.random.split(jax.random.key(seed), 18)
    tokens = bell_draw(arg_keys[0], (ROWS, D), 1.0, 6.0, ((0, 32),))
    cotangent = bell_draw(arg_keys[1], (ROWS, D), 1.0, 6.0, ((0, 32),))
    lengths = draw_lengths(jax.random.fold_in(arg_keys[17], 71), 0)
    adam_step = jax.random.randint(arg_keys[3], (1,), 1, 65).astype(jnp.int32)
    learn_rate = jnp.clip(jnp.exp(jax.random.uniform(arg_keys[4], (1,), jnp.float32, math.log(0.1), math.log(0.4))), 0.1, 0.4)
    attn_w = draw_attn_w(jax.random.fold_in(arg_keys[17], 71), 0)
    attn_m = bell_draw(arg_keys[6], (D, 4 * D), 1.0, 6.0, ((0, 16),), jnp.float32)
    attn_v = jnp.clip(jnp.exp(math.log(5.0) - 2.3025851 * jax.random.uniform(arg_keys[7], (D, 4 * D), jnp.float32) ** block_scale(arg_keys[7], (D, 4 * D), ((0, 16),), -0.2, 0.2)), 0.5, 5.0)
    ffn_w = draw_ffn_w(jax.random.fold_in(arg_keys[17], 71), 0)
    ffn_m = bell_draw(arg_keys[9], (D, 2 * FF), 1.0, 6.0, ((0, 16),), jnp.float32)
    ffn_v = jnp.clip(jnp.exp(math.log(5.0) - 2.3025851 * jax.random.uniform(arg_keys[10], (D, 2 * FF), jnp.float32) ** block_scale(arg_keys[10], (D, 2 * FF), ((0, 16),), -0.2, 0.2)), 0.5, 5.0)
    vecs = draw_vecs(jax.random.fold_in(arg_keys[17], 71), 0)
    vecs_m = bell_draw(arg_keys[12], (D, 8), 1.0, 6.0, ((0, 16),), jnp.float32)
    vecs_v = jnp.clip(jnp.exp(math.log(5.0) - 2.3025851 * jax.random.uniform(arg_keys[13], (D, 8), jnp.float32) ** block_scale(arg_keys[13], (D, 8), ((0, 16),), -0.2, 0.2)), 0.5, 5.0)
    b_ff = bell_draw(arg_keys[14], (FF,), 0.3, 2.0, ((0, 16),), jnp.float32)
    bff_m = bell_draw(arg_keys[15], (FF,), 1.0, 6.0, ((0, 16),), jnp.float32)
    bff_v = jnp.clip(jnp.exp(math.log(5.0) - 2.3025851 * jax.random.uniform(arg_keys[16], (FF,), jnp.float32) ** block_scale(arg_keys[16], (FF,), ((0, 16),), -0.2, 0.2)), 0.5, 5.0)
    return {"tokens": tokens, "cotangent": cotangent, "lengths": lengths, "adam_step": adam_step, "learn_rate": learn_rate, "attn_w": attn_w, "attn_m": attn_m, "attn_v": attn_v, "ffn_w": ffn_w, "ffn_m": ffn_m, "ffn_v": ffn_v, "vecs": vecs, "vecs_m": vecs_m, "vecs_v": vecs_v, "b_ff": b_ff, "bff_m": bff_m, "bff_v": bff_v}


@jax.custom_vjp
def low(v):
    return lax.optimization_barrier(v.astype(jnp.bfloat16)).astype(jnp.float32)

@jax.custom_vjp
def low_back(v):
    return v

def low_keep(v):
    return (low(v), None)

def low_pass(kept, grad):
    return (grad,)

def back_keep(v):
    return (v, None)

def back_low(kept, grad):
    return (low(grad),)
low.defvjp(low_keep, low_pass)
low_back.defvjp(back_keep, back_low)
PRECISE = lax.Precision.HIGHEST
NORM_EPSILON = 1e-05

def matmul(left, right):
    return jnp.dot(left, right, precision=PRECISE, preferred_element_type=jnp.float32)

def layer_norm(resid, gain, shift):
    centre = resid - lax.optimization_barrier(jnp.mean(resid, axis=-1, keepdims=True))
    spread = lax.optimization_barrier(jnp.mean(centre * centre, axis=-1, keepdims=True))
    return centre * lax.rsqrt(spread + NORM_EPSILON) * gain + shift

def attend_slot(pieces):
    queries, keys_all, values_all, length = pieces
    query_heads = queries.reshape(LMAX, HEADS, HEAD)
    key_heads = keys_all.reshape(LMAX, HEADS, HEAD)
    value_heads = values_all.reshape(LMAX, HEADS, HEAD)
    scores = low_back(jnp.einsum('qhd,khd->hqk', query_heads, key_heads, precision=PRECISE) * HEAD ** (-0.5))
    key_keep = jnp.arange(LMAX, dtype=jnp.int32) < length
    scores = jnp.where(key_keep[None, None, :], scores, -1e+30)
    weights_soft = jax.nn.softmax(scores, axis=-1)
    mixed_heads = jnp.einsum('hqk,khd->qhd', low(weights_soft), value_heads, precision=PRECISE)
    return mixed_heads.reshape(LMAX, HEADS * HEAD)

def forward_group(tokens_f, attn_master, ffn_master, vec_master, bias_master, group_lengths):
    slot_count = group_lengths.shape[0]
    attn_low = low(attn_master)
    ffn_low = low(ffn_master)
    vec_low = low(vec_master)
    bias_low = low(bias_master)
    projected = matmul(tokens_f, attn_low[:, :3 * D])
    queries = low(low_back(projected[:, :D] + vec_low[:, 0]))
    keys_all = low(low_back(projected[:, D:2 * D]))
    values_all = low(low_back(projected[:, 2 * D:3 * D] + vec_low[:, 1]))
    slot_shape = (slot_count, LMAX, D)
    mixed_all = lax.map(jax.checkpoint(attend_slot), (queries.reshape(slot_shape), keys_all.reshape(slot_shape), values_all.reshape(slot_shape), group_lengths))
    mixed_all = low(low_back(mixed_all.reshape(slot_count * LMAX, D)))
    branch = low_back(matmul(mixed_all, attn_low[:, 3 * D:]) + vec_low[:, 2])
    hidden = layer_norm(tokens_f + branch, vec_low[:, 3], vec_low[:, 4])
    inner_pre = low_back(matmul(low(hidden), ffn_low[:, :FF]) + bias_low)
    activated = low(jax.nn.gelu(inner_pre, approximate=False))
    outer_pre = low_back(matmul(activated, ffn_low[:, FF:].T) + vec_low[:, 5])
    normed = layer_norm(hidden + outer_pre, vec_low[:, 6], vec_low[:, 7])
    row_keep = (jnp.arange(LMAX, dtype=jnp.int32)[None, :] < group_lengths[:, None]).reshape(-1)
    return jnp.where(row_keep[:, None], normed, 0.0)

def adam_update(gradient, moment, second, master, adam_step, learn_rate):
    count = adam_step[0].astype(jnp.float32)
    moment_new = 0.9 * moment + 0.1 * gradient
    second_new = 0.98 * second + 0.02 * gradient * gradient
    first_fix = moment_new / (1.0 - jnp.power(0.9, count))
    second_fix = second_new / (1.0 - jnp.power(0.98, count))
    master_new = master - learn_rate[0] * (first_fix / (jnp.sqrt(second_fix) + 1e-06) + 0.01 * master)
    return (moment_new, second_new, master_new, master_new.astype(jnp.bfloat16))

def reference(tokens, cotangent, lengths, adam_step, learn_rate, attn_w, attn_m, attn_v, ffn_w, ffn_m, ffn_v, vecs, vecs_m, vecs_v, b_ff, bff_m, bff_v):
    group_slots = 8
    groups = SLOTS // group_slots
    token_groups = tokens.astype(jnp.float32).reshape(groups, group_slots * LMAX, D)
    cot_groups = cotangent.astype(jnp.float32).reshape(groups, group_slots * LMAX, D)
    length_groups = lengths.reshape(groups, group_slots)

    def one_group(running, pieces):
        tok_group, cot_group, len_group = pieces

        def forward(tok_f, attn_f, ffn_f, vec_f, bias_f):
            return forward_group(tok_f, attn_f, ffn_f, vec_f, bias_f, len_group)
        result, pullback = jax.vjp(forward, tok_group, attn_w, ffn_w, vecs, b_ff)
        gradients = pullback(cot_group)
        running = tuple((summed + part_grad for summed, part_grad in zip(running, gradients[1:])))
        return (running, (result, gradients[0]))
    initial = (jnp.zeros_like(attn_w), jnp.zeros_like(ffn_w), jnp.zeros_like(vecs), jnp.zeros_like(b_ff))
    totals, (results, input_grads) = lax.scan(one_group, initial, (token_groups, cot_groups, length_groups))
    outputs = results.reshape(ROWS, D).astype(jnp.bfloat16)
    input_grad = input_grads.reshape(ROWS, D)
    attn_new = adam_update(totals[0], attn_m, attn_v, attn_w, adam_step, learn_rate)
    ffn_new = adam_update(totals[1], ffn_m, ffn_v, ffn_w, adam_step, learn_rate)
    vecs_new = adam_update(totals[2], vecs_m, vecs_v, vecs, adam_step, learn_rate)
    bff_new = adam_update(totals[3], bff_m, bff_v, b_ff, adam_step, learn_rate)
    return (outputs, input_grad, totals[0], attn_new[0], attn_new[1], attn_new[2], attn_new[3], totals[1], ffn_new[0], ffn_new[1], ffn_new[2], ffn_new[3], totals[2], vecs_new[0], vecs_new[1], vecs_new[2], vecs_new[3], totals[3], bff_new[0], bff_new[1], bff_new[2], bff_new[3])
```

```python
import functools

import jax
import jax.numpy as jnp
from jax import lax
from jax.experimental import pallas as pl
from jax.experimental.pallas import tpu as pltpu
from jax.sharding import PartitionSpec as P

MESH = pl.DeviceIdType.MESH


def place(na):
    me = lax.axis_index("fsdp"); p = lax.axis_index("dp")
    a = me // 4; b = (me // 2) % 2; c = me % 2
    par = p % 2
    f2 = lambda aa, bb, cc: (aa, bb + (1 - 2*bb)*(1 - par), cc + (1 - 2*cc)*par)
    f3 = lambda aa, bb, cc: (aa, bb + (1 - 2*bb)*par, cc + (1 - 2*cc)*(1 - par))
    idx = lambda t: (t[0]*2 + t[1])*2 + t[2]
    return me, p, (a, b, c), f2, f3, idx

def barrier_all(na, ndp):
    me, p, (a, b, c), f2, f3, idx = place(na)
    sem = pltpu.get_barrier_semaphore()
    n = 0
    def sig(f, q):
        pl.semaphore_signal(sem, inc=1, device_id=(f, q), device_id_type=MESH)
    for k in range(1, na):
        sig(idx(((a + k) % na, b, c)), p); n += 1
    sig(idx(f2(a, b, c)), p); n += 1
    sig(idx(f3(a, b, c)), p); n += 1
    for k in range(1, ndp):
        sig(me, (p + k) % ndp); n += 1
    pl.semaphore_wait(sem, n)

def ag_kernel(na, ndp, *refs):
    narr = 2
    shards = refs[:narr]; ex = refs[narr]; outs = refs[narr+1:2*narr+1]; exo = refs[2*narr+1]
    scr = refs[2*narr+2:]
    me, p, (a, b, c), f2, f3, idx = place(na)
    barrier_all(na, ndp)
    casts = scr[:narr]; lsem = scr[narr]; sems = scr[narr+1:]
    xss, xrs = sems[2*narr], sems[2*narr+1]
    exo[me] = ex[...].astype(jnp.bfloat16).astype(jnp.float32)
    pend = []
    locs = []
    st = []
    for i in range(narr):
        C = shards[i].shape[1]; w = C // ndp
        casts[i][...] = shards[i][...].astype(jnp.bfloat16)
        loc = pltpu.make_async_copy(casts[i], outs[i].at[me], lsem.at[i])
        loc.start(); locs.append(loc)
        ssem, rsem = sems[2*i], sems[2*i+1]
        cols = pl.ds(pl.multiple_of(p*w, 128), w)
        def rc(src, f, dst_dev, j, i=i, cols=cols, ssem=ssem, rsem=rsem):
            return pltpu.make_async_remote_copy(src_ref=src, dst_ref=outs[i].at[f, :, cols],
                send_sem=ssem.at[j], recv_sem=rsem.at[j], device_id=dst_dev, device_id_type=MESH)
        own = casts[i].at[:, cols]
        st.append((rc, own, cols))
    NS = (na - 1) + na + 2*na + (ndp - 1)*(4*na - 1)
    p2 = idx(f2(a, b, c)); p3 = idx(f3(a, b, c))
    sends = []
    recvs = [dict() for _ in range(narr)]
    def send(i, src, f, dev, j):
        d = st[i][0](src, f, dev, j); d.start(); sends.append(d)
    def wait(i, f, j):
        d = st[i][0](outs[i].at[f, :, st[i][2]], f, (me, p), j); d.wait_recv()
    J2 = na - 1; J3 = J2 + na; JD = J3 + 2*na
    def xsend(f, dev, j):
        d = pltpu.make_async_remote_copy(src_ref=exo.at[f], dst_ref=exo.at[f], send_sem=xss.at[j], recv_sem=xrs.at[j], device_id=dev, device_id_type=MESH)
        d.start(); sends.append(d)
    def xwait(f, j):
        pltpu.make_async_remote_copy(src_ref=exo.at[f], dst_ref=exo.at[f], send_sem=xss.at[j], recv_sem=xrs.at[j], device_id=(me, p), device_id_type=MESH).wait_recv()
    for k in range(1, na):
        xsend(me, (idx(((a + k) % na, b, c)), p), k - 1)
    xsend(me, (p2, p), J2)
    xsend(me, (p3, p), J3)
    for i in range(narr):
        for k in range(1, na):
            send(i, st[i][1], me, (idx(((a + k) % na, b, c)), p), k - 1)
        send(i, st[i][1], me, (p2, p), J2)
        send(i, st[i][1], me, (p3, p), J3)
    for i in range(narr):
        at = lambda f, i=i: outs[i].at[f, :, st[i][2]]
        def dp(f, m):
            for q in range(1, ndp):
                send(i, at(f), f, (me, (p + q) % ndp), JD + (q-1)*(4*na-1) + m)
        A = [(a + na - k) % na for k in range(na)]
        own = [idx((A[k], b, c)) for k in range(na)]
        col2 = [idx(f2(A[k], b, c)) for k in range(na)]
        col3 = [idx(f3(A[k], b, c)) for k in range(na)]
        t = f2(a, b, c)
        col23 = [idx(f3(A[k], t[1], t[2])) for k in range(na)]
        for k in range(na):
            if k > 0:
                wait(i, own[k], k - 1)
                if i == 0:
                    xwait(own[k], k - 1)
                    xsend(own[k], (p2, p), J2 + k)
                    xsend(own[k], (p3, p), J3 + k)
                send(i, at(own[k]), own[k], (p2, p), J2 + k)
                send(i, at(own[k]), own[k], (p3, p), J3 + k)
                dp(own[k], k - 1)
            wait(i, col2[k], J2 + k)
            if i == 0:
                xwait(col2[k], J2 + k)
                xsend(col2[k], (p3, p), J3 + na + k)
            send(i, at(col2[k]), col2[k], (p3, p), J3 + na + k)
            dp(col2[k], na - 1 + k)
            wait(i, col3[k], J3 + k)
            if i == 0: xwait(col3[k], J3 + k)
            dp(col3[k], 2*na - 1 + k)
        for k in range(na):
            wait(i, col23[k], J3 + na + k)
            if i == 0: xwait(col23[k], J3 + na + k)
            dp(col23[k], 3*na - 1 + k)
    for i in range(narr):
        w = st[i][2].size
        for q in range(1, ndp):
            src_p = (p + ndp - q) % ndp
            for m in range(4*na - 1):
                cols = pl.ds(pl.multiple_of(src_p*w, 128), w)
                rsem = sems[2*i+1]; ssem = sems[2*i]
                j = JD + (q-1)*(4*na-1) + m
                r = outs[i].at[me, :, cols]
                pltpu.make_async_remote_copy(src_ref=r, dst_ref=r, send_sem=ssem.at[j], recv_sem=rsem.at[j], device_id=(me, p), device_id_type=MESH).wait_recv()
    for d in sends: d.wait_send()
    for l in locs: l.wait()

def all_gather(mesh_shape, shards, ex, cid):
    F, ndp = mesh_shape
    na = F // 4
    NS = (na - 1) + na + 2*na + (ndp - 1)*(4*na - 1)
    scr = [pltpu.VMEM(s.shape, jnp.bfloat16) for s in shards] + [pltpu.SemaphoreType.DMA((len(shards),))]
    for s in list(shards) + [ex]:
        scr += [pltpu.SemaphoreType.DMA((NS,)), pltpu.SemaphoreType.DMA((NS,))]
    V = pl.BlockSpec(memory_space=pltpu.VMEM)
    return pl.pallas_call(
        functools.partial(ag_kernel, na, ndp),
        out_shape=[jax.ShapeDtypeStruct((F,) + s.shape, jnp.bfloat16) for s in shards] + [jax.ShapeDtypeStruct((F,) + ex.shape, jnp.float32)],
        in_specs=[V]*(len(shards) + 1),
        out_specs=[pl.BlockSpec(memory_space=pl.ANY)]*len(shards) + [V],
        scratch_shapes=scr,
        compiler_params=pltpu.CompilerParams(collective_id=cid, has_side_effects=True),
    )(*shards, ex)

def rs_kernel(na, ndp, narr, *refs):
    grads = refs[:narr]; ex = refs[narr]
    outs = refs[narr+1:2*narr+1]; exo = refs[2*narr+1]
    scr = refs[2*narr+2:]
    me, p, (a, b, c), f2, f3, idx = place(na)
    barrier_all(na, ndp)
    exb, exs, exr = scr[0:3]
    lsem = scr[3]
    bufs = [scr[4+7*i:4+7*i+7] for i in range(narr)]
    t2 = f2(a, b, c); t3 = f3(a, b, c); p2 = idx(t2); p3 = idx(t3)
    t23 = f2(*t3)
    R = grads[0].shape[1]
    sends = []; locs = []
    def rc(src, dst, ss, rs, dev):
        return pltpu.make_async_remote_copy(src_ref=src, dst_ref=dst, send_sem=ss, recv_sem=rs, device_id=dev, device_id_type=MESH)
    def start(*x):
        d = rc(*x); d.start(); sends.append(d)
    def waitr(dst, rs):
        rc(dst, dst, rs, rs, (me, p)).wait_recv()
    order_a = [(a + 1 + k) % na for k in range(na)]
    def shard(aa, flip2, flip3):
        t = (aa, b, c)
        if flip2: t = f2(*t)
        if flip3: t = f3(*t)
        return idx(t)
    seq = [(k, 1, 1) for k in range(na)] + [(k, 0, 1) for k in range(na)] + [(k, 1, 0) for k in range(na)] + [(k, 0, 0) for k in range(na)]
    for i in range(narr):
        own, rD, r3, r2, r1, ss, rs = bufs[i]
        w = grads[i].shape[2] // ndp
        cols = pl.ds(pl.multiple_of(p*w, 128), w)
        for m, (k, y2, y3) in enumerate(seq):
            for q in range(1, ndp):
                f = shard(order_a[k], y2, y3) if q % 2 == 0 else shard(order_a[k], y3, y2)
                dq = (p + q) % ndp
                qc = pl.ds(pl.multiple_of(dq*w, 128), w)
                start(grads[i].at[f, :, qc], rD.at[q-1, f], ss.at[(q-1)*4*na + m], rs.at[(q-1)*4*na + f], (me, dq))
        l = pltpu.make_async_copy(grads[i].at[:, :, cols], own, lsem.at[i])
        l.start(); locs.append(l)
    NX = (ndp - 1) + 2 + (na - 1)
    xs, xr = scr[4+7*narr], scr[4+7*narr+1]
    exb[...] = ex[...]
    for q in range(1, ndp):
        start(exb, exr.at[q-1], xs.at[q-1], xr.at[q-1], (me, (p + q) % ndp))
    def add_into(i, f, srcs, dst):
        own = bufs[i][0]
        w = own.shape[2]; CH = 512 if w % 512 == 0 else (384 if w % 384 == 0 else 128)
        def body(j, _):
            s = pl.ds(pl.multiple_of(j*CH, 128), CH)
            v = own[f, :, s].astype(jnp.float32)
            for r in srcs:
                v = v + r[:, s].astype(jnp.float32)
            dst[:, s] = v.astype(dst.dtype)
            return 0
        lax.fori_loop(0, w // CH, body, 0)
    B2 = (ndp - 1)*4*na
    B3 = B2 + 2*na; B1 = B3 + na
    for l in locs: l.wait()
    def wD(i, f):
        for q in range(1, ndp):
            waitr(bufs[i][1].at[q-1, f], bufs[i][6].at[(q-1)*4*na + f])
        return [bufs[i][1].at[q-1, f] for q in range(1, ndp)]
    par = p % 2
    bit2 = b*(1 - par) + c*par
    for i in range(narr):
        own, rD, r3, r2, r1, ss, rs = bufs[i]
        for x2 in (1, 0):
            for k in range(na):
                f = shard(order_a[k], x2, 1)
                srcs = wD(i, f)
                add_into(i, f, srcs, own.at[f])
                b2 = bit2 + (1 - 2*bit2)*x2
                slot = order_a[k]*2 + b2
                m = (1 - x2)*na + k
                start(own.at[f], r3.at[slot], ss.at[B2 + m], rs.at[B2 + slot], (p3, p))
    for i in range(narr):
        own, rD, r3, r2, r1, ss, rs = bufs[i]
        for k in range(na):
            f = shard(order_a[k], 1, 0)
            slot = order_a[k]*2 + (1 - bit2)
            srcs = wD(i, f)
            waitr(r3.at[slot], rs.at[B2 + slot])
            add_into(i, f, srcs + [r3.at[slot]], own.at[f])
            start(own.at[f], r2.at[order_a[k]], ss.at[B3 + k], rs.at[B3 + order_a[k]], (p2, p))
    for i in range(narr):
        own, rD, r3, r2, r1, ss, rs = bufs[i]
        for k in range(na - 1):
            f = shard(order_a[k], 0, 0)
            slot = order_a[k]*2 + bit2
            srcs = wD(i, f)
            waitr(r3.at[slot], rs.at[B2 + slot])
            waitr(r2.at[order_a[k]], rs.at[B3 + order_a[k]])
            add_into(i, f, srcs + [r3.at[slot], r2.at[order_a[k]]], own.at[f])
            start(own.at[f], r1.at[k], ss.at[B1 + k], rs.at[B1 + k], (f, p))
    for q in range(1, ndp):
        waitr(exr.at[q-1], xr.at[q-1])
    def exsum(n0, n):
        v = exs[0]
    if ndp == 2:
        exs[0] = exb[...] + exr[0]
    else:
        def pick(j):
            v = exb[...]
            for q in range(1, ndp):
                v = jnp.where((p + ndp - q) % ndp == j, exr[q-1], v)
            return v
        v = pick(0)
        for j in range(1, ndp): v = v + pick(j)
        exs[0] = v
    X2 = ndp - 1
    start(exs.at[0], exr.at[X2], xs.at[X2], xr.at[X2], (idx((a, b, 1 - c)), p))
    waitr(exr.at[X2], xr.at[X2])
    exs[1] = exs[0] + exr[X2]
    start(exs.at[1], exr.at[X2+1], xs.at[X2+1], xr.at[X2+1], (idx((a, 1 - b, c)), p))
    waitr(exr.at[X2+1], xr.at[X2+1])
    exs[2] = exs[1] + exr[X2+1]
    for k in range(1, na):
        start(exs.at[2], exr.at[X2+1+k], xs.at[X2+1+k], xr.at[X2+1+k], (idx(((a + k) % na, b, c)), p))
    for k in range(1, na):
        waitr(exr.at[X2+1+k], xr.at[X2+1+k])
    def picka(j):
        v = exs[2]
        for k in range(1, na):
            v = jnp.where((a + na - k) % na == j, exr[X2+1+k], v)
        return v
    v = picka(0)
    for j in range(1, na): v = v + picka(j)
    exo[...] = v
    B0 = B1 + na - 1
    for i in range(narr):
        own, rD, r3, r2, r1, ss, rs = bufs[i]
        w = own.shape[2]
        f = me
        slot = a*2 + bit2
        srcs = wD(i, f)
        waitr(r3.at[slot], rs.at[B2 + slot])
        waitr(r2.at[a], rs.at[B3 + a])
        for k in range(na - 1): waitr(r1.at[k], rs.at[B1 + k])
        cols = pl.ds(pl.multiple_of(p*w, 128), w)
        dst = outs[i].at[:, cols]
        add_into(i, f, srcs + [r3.at[slot], r2.at[a]] + [r1.at[k] for k in range(na - 1)], dst)
        for q in range(1, ndp):
            start(dst, dst, ss.at[B0 + q - 1], rs.at[B0 + q - 1], (me, (p + q) % ndp))
    for i in range(narr):
        own, rD, r3, r2, r1, ss, rs = bufs[i]
        w = own.shape[2]
        for q in range(1, ndp):
            src_p = (p + ndp - q) % ndp
            waitr(outs[i].at[:, pl.ds(pl.multiple_of(src_p*w, 128), w)], rs.at[B0 + q - 1])
    for d in sends: d.wait_send()

def reduce_scatter(mesh_shape, grads, ex, cid):
    F, ndp = mesh_shape
    na = F // 4
    narr = len(grads)
    NX = (ndp - 1) + 2 + (na - 1)
    scr = [pltpu.VMEM(ex.shape, jnp.float32), pltpu.VMEM((3,) + ex.shape, jnp.float32), pltpu.VMEM((NX,) + ex.shape, jnp.float32), pltpu.SemaphoreType.DMA((narr,))]
    for g in grads:
        w = g.shape[2] // ndp; R = g.shape[1]
        NS = (ndp - 1)*4*na + 2*na + na + na - 1 + ndp - 1
        scr += [pltpu.VMEM((F, R, w), jnp.bfloat16), pltpu.VMEM((ndp - 1, F, R, w), jnp.bfloat16), pltpu.VMEM((2*na, R, w), jnp.bfloat16),
                pltpu.VMEM((na, R, w), jnp.bfloat16), pltpu.VMEM((na - 1, R, w), jnp.bfloat16), pltpu.SemaphoreType.DMA((NS,)), pltpu.SemaphoreType.DMA((NS,))]
    scr += [pltpu.SemaphoreType.DMA((NX,)), pltpu.SemaphoreType.DMA((NX,))]
    V = pl.BlockSpec(memory_space=pltpu.VMEM)
    return pl.pallas_call(
        functools.partial(rs_kernel, na, ndp, narr),
        out_shape=[jax.ShapeDtypeStruct(g.shape[1:], jnp.float32) for g in grads] + [jax.ShapeDtypeStruct(ex.shape, jnp.float32)],
        in_specs=[pl.BlockSpec(memory_space=pl.ANY)]*narr + [V],
        out_specs=[V]*(narr + 1),
        scratch_shapes=scr,
        compiler_params=pltpu.CompilerParams(collective_id=cid, has_side_effects=True, vmem_limit_bytes=50 << 20),
    )(*grads, ex)


D = 768
HEADS = 12
HEAD = 64
FF = 3072
LMAX = 512


NORM_EPSILON = 1e-05
CONTRACT_ROWS = (((0,), (0,)), ((), ()))
CONTRACT_COLS = (((1,), (1,)), ((), ()))


def layer_norm(resid, gain, shift):
    centre = resid - jnp.mean(resid, axis=-1, keepdims=True)
    spread = jnp.mean(centre * centre, axis=-1, keepdims=True)
    return centre * lax.rsqrt(spread + NORM_EPSILON) * gain + shift


def exact_gelu(inner_pre):
    return jax.nn.gelu(inner_pre, approximate=False)


def slot_scores(queries, keys_all, key_keep):
    query_heads = queries.reshape(LMAX, HEADS, HEAD)
    key_heads = keys_all.reshape(LMAX, HEADS, HEAD)
    scores = jnp.einsum(
        "qhd,khd->hqk", query_heads, key_heads, preferred_element_type=jnp.float32
    ) * HEAD ** (-0.5)
    return jnp.where(key_keep[None, None, :], scores, -1e30)


def attend_forward(pieces):
    queries, keys_all, values_all, key_keep = pieces
    scores = slot_scores(queries, keys_all, key_keep)
    row_top = jnp.max(scores, axis=-1, keepdims=True)
    expo_scores = jnp.exp(scores - row_top)
    row_total = jnp.sum(expo_scores, axis=-1, keepdims=True)
    weights_low = (expo_scores / row_total).astype(jnp.bfloat16)
    value_heads = values_all.reshape(LMAX, HEADS, HEAD)
    mixed_heads = jnp.einsum(
        "hqk,khd->qhd", weights_low, value_heads, preferred_element_type=jnp.float32
    )
    return (mixed_heads.reshape(LMAX, HEADS * HEAD), (row_top + jnp.log(row_total))[..., 0])


def attend_backward(pieces):
    queries, keys_all, values_all, key_keep, log_total, grad_mixed = pieces
    scores = slot_scores(queries, keys_all, key_keep)
    probs_full = jnp.exp(scores - log_total[..., None])
    query_heads = queries.reshape(LMAX, HEADS, HEAD)
    key_heads = keys_all.reshape(LMAX, HEADS, HEAD)
    value_heads = values_all.reshape(LMAX, HEADS, HEAD)
    grad_heads = grad_mixed.reshape(LMAX, HEADS, HEAD)
    grad_values = jnp.einsum(
        "hqk,qhd->khd",
        probs_full.astype(jnp.bfloat16),
        grad_heads,
        preferred_element_type=jnp.float32,
    )
    grad_probs = jnp.einsum(
        "qhd,khd->hqk", grad_heads, value_heads, preferred_element_type=jnp.float32
    )
    grad_scores = probs_full * (
        grad_probs - jnp.sum(probs_full * grad_probs, axis=-1, keepdims=True)
    )
    grad_low = grad_scores.astype(jnp.bfloat16)
    grad_queries = jnp.einsum(
        "hqk,khd->qhd", grad_low, key_heads, preferred_element_type=jnp.float32
    ) * HEAD ** (-0.5)
    grad_keys = jnp.einsum(
        "hqk,qhd->khd", grad_low, query_heads, preferred_element_type=jnp.float32
    ) * HEAD ** (-0.5)
    return (
        grad_queries.reshape(LMAX, D).astype(jnp.bfloat16),
        grad_keys.reshape(LMAX, D).astype(jnp.bfloat16),
        grad_values.reshape(LMAX, D).astype(jnp.bfloat16),
    )


def adam_update(gradient, moment, second, master, adam_step, learn_rate):
    count = adam_step[0].astype(jnp.float32)
    moment_new = 0.9 * moment + 0.1 * gradient
    second_new = 0.98 * second + 0.02 * gradient * gradient
    first_fix = moment_new / (1.0 - jnp.power(0.9, count))
    second_fix = second_new / (1.0 - jnp.power(0.98, count))
    master_new = master - learn_rate[0] * (
        first_fix / (jnp.sqrt(second_fix) + 1e-06) + 0.01 * master
    )
    return (moment_new, second_new, master_new, master_new.astype(jnp.bfloat16))


def local(
    mesh_shape,
    tokens,
    cotangent,
    lengths,
    adam_step,
    learn_rate,
    attn_w,
    attn_m,
    attn_v,
    ffn_w,
    ffn_m,
    ffn_v,
    vecs,
    vecs_m,
    vecs_v,
    b_ff,
    bff_m,
    bff_v,
):
    slot_count = lengths.shape[0]
    row_count = tokens.shape[0]
    slot_shape = (slot_count, LMAX, D)
    positions = jnp.arange(LMAX, dtype=jnp.int32)
    key_keep = positions[None, :] < lengths[:, None]
    row_keep = key_keep.reshape(row_count, 1)
    shards, rows = mesh_shape[0], vecs.shape[0]
    extras = jnp.concatenate([vecs.T, b_ff.reshape(4, rows)], axis=0)
    extras = jnp.pad(extras, ((0, 4), (0, 128 - rows)))
    attn_low, ffn_low, ex_all = all_gather(mesh_shape, [attn_w, ffn_w], extras, 1)
    attn_low = attn_low.reshape(D, 4 * D)
    ffn_low = ffn_low.reshape(D, 2 * FF)
    vec_full = ex_all[:, :8, :rows].transpose(0, 2, 1).reshape(D, 8)
    bias_full = ex_all[:, 8:12, :rows].reshape(FF)
    projected = jnp.dot(tokens, attn_low[:, : 3 * D], preferred_element_type=jnp.float32)
    queries = (projected[:, :D] + vec_full[:, 0]).astype(jnp.bfloat16)
    keys_all = projected[:, D : 2 * D].astype(jnp.bfloat16)
    values_all = (projected[:, 2 * D :] + vec_full[:, 1]).astype(jnp.bfloat16)
    mixed_all, log_total = lax.map(
        attend_forward,
        (
            queries.reshape(slot_shape),
            keys_all.reshape(slot_shape),
            values_all.reshape(slot_shape),
            key_keep,
        ),
    )
    mixed_low = mixed_all.reshape(row_count, D).astype(jnp.bfloat16)
    branch = (
        jnp.dot(mixed_low, attn_low[:, 3 * D :], preferred_element_type=jnp.float32)
        + vec_full[:, 2]
    )
    hidden, norm_first = jax.vjp(
        layer_norm, tokens.astype(jnp.float32) + branch, vec_full[:, 3], vec_full[:, 4]
    )
    hidden_low = hidden.astype(jnp.bfloat16)
    inner_pre = jnp.dot(
        hidden_low, ffn_low[:, :FF], preferred_element_type=jnp.float32
    ) + bias_full
    activated, gelu_pull = jax.vjp(exact_gelu, inner_pre)
    act_low = activated.astype(jnp.bfloat16)
    outer_pre = (
        lax.dot_general(act_low, ffn_low[:, FF:], CONTRACT_COLS, preferred_element_type=jnp.float32)
        + vec_full[:, 5]
    )
    normed, norm_second = jax.vjp(layer_norm, hidden + outer_pre, vec_full[:, 6], vec_full[:, 7])
    outputs = jnp.where(row_keep, normed, 0.0).astype(jnp.bfloat16)
    grad_out = jnp.where(row_keep, cotangent.astype(jnp.float32), 0.0)
    grad_resid2, grad_gain2, grad_shift2 = norm_second(grad_out)
    grad_outer = grad_resid2.astype(jnp.bfloat16)
    grad_bias2 = jnp.sum(grad_outer.astype(jnp.float32), axis=0)
    grad_down = lax.dot_general(
        grad_outer, act_low, CONTRACT_ROWS, preferred_element_type=jnp.float32
    )
    grad_act = jnp.dot(grad_outer, ffn_low[:, FF:], preferred_element_type=jnp.float32)
    (grad_inner,) = gelu_pull(grad_act)
    grad_inner_low = grad_inner.astype(jnp.bfloat16)
    grad_bias1 = jnp.sum(grad_inner_low.astype(jnp.float32), axis=0)
    grad_up = lax.dot_general(
        hidden_low, grad_inner_low, CONTRACT_ROWS, preferred_element_type=jnp.float32
    )
    grad_hidden = grad_resid2 + lax.dot_general(
        grad_inner_low, ffn_low[:, :FF], CONTRACT_COLS, preferred_element_type=jnp.float32
    )
    grad_ffn = jnp.concatenate([grad_up, grad_down], axis=1)
    grad_resid1, grad_gain1, grad_shift1 = norm_first(grad_hidden)
    grad_branch = grad_resid1.astype(jnp.bfloat16)
    grad_bias_out = jnp.sum(grad_branch.astype(jnp.float32), axis=0)
    grad_out_proj = lax.dot_general(
        mixed_low, grad_branch, CONTRACT_ROWS, preferred_element_type=jnp.float32
    )
    grad_mixed = lax.dot_general(
        grad_branch, attn_low[:, 3 * D :], CONTRACT_COLS, preferred_element_type=jnp.float32
    ).astype(jnp.bfloat16)
    grad_query, grad_key, grad_value = lax.map(
        attend_backward,
        (
            queries.reshape(slot_shape),
            keys_all.reshape(slot_shape),
            values_all.reshape(slot_shape),
            key_keep,
            log_total,
            grad_mixed.reshape(slot_shape),
        ),
    )
    grad_query = grad_query.reshape(row_count, D)
    grad_key = grad_key.reshape(row_count, D)
    grad_value = grad_value.reshape(row_count, D)
    grad_proj = jnp.concatenate([grad_query, grad_key, grad_value], axis=1)
    grad_bias_query = jnp.sum(grad_query.astype(jnp.float32), axis=0)
    grad_bias_value = jnp.sum(grad_value.astype(jnp.float32), axis=0)
    grad_in_proj = lax.dot_general(
        tokens, grad_proj, CONTRACT_ROWS, preferred_element_type=jnp.float32
    )
    input_grad = grad_resid1 + lax.dot_general(
        grad_proj, attn_low[:, : 3 * D], CONTRACT_COLS, preferred_element_type=jnp.float32
    )
    grad_attn = jnp.concatenate([grad_in_proj, grad_out_proj], axis=1)
    grad_small = jnp.concatenate(
        [
            grad_bias_query[None],
            grad_bias_value[None],
            grad_bias_out[None],
            grad_gain1[None],
            grad_shift1[None],
            grad_bias2[None],
            grad_gain2[None],
            grad_shift2[None],
            grad_bias1.reshape(4, D),
            jnp.zeros((4, D), jnp.float32),
        ],
        axis=0,
    )
    summed_attn, summed_ffn, summed_small = reduce_scatter(
        mesh_shape,
        [
            grad_attn.astype(jnp.bfloat16).reshape(shards, rows, 4 * D),
            grad_ffn.astype(jnp.bfloat16).reshape(shards, rows, 2 * FF),
        ],
        grad_small,
        2,
    )
    mine = lax.axis_index("fsdp")
    summed_vecs = lax.dynamic_slice(summed_small, (0, mine * rows), (8, rows)).T
    summed_bias = lax.dynamic_slice(summed_small[8:12].reshape(FF), (mine * 4 * rows,), (4 * rows,))
    attn_new = adam_update(summed_attn, attn_m, attn_v, attn_w, adam_step, learn_rate)
    ffn_new = adam_update(summed_ffn, ffn_m, ffn_v, ffn_w, adam_step, learn_rate)
    vecs_new = adam_update(summed_vecs, vecs_m, vecs_v, vecs, adam_step, learn_rate)
    bff_new = adam_update(summed_bias, bff_m, bff_v, b_ff, adam_step, learn_rate)
    return (
        outputs,
        input_grad,
        summed_attn,
        attn_new[0],
        attn_new[1],
        attn_new[2],
        attn_new[3],
        summed_ffn,
        ffn_new[0],
        ffn_new[1],
        ffn_new[2],
        ffn_new[3],
        summed_vecs,
        vecs_new[0],
        vecs_new[1],
        vecs_new[2],
        vecs_new[3],
        summed_bias,
        bff_new[0],
        bff_new[1],
        bff_new[2],
        bff_new[3],
    )


def solution(mesh):
    placed = (
        P(("fsdp", "dp"), None),
        P(("fsdp", "dp"), None),
        P(("fsdp", "dp")),
        P(),
        P(),
        P("fsdp", None),
        P("fsdp", None),
        P("fsdp", None),
        P("fsdp", None),
        P("fsdp", None),
        P("fsdp", None),
        P("fsdp", None),
        P("fsdp", None),
        P("fsdp", None),
        P("fsdp"),
        P("fsdp"),
        P("fsdp"),
    )
    return jax.shard_map(
        functools.partial(local, (mesh.shape["fsdp"], mesh.shape["dp"])),
        mesh=mesh,
        in_specs=placed,
        out_specs=(
            P(("fsdp", "dp"), None),
            P(("fsdp", "dp"), None),
            P("fsdp", None),
            P("fsdp", None),
            P("fsdp", None),
            P("fsdp", None),
            P("fsdp", None),
            P("fsdp", None),
            P("fsdp", None),
            P("fsdp", None),
            P("fsdp", None),
            P("fsdp", None),
            P("fsdp", None),
            P("fsdp", None),
            P("fsdp", None),
            P("fsdp", None),
            P("fsdp", None),
            P("fsdp"),
            P("fsdp"),
            P("fsdp"),
            P("fsdp"),
            P("fsdp"),
        ),
        check_vma=False,
    )
```

```python
import functools

import jax
import jax.numpy as jnp
from jax import lax
from jax.experimental import pallas as pl
from jax.experimental.pallas import tpu as pltpu
from jax.sharding import PartitionSpec as P

MESH = pl.DeviceIdType.MESH

def place(na):
    me = lax.axis_index("fsdp"); p = lax.axis_index("dp")
    a = me // 4; b = (me // 2) % 2; c = me % 2
    par = p % 2
    f2 = lambda aa, bb, cc: (aa, bb + (1 - 2*bb)*(1 - par), cc + (1 - 2*cc)*par)
    f3 = lambda aa, bb, cc: (aa, bb + (1 - 2*bb)*par, cc + (1 - 2*cc)*(1 - par))
    idx = lambda t: (t[0]*2 + t[1])*2 + t[2]
    return me, p, (a, b, c), f2, f3, idx

def barrier_all(na, ndp):
    me, p, (a, b, c), f2, f3, idx = place(na)
    sem = pltpu.get_barrier_semaphore()
    n = 0
    def sig(f, q):
        pl.semaphore_signal(sem, inc=1, device_id=(f, q), device_id_type=MESH)
    for k in range(1, na):
        sig(idx(((a + k) % na, b, c)), p); n += 1
    sig(idx(f2(a, b, c)), p); n += 1
    sig(idx(f3(a, b, c)), p); n += 1
    for k in range(1, ndp):
        sig(me, (p + k) % ndp); n += 1
    pl.semaphore_wait(sem, n)

def ag_kernel(na, ndp, *refs):
    narr = 2
    shards = refs[:narr]; ex = refs[narr]; outs = refs[narr+1:2*narr+1]; exo = refs[2*narr+1]
    scr = refs[2*narr+2:]
    me, p, (a, b, c), f2, f3, idx = place(na)
    barrier_all(na, ndp)
    casts = scr[:narr]; lsem = scr[narr]; sems = scr[narr+1:]
    xss, xrs = sems[2*narr], sems[2*narr+1]
    exo[me] = ex[...].astype(jnp.bfloat16).astype(jnp.float32)
    pend = []
    locs = []
    st = []
    for i in range(narr):
        C = shards[i].shape[1]; w = C // ndp
        casts[i][...] = shards[i][...].astype(jnp.bfloat16)
        loc = pltpu.make_async_copy(casts[i], outs[i].at[me], lsem.at[i])
        loc.start(); locs.append(loc)
        ssem, rsem = sems[2*i], sems[2*i+1]
        cols = pl.ds(pl.multiple_of(p*w, 128), w)
        def rc(src, f, dst_dev, j, i=i, cols=cols, ssem=ssem, rsem=rsem):
            return pltpu.make_async_remote_copy(src_ref=src, dst_ref=outs[i].at[f, :, cols],
                send_sem=ssem.at[j], recv_sem=rsem.at[j], device_id=dst_dev, device_id_type=MESH)
        own = casts[i].at[:, cols]
        st.append((rc, own, cols))
    NS = (na - 1) + na + 2*na + (ndp - 1)*(4*na - 1)
    p2 = idx(f2(a, b, c)); p3 = idx(f3(a, b, c))
    sends = []
    recvs = [dict() for _ in range(narr)]
    def send(i, src, f, dev, j):
        d = st[i][0](src, f, dev, j); d.start(); sends.append(d)
    def wait(i, f, j):
        d = st[i][0](outs[i].at[f, :, st[i][2]], f, (me, p), j); d.wait_recv()
    J2 = na - 1; J3 = J2 + na; JD = J3 + 2*na
    def xsend(f, dev, j):
        d = pltpu.make_async_remote_copy(src_ref=exo.at[f], dst_ref=exo.at[f], send_sem=xss.at[j], recv_sem=xrs.at[j], device_id=dev, device_id_type=MESH)
        d.start(); sends.append(d)
    def xwait(f, j):
        pltpu.make_async_remote_copy(src_ref=exo.at[f], dst_ref=exo.at[f], send_sem=xss.at[j], recv_sem=xrs.at[j], device_id=(me, p), device_id_type=MESH).wait_recv()
    for k in range(1, na):
        xsend(me, (idx(((a + k) % na, b, c)), p), k - 1)
    xsend(me, (p2, p), J2)
    xsend(me, (p3, p), J3)
    for i in range(narr):
        for k in range(1, na):
            send(i, st[i][1], me, (idx(((a + k) % na, b, c)), p), k - 1)
        send(i, st[i][1], me, (p2, p), J2)
        send(i, st[i][1], me, (p3, p), J3)
    for i in range(narr):
        at = lambda f, i=i: outs[i].at[f, :, st[i][2]]
        def dp(f, m):
            for q in range(1, ndp):
                send(i, at(f), f, (me, (p + q) % ndp), JD + (q-1)*(4*na-1) + m)
        A = [(a + na - k) % na for k in range(na)]
        own = [idx((A[k], b, c)) for k in range(na)]
        col2 = [idx(f2(A[k], b, c)) for k in range(na)]
        col3 = [idx(f3(A[k], b, c)) for k in range(na)]
        t = f2(a, b, c)
        col23 = [idx(f3(A[k], t[1], t[2])) for k in range(na)]
        for k in range(na):
            if k > 0:
                wait(i, own[k], k - 1)
                if i == 0:
                    xwait(own[k], k - 1)
                    xsend(own[k], (p2, p), J2 + k)
                    xsend(own[k], (p3, p), J3 + k)
                send(i, at(own[k]), own[k], (p2, p), J2 + k)
                send(i, at(own[k]), own[k], (p3, p), J3 + k)
                dp(own[k], k - 1)
            wait(i, col2[k], J2 + k)
            if i == 0:
                xwait(col2[k], J2 + k)
                xsend(col2[k], (p3, p), J3 + na + k)
            send(i, at(col2[k]), col2[k], (p3, p), J3 + na + k)
            dp(col2[k], na - 1 + k)
            wait(i, col3[k], J3 + k)
            if i == 0: xwait(col3[k], J3 + k)
            dp(col3[k], 2*na - 1 + k)
        for k in range(na):
            wait(i, col23[k], J3 + na + k)
            if i == 0: xwait(col23[k], J3 + na + k)
            dp(col23[k], 3*na - 1 + k)
    for i in range(narr):
        w = st[i][2].size
        for q in range(1, ndp):
            src_p = (p + ndp - q) % ndp
            for m in range(4*na - 1):
                cols = pl.ds(pl.multiple_of(src_p*w, 128), w)
                rsem = sems[2*i+1]; ssem = sems[2*i]
                j = JD + (q-1)*(4*na-1) + m
                r = outs[i].at[me, :, cols]
                pltpu.make_async_remote_copy(src_ref=r, dst_ref=r, send_sem=ssem.at[j], recv_sem=rsem.at[j], device_id=(me, p), device_id_type=MESH).wait_recv()
    for d in sends: d.wait_send()
    for l in locs: l.wait()

def all_gather(mesh_shape, shards, ex, cid):
    F, ndp = mesh_shape
    na = F // 4
    NS = (na - 1) + na + 2*na + (ndp - 1)*(4*na - 1)
    scr = [pltpu.VMEM(s.shape, jnp.bfloat16) for s in shards] + [pltpu.SemaphoreType.DMA((len(shards),))]
    for s in list(shards) + [ex]:
        scr += [pltpu.SemaphoreType.DMA((NS,)), pltpu.SemaphoreType.DMA((NS,))]
    V = pl.BlockSpec(memory_space=pltpu.VMEM)
    return pl.pallas_call(
        functools.partial(ag_kernel, na, ndp),
        out_shape=[jax.ShapeDtypeStruct((F,) + s.shape, jnp.bfloat16) for s in shards] + [jax.ShapeDtypeStruct((F,) + ex.shape, jnp.float32)],
        in_specs=[V]*(len(shards) + 1),
        out_specs=[pl.BlockSpec(memory_space=pl.ANY)]*len(shards) + [V],
        scratch_shapes=scr,
        compiler_params=pltpu.CompilerParams(collective_id=cid, has_side_effects=True),
    )(*shards, ex)

def rs_kernel(na, ndp, narr, *refs):
    grads = refs[:narr]; ex = refs[narr]
    outs = refs[narr+1:2*narr+1]; exo = refs[2*narr+1]
    scr = refs[2*narr+2:]
    me, p, (a, b, c), f2, f3, idx = place(na)
    barrier_all(na, ndp)
    exb, exs, exr = scr[0:3]
    lsem = scr[3]
    bufs = [scr[4+7*i:4+7*i+7] for i in range(narr)]
    t2 = f2(a, b, c); t3 = f3(a, b, c); p2 = idx(t2); p3 = idx(t3)
    t23 = f2(*t3)
    R = grads[0].shape[1]
    sends = []; locs = []
    def rc(src, dst, ss, rs, dev):
        return pltpu.make_async_remote_copy(src_ref=src, dst_ref=dst, send_sem=ss, recv_sem=rs, device_id=dev, device_id_type=MESH)
    def start(*x):
        d = rc(*x); d.start(); sends.append(d)
    def waitr(dst, rs):
        rc(dst, dst, rs, rs, (me, p)).wait_recv()
    order_a = [(a + 1 + k) % na for k in range(na)]
    def shard(aa, flip2, flip3):
        t = (aa, b, c)
        if flip2: t = f2(*t)
        if flip3: t = f3(*t)
        return idx(t)
    seq = [(k, 1, 1) for k in range(na)] + [(k, 0, 1) for k in range(na)] + [(k, 1, 0) for k in range(na)] + [(k, 0, 0) for k in range(na)]
    for i in range(narr):
        own, rD, r3, r2, r1, ss, rs = bufs[i]
        w = grads[i].shape[2] // ndp
        cols = pl.ds(pl.multiple_of(p*w, 128), w)
        for m, (k, y2, y3) in enumerate(seq):
            for q in range(1, ndp):
                f = shard(order_a[k], y2, y3) if q % 2 == 0 else shard(order_a[k], y3, y2)
                dq = (p + q) % ndp
                qc = pl.ds(pl.multiple_of(dq*w, 128), w)
                start(grads[i].at[f, :, qc], rD.at[q-1, f], ss.at[(q-1)*4*na + m], rs.at[(q-1)*4*na + f], (me, dq))
        l = pltpu.make_async_copy(grads[i].at[:, :, cols], own, lsem.at[i])
        l.start(); locs.append(l)
    NX = (ndp - 1) + 2 + (na - 1)
    xs, xr = scr[4+7*narr], scr[4+7*narr+1]
    exb[...] = ex[...]
    for q in range(1, ndp):
        start(exb, exr.at[q-1], xs.at[q-1], xr.at[q-1], (me, (p + q) % ndp))
    def add_into(i, f, srcs, dst):
        own = bufs[i][0]
        w = own.shape[2]; CH = 512 if w % 512 == 0 else (384 if w % 384 == 0 else 128)
        def body(j, _):
            s = pl.ds(pl.multiple_of(j*CH, 128), CH)
            v = own[f, :, s].astype(jnp.float32)
            for r in srcs:
                v = v + r[:, s].astype(jnp.float32)
            dst[:, s] = v.astype(dst.dtype)
            return 0
        lax.fori_loop(0, w // CH, body, 0)
    B2 = (ndp - 1)*4*na
    B3 = B2 + 2*na; B1 = B3 + na
    for l in locs: l.wait()
    def wD(i, f):
        for q in range(1, ndp):
            waitr(bufs[i][1].at[q-1, f], bufs[i][6].at[(q-1)*4*na + f])
        return [bufs[i][1].at[q-1, f] for q in range(1, ndp)]
    par = p % 2
    bit2 = b*(1 - par) + c*par
    for i in range(narr):
        own, rD, r3, r2, r1, ss, rs = bufs[i]
        for x2 in (1, 0):
            for k in range(na):
                f = shard(order_a[k], x2, 1)
                srcs = wD(i, f)
                add_into(i, f, srcs, own.at[f])
                b2 = bit2 + (1 - 2*bit2)*x2
                slot = order_a[k]*2 + b2
                m = (1 - x2)*na + k
                start(own.at[f], r3.at[slot], ss.at[B2 + m], rs.at[B2 + slot], (p3, p))
    for i in range(narr):
        own, rD, r3, r2, r1, ss, rs = bufs[i]
        for k in range(na):
            f = shard(order_a[k], 1, 0)
            slot = order_a[k]*2 + (1 - bit2)
            srcs = wD(i, f)
            waitr(r3.at[slot], rs.at[B2 + slot])
            add_into(i, f, srcs + [r3.at[slot]], own.at[f])
            start(own.at[f], r2.at[order_a[k]], ss.at[B3 + k], rs.at[B3 + order_a[k]], (p2, p))
    for i in range(narr):
        own, rD, r3, r2, r1, ss, rs = bufs[i]
        for k in range(na - 1):
            f = shard(order_a[k], 0, 0)
            slot = order_a[k]*2 + bit2
            srcs = wD(i, f)
            waitr(r3.at[slot], rs.at[B2 + slot])
            waitr(r2.at[order_a[k]], rs.at[B3 + order_a[k]])
            add_into(i, f, srcs + [r3.at[slot], r2.at[order_a[k]]], own.at[f])
            start(own.at[f], r1.at[k], ss.at[B1 + k], rs.at[B1 + k], (f, p))
    for q in range(1, ndp):
        waitr(exr.at[q-1], xr.at[q-1])
    def exsum(n0, n):
        v = exs[0]
    if ndp == 2:
        exs[0] = exb[...] + exr[0]
    else:
        def pick(j):
            v = exb[...]
            for q in range(1, ndp):
                v = jnp.where((p + ndp - q) % ndp == j, exr[q-1], v)
            return v
        v = pick(0)
        for j in range(1, ndp): v = v + pick(j)
        exs[0] = v
    X2 = ndp - 1
    start(exs.at[0], exr.at[X2], xs.at[X2], xr.at[X2], (idx((a, b, 1 - c)), p))
    waitr(exr.at[X2], xr.at[X2])
    exs[1] = exs[0] + exr[X2]
    start(exs.at[1], exr.at[X2+1], xs.at[X2+1], xr.at[X2+1], (idx((a, 1 - b, c)), p))
    waitr(exr.at[X2+1], xr.at[X2+1])
    exs[2] = exs[1] + exr[X2+1]
    for k in range(1, na):
        start(exs.at[2], exr.at[X2+1+k], xs.at[X2+1+k], xr.at[X2+1+k], (idx(((a + k) % na, b, c)), p))
    for k in range(1, na):
        waitr(exr.at[X2+1+k], xr.at[X2+1+k])
    def picka(j):
        v = exs[2]
        for k in range(1, na):
            v = jnp.where((a + na - k) % na == j, exr[X2+1+k], v)
        return v
    v = picka(0)
    for j in range(1, na): v = v + picka(j)
    exo[...] = v
    B0 = B1 + na - 1
    for i in range(narr):
        own, rD, r3, r2, r1, ss, rs = bufs[i]
        w = own.shape[2]
        f = me
        slot = a*2 + bit2
        srcs = wD(i, f)
        waitr(r3.at[slot], rs.at[B2 + slot])
        waitr(r2.at[a], rs.at[B3 + a])
        for k in range(na - 1): waitr(r1.at[k], rs.at[B1 + k])
        cols = pl.ds(pl.multiple_of(p*w, 128), w)
        dst = outs[i].at[:, cols]
        add_into(i, f, srcs + [r3.at[slot], r2.at[a]] + [r1.at[k] for k in range(na - 1)], dst)
        for q in range(1, ndp):
            start(dst, dst, ss.at[B0 + q - 1], rs.at[B0 + q - 1], (me, (p + q) % ndp))
    for i in range(narr):
        own, rD, r3, r2, r1, ss, rs = bufs[i]
        w = own.shape[2]
        for q in range(1, ndp):
            src_p = (p + ndp - q) % ndp
            waitr(outs[i].at[:, pl.ds(pl.multiple_of(src_p*w, 128), w)], rs.at[B0 + q - 1])
    for d in sends: d.wait_send()

def reduce_scatter(mesh_shape, grads, ex, cid):
    F, ndp = mesh_shape
    na = F // 4
    narr = len(grads)
    NX = (ndp - 1) + 2 + (na - 1)
    scr = [pltpu.VMEM(ex.shape, jnp.float32), pltpu.VMEM((3,) + ex.shape, jnp.float32), pltpu.VMEM((NX,) + ex.shape, jnp.float32), pltpu.SemaphoreType.DMA((narr,))]
    for g in grads:
        w = g.shape[2] // ndp; R = g.shape[1]
        NS = (ndp - 1)*4*na + 2*na + na + na - 1 + ndp - 1
        scr += [pltpu.VMEM((F, R, w), jnp.bfloat16), pltpu.VMEM((ndp - 1, F, R, w), jnp.bfloat16), pltpu.VMEM((2*na, R, w), jnp.bfloat16),
                pltpu.VMEM((na, R, w), jnp.bfloat16), pltpu.VMEM((na - 1, R, w), jnp.bfloat16), pltpu.SemaphoreType.DMA((NS,)), pltpu.SemaphoreType.DMA((NS,))]
    scr += [pltpu.SemaphoreType.DMA((NX,)), pltpu.SemaphoreType.DMA((NX,))]
    V = pl.BlockSpec(memory_space=pltpu.VMEM)
    return pl.pallas_call(
        functools.partial(rs_kernel, na, ndp, narr),
        out_shape=[jax.ShapeDtypeStruct(g.shape[1:], jnp.float32) for g in grads] + [jax.ShapeDtypeStruct(ex.shape, jnp.float32)],
        in_specs=[pl.BlockSpec(memory_space=pl.ANY)]*narr + [V],
        out_specs=[V]*(narr + 1),
        scratch_shapes=scr,
        compiler_params=pltpu.CompilerParams(collective_id=cid, has_side_effects=True, vmem_limit_bytes=50 << 20),
    )(*grads, ex)


D = 768; HEADS = 12; HEAD = 64; FF = 3072; LMAX = 512
NN = (((1,), (0,)), ((), ()))
NT = (((1,), (1,)), ((), ()))
TN = (((0,), (0,)), ((), ()))
F32 = jnp.float32; BF16 = jnp.bfloat16
QC = 256

def mm(a, b, dims=NN):
    return lax.dot_general(a, b, dims, preferred_element_type=F32)

def attend_fwd_kernel(lens_ref, tok_ref, wq_ref, wk_ref, wv_ref, vec_ref, q_ref, k_ref, v_ref, o_ref, lse_ref, ot_ref):
    n = lens_ref[pl.program_id(0)]
    x = tok_ref[...]
    q_ref[...] = ((mm(x, wq_ref[...]) + vec_ref[0:1, :]).astype(BF16) * 0.125).astype(BF16)
    k_ref[...] = mm(x, wk_ref[...]).astype(BF16)
    v_ref[...] = (mm(x, wv_ref[...]) + vec_ref[1:2, :]).astype(BF16)
    lane = lax.broadcasted_iota(jnp.int32, (LMAX, 128), 1)
    row = lax.broadcasted_iota(jnp.int32, (LMAX, 128), 0)
    bar = jnp.where(row < n, 0.0, -1e30).astype(BF16)
    one = jnp.ones((LMAX, 128), BF16); zero = jnp.zeros((LMAX, 128), BF16)

    def pair(j, _):
        ls = pl.ds(pl.multiple_of(j * 128, 128), 128)
        q2 = q_ref[:, ls]; k2 = k_ref[:, ls]
        vt = v_ref[:, ls].T
        for e in range(2):
            other = 64 * (1 - e)
            ka = jnp.where((lane >= 64) == (e == 1), k2, jnp.where(lane == other, bar, zero))
            qa = jnp.where(lane == other, one, q2)
            for c in range(LMAX // QC):
                s = mm(ka, qa[c*QC:(c+1)*QC], NT)
                top = jnp.max(s, axis=0, keepdims=True)
                p = jnp.exp(s - top)
                tot = jnp.sum(p, axis=0, keepdims=True)
                o = mm(vt[64*e:64*e+64], p.astype(BF16))
                ot_ref[64*e:64*e+64, c*QC:(c+1)*QC] = o / tot
                lse_ref[pl.ds(2*j + e, 1), c*QC:(c+1)*QC] = top + jnp.log(tot)
        o_ref[:, ls] = ot_ref[...].T.astype(BF16)
        return 0
    lax.fori_loop(0, HEADS // 2, pair, 0)

def attend_fwd(tokens, wa, vec8, lens):
    S = tokens.shape[0] // LMAX
    row = pl.BlockSpec((LMAX, D), lambda s, l: (s, 0))
    w = lambda i: pl.BlockSpec((D, D), lambda s, l, i=i: (0, i))
    return pl.pallas_call(
        attend_fwd_kernel,
        out_shape=[jax.ShapeDtypeStruct((S*LMAX, D), BF16)]*4 + [jax.ShapeDtypeStruct((S*16, LMAX), F32)],
        grid_spec=pltpu.PrefetchScalarGridSpec(num_scalar_prefetch=1, grid=(S,),
            in_specs=[row, w(0), w(1), w(2), pl.BlockSpec((8, D), lambda s, l: (0, 0))],
            out_specs=[row]*4 + [pl.BlockSpec((16, LMAX), lambda s, l: (s, 0))],
            scratch_shapes=[pltpu.VMEM((128, LMAX), F32)]),
        name="attend_fwd",
    )(lens, tokens, wa, wa, wa, vec8)

def attend_bwd_kernel(lens_ref, q_ref, k_ref, v_ref, do_ref, lse_ref, tok_ref, dz_ref, wq_ref, wk_ref, wv_ref, dx_ref, dw_ref, small_ref,
                      dq_s, dk_s, dv_s, xt_s, dqt_s, acck, accv, lse_s):
    S = tok_ref.shape[0] // LMAX
    lane = lax.broadcasted_iota(jnp.int32, (LMAX, 128), 1)
    row = lax.broadcasted_iota(jnp.int32, (LMAX, 128), 0)
    one = jnp.ones((LMAX, 128), BF16); zero = jnp.zeros((LMAX, 128), BF16)
    xt_s[...] = tok_ref[...].T

    def task(t, _):
        sl = t // (HEADS // 2); j = t % (HEADS // 2)
        rs = pl.ds(pl.multiple_of(sl * LMAX, LMAX), LMAX)
        ls = pl.ds(pl.multiple_of(j * 128, 128), 128)
        bar = jnp.where(row < lens_ref[sl], 0.0, -1e30).astype(BF16)
        q2 = q_ref[rs, ls]; k2 = k_ref[rs, ls]; v2 = v_ref[rs, ls]; do2 = do_ref[rs, ls]
        kt = k2.T
        for e in range(2):
            other = 64 * (1 - e)
            mine = (lane >= 64) == (e == 1)
            ka = jnp.where(mine, k2, jnp.where(lane == other, bar, zero))
            va = jnp.where(mine, v2, zero)
            qa = jnp.where(lane == other, one, q2)
            lse_row = lse_ref[pl.ds(sl * 16 + 2*j + e, 1), :]
            for c in range(LMAX // QC):
                cs = slice(c*QC, (c+1)*QC)
                s = mm(ka, qa[cs], NT)
                p = jnp.exp(s - lse_row[:, cs])
                dp = mm(va, do2[cs], NT)
                pd = p * dp
                dsum = jnp.sum(pd, axis=0, keepdims=True)
                ds = (pd - p * dsum).astype(BF16)
                dvc = mm(p.astype(BF16), do2[cs])
                dkc = mm(ds, q2[cs])
                if c == 0:
                    dva, dka = dvc, dkc
                else:
                    dva, dka = dva + dvc, dka + dkc
                dqt_s[64*e:64*e+64, cs] = mm(kt[64*e:64*e+64], ds)
            if e == 0:
                accv[...] = dva; acck[...] = dka
            else:
                dv_s[rs, ls] = jnp.where(mine, dva, accv[...]).astype(BF16)
                dk_s[rs, ls] = jnp.where(mine, dka, acck[...]).astype(BF16)
        dq_s[rs, ls] = (dqt_s[...].T * 0.125).astype(BF16)
        return 0
    lax.fori_loop(0, S * (HEADS // 2), task, 0)
    small_ref[...] = jnp.zeros_like(small_ref)
    small_ref[0:1, :] = jnp.sum(dq_s[...].astype(F32), axis=0, keepdims=True)
    small_ref[1:2, :] = jnp.sum(dv_s[...].astype(F32), axis=0, keepdims=True)
    def rows(r, _):
        rr = pl.ds(pl.multiple_of(r * 256, 256), 256)
        dx_ref[rr, :] = dz_ref[rr, :] + mm(dq_s[rr, :], wq_ref[...], NT) + mm(dk_s[rr, :], wk_ref[...], NT) + mm(dv_s[rr, :], wv_ref[...], NT)
        return 0
    lax.fori_loop(0, S * LMAX // 256, rows, 0)
    for i, g in enumerate((dq_s, dk_s, dv_s)):
        def wg(r, _, g=g, i=i):
            rr = pl.ds(pl.multiple_of(r * 256, 256), 256)
            dw_ref[rr, i*D:(i+1)*D] = mm(xt_s[rr, :], g[...]).astype(BF16)
            return 0
        lax.fori_loop(0, D // 256, wg, 0)

def attend_bwd(q, k, v, do, lse, tokens, dz, wa, lens):
    T = tokens.shape[0]
    V = pl.BlockSpec(memory_space=pltpu.VMEM)
    w = lambda i: pl.BlockSpec((D, D), lambda s, l, i=i: (0, i))
    full = lambda a: pl.BlockSpec(a.shape, lambda s, l: (0, 0))
    o = lambda sh: pl.BlockSpec(sh, lambda s, l: (0, 0))
    return pl.pallas_call(
        attend_bwd_kernel,
        out_shape=[jax.ShapeDtypeStruct((T, D), F32), jax.ShapeDtypeStruct((D, 3*D), BF16), jax.ShapeDtypeStruct((8, D), F32)],
        grid_spec=pltpu.PrefetchScalarGridSpec(num_scalar_prefetch=1, grid=(1,),
            in_specs=[full(q)]*4 + [full(lse), full(tokens), full(dz), w(0), w(1), w(2)],
            out_specs=[o((T, D)), o((D, 3*D)), o((8, D))],
            scratch_shapes=[pltpu.VMEM((T, D), BF16)]*3 + [pltpu.VMEM((D, T), BF16), pltpu.VMEM((128, LMAX), F32), pltpu.VMEM((LMAX, 128), F32), pltpu.VMEM((LMAX, 128), F32), pltpu.VMEM((8, 128), F32)]),
        name="attend_bwd",
    )(lens, q, k, v, do, lse, tokens, dz, wa, wa, wa)


M = 256
CF = 512
ERF_P = 0.47 * 0.7071067811865476
ERF_C = [0.26618060444990516, 0.2492263717857657, 0.33168688252906103, -0.11731296726838297, 0.5981763964403582, -0.41518397881696706, 0.08722668027552141]

def gelu_pair(u):
    au = jnp.abs(u)
    t = 1.0 / (1.0 + ERF_P * au)
    e = jnp.exp(-0.5 * (u * u))
    acc = ERF_C[-1] * 0.5
    for cf in ERF_C[-2::-1]:
        acc = acc * t + 0.5 * cf
    h = acc * t * e
    phi = jnp.where(u < 0, h, 1.0 - h)
    return u * phi, phi + u * (e * 0.3989422804014327)

def norm_stats(z):
    mean = jnp.mean(z, axis=-1, keepdims=True)
    c = z - mean
    var = jnp.mean(c * c, axis=-1, keepdims=True)
    r = lax.rsqrt(var + 1e-5)
    return c * r, r

def norm_back(dxh, xh, r):
    return r * (dxh - jnp.mean(dxh, axis=-1, keepdims=True) - xh * jnp.mean(dxh * xh, axis=-1, keepdims=True))

def colsum(x):
    return jnp.sum(x, axis=0, keepdims=True)

def ffn_kernel(lens_ref, o_ref, tok_ref, cot_ref, wo_ref, w1_ref, w2_ref, vec_ref, b1_ref,
               out_ref, dz_ref, do_ref, ot_ref, da_ref, ht_ref, dft_ref, g_ref, du_ref, small_ref,
               gp_s, facc, hacc):
    t = pl.program_id(0); per = LMAX // M
    sl = t // per; base = (t % per) * M
    n = lens_ref[sl] - base

    @pl.when(t == 0)
    def _():
        small_ref[...] = jnp.zeros_like(small_ref)

    @pl.when(n <= 0)
    def _():
        for r in (out_ref, dz_ref, do_ref, ot_ref, da_ref, ht_ref, dft_ref, g_ref, du_ref):
            r[...] = jnp.zeros_like(r)

    @pl.when(n > 0)
    def _():
        v = lambda i: vec_ref[i:i+1, :]
        o = o_ref[...]
        z1 = tok_ref[...].astype(F32) + (mm(o, wo_ref[...]) + v(2))
        xh1, r1 = norm_stats(z1)
        h = xh1 * v(3) + v(4)
        hb = h.astype(BF16)
        facc[...] = jnp.zeros_like(facc)
        def up(j, _):
            cs = pl.ds(pl.multiple_of(j * CF, 128), CF)
            u = mm(hb, w1_ref[:, cs]) + b1_ref[:, cs]
            g, gp = gelu_pair(u)
            gb = g.astype(BF16)
            g_ref[:, cs] = gb
            gp_s[:, cs] = gp
            facc[...] += mm(gb, w2_ref[:, cs], NT)
            return 0
        lax.fori_loop(0, FF // CF, up, 0)
        z2 = h + (facc[...] + v(5))
        xh2, r2 = norm_stats(z2)
        keep = lax.broadcasted_iota(jnp.int32, (M, 1), 0) < n
        out_ref[...] = jnp.where(keep, xh2 * v(6) + v(7), 0.0).astype(BF16)
        dy = jnp.where(keep, cot_ref[...].astype(F32), 0.0)
        small_ref[7:8, :] += colsum(dy)
        small_ref[6:7, :] += colsum(dy * xh2)
        dz2 = norm_back(dy * v(6), xh2, r2)
        df = dz2.astype(BF16)
        small_ref[5:6, :] += colsum(df.astype(F32))
        hacc[...] = dz2
        def down(j, _):
            cs = pl.ds(pl.multiple_of(j * CF, 128), CF)
            dg = mm(df, w2_ref[:, cs])
            du = (gp_s[:, cs] * dg).astype(BF16)
            du_ref[:, cs] = du
            b1g_ref = small_ref
            gp_s[0:1, cs] = colsum(du.astype(F32))
            hacc[...] += mm(du, w1_ref[:, cs], NT)
            return 0
        lax.fori_loop(0, FF // CF, down, 0)
        for i in range(4):
            small_ref[8+i:9+i, :] += gp_s[0:1, i*D:(i+1)*D]
        dh = hacc[...]
        small_ref[4:5, :] += colsum(dh)
        small_ref[3:4, :] += colsum(dh * xh1)
        dz1 = norm_back(dh * v(3), xh1, r1)
        da = dz1.astype(BF16)
        small_ref[2:3, :] += colsum(da.astype(F32))
        dz_ref[...] = dz1
        da_ref[...] = da
        do_ref[...] = mm(da, wo_ref[...], NT).astype(BF16)
        ot_ref[...] = o.T
        ht_ref[...] = hb.T
        dft_ref[...] = df.T

def tile_order(lens, T):
    per = LMAX // M
    tiles = T // M
    live = (jnp.arange(tiles) % per) * M < lens[jnp.arange(tiles) // per]
    nl = jnp.sum(live.astype(jnp.int32))
    before = jnp.cumsum(live.astype(jnp.int32)) - live
    dead = jnp.arange(tiles) - before
    return jnp.where(live, before, nl + dead).astype(jnp.int32), nl

def ffn_rows(o, tokens, cot, wa, wf, vec8, b1, lens, order):
    T = tokens.shape[0]
    row = pl.BlockSpec((M, D), lambda t, l, q: (t, 0))
    one = lambda sh, i: pl.BlockSpec(sh, lambda t, l, q: (0, i), pipeline_mode=pl.Buffered(1))
    comp = lambda w: pl.BlockSpec((M, w), lambda t, l, q: (q[t], 0))
    compT = pl.BlockSpec((D, M), lambda t, l, q: (0, q[t]))
    S = jax.ShapeDtypeStruct
    def kern(lens_ref, order_ref, *refs): return ffn_kernel(lens_ref, *refs)
    return pl.pallas_call(
        kern,
        out_shape=[S((T, D), BF16), S((T, D), F32), S((T, D), BF16), S((D, T), BF16), S((T, D), BF16), S((D, T), BF16), S((D, T), BF16), S((T, FF), BF16), S((T, FF), BF16), S((16, D), F32)],
        grid_spec=pltpu.PrefetchScalarGridSpec(num_scalar_prefetch=2, grid=(T // M,),
            in_specs=[row, row, row, one((D, D), 3), one((D, FF), 0), one((D, FF), 1), one((8, D), 0), one((1, FF), 0)],
            out_specs=[row, row, row, compT, comp(D), compT, compT, comp(FF), comp(FF), pl.BlockSpec((16, D), lambda t, l, q: (0, 0))],
            scratch_shapes=[pltpu.VMEM((M, FF), F32), pltpu.VMEM((M, D), F32), pltpu.VMEM((M, D), F32)]),
        name="ffn_rows",
    )(lens, order, o, tokens, cot, wa, wf, wf, vec8, b1)

NB = 512
def ffn_grads_kernel(nl_ref, ht_ref, dft_ref, du_ref, g_ref, out_ref):
    i = pl.program_id(0)
    half = FF // NB
    T = ht_ref.shape[1]
    k4 = (nl_ref[0] * M + 255) // 256
    for s in range(2):
        lt, r = ((ht_ref, du_ref), (dft_ref, g_ref))[s]
        for kk in range(1, T // 256 + 1):
            @pl.when(((i < half) == (s == 0)) & (k4 == kk))
            def _(lt=lt, r=r, K=kk*256):
                out_ref[...] = mm(lt[:, :K], r[:K, :]).astype(BF16)

def ffn_grads(ht, dft, du, g, nl):
    T = ht.shape[1]; half = FF // NB
    full = pl.BlockSpec((D, T), lambda i, n: (0, 0), pipeline_mode=pl.Buffered(1))
    return pl.pallas_call(
        ffn_grads_kernel,
        out_shape=jax.ShapeDtypeStruct((D, 2*FF), BF16),
        grid_spec=pltpu.PrefetchScalarGridSpec(num_scalar_prefetch=1, grid=(2*half,),
            in_specs=[full, full, pl.BlockSpec((T, NB), lambda i, n: (0, jnp.minimum(i, half-1))), pl.BlockSpec((T, NB), lambda i, n: (0, jnp.maximum(i-half, 0)))],
            out_specs=pl.BlockSpec((D, NB), lambda i, n: (0, i))),
        name="ffn_grads",
    )(nl, ht, dft, du, g)


def adam_update(gradient, moment, second, master, adam_step, learn_rate):
    count = adam_step[0].astype(jnp.float32)
    moment_new = 0.9 * moment + 0.1 * gradient
    second_new = 0.98 * second + 0.02 * gradient * gradient
    first_fix = moment_new / (1.0 - jnp.power(0.9, count))
    second_fix = second_new / (1.0 - jnp.power(0.98, count))
    master_new = master - learn_rate[0] * (
        first_fix / (jnp.sqrt(second_fix) + 1e-06) + 0.01 * master
    )
    return (moment_new, second_new, master_new, master_new.astype(jnp.bfloat16))


def local(mesh_shape, tokens, cotangent, lengths, adam_step, learn_rate, attn_w, attn_m, attn_v, ffn_w, ffn_m, ffn_v,
          vecs, vecs_m, vecs_v, b_ff, bff_m, bff_v):
    shards, rows = mesh_shape[0], vecs.shape[0]
    T = tokens.shape[0]
    extras = jnp.concatenate([vecs.T, b_ff.reshape(4, rows)], axis=0)
    extras = jnp.pad(extras, ((0, 4), (0, 128 - rows)))
    attn_low, ffn_low, ex_all = all_gather(mesh_shape, [attn_w, ffn_w], extras, 1)
    attn_low = attn_low.reshape(D, 4 * D)
    ffn_low = ffn_low.reshape(D, 2 * FF)
    vec8 = ex_all[:, :8, :rows].transpose(1, 0, 2).reshape(8, D)
    bias = ex_all[:, 8:12, :rows].reshape(1, FF)
    order, live = tile_order(lengths, T)
    q, k, v, o, lse = attend_fwd(tokens, attn_low, vec8, lengths)
    outputs, dz1, do, ot, da, ht, dft, g, du, small_ffn = ffn_rows(
        o, tokens, cotangent, attn_low, ffn_low, vec8, bias, lengths, order)
    grad_ffn = ffn_grads(ht, dft, du, g, live[None])
    grad_wo = mm(ot, da).astype(BF16)
    input_grad, grad_qkv, small_attn = attend_bwd(q, k, v, do, lse, tokens, dz1, attn_low, lengths)
    grad_attn = jnp.concatenate([grad_qkv, grad_wo], axis=1)
    small = jnp.concatenate([small_attn[:2], small_ffn[2:]], axis=0)
    summed_attn, summed_ffn, summed_small = reduce_scatter(
        mesh_shape, [grad_attn.reshape(shards, rows, 4 * D), grad_ffn.reshape(shards, rows, 2 * FF)], small, 2)
    mine = lax.axis_index("fsdp")
    summed_vecs = lax.dynamic_slice(summed_small, (0, mine * rows), (8, rows)).T
    summed_bias = lax.dynamic_slice(summed_small[8:12].reshape(FF), (mine * 4 * rows,), (4 * rows,))
    attn_new = adam_update(summed_attn, attn_m, attn_v, attn_w, adam_step, learn_rate)
    ffn_new = adam_update(summed_ffn, ffn_m, ffn_v, ffn_w, adam_step, learn_rate)
    vecs_new = adam_update(summed_vecs, vecs_m, vecs_v, vecs, adam_step, learn_rate)
    bff_new = adam_update(summed_bias, bff_m, bff_v, b_ff, adam_step, learn_rate)
    return (outputs, input_grad, summed_attn, *attn_new, summed_ffn, *ffn_new, summed_vecs, *vecs_new, summed_bias, *bff_new)


def solution(mesh):
    both, rows, whole = P(("fsdp", "dp")), P("fsdp"), P()
    return jax.shard_map(
        functools.partial(local, (mesh.shape["fsdp"], mesh.shape["dp"])),
        mesh=mesh,
        in_specs=(both, both, both, whole, whole) + (rows,) * 12,
        out_specs=(both, both) + (rows,) * 20,
        check_vma=False,
    )
```

```python
import functools

import jax
import jax.numpy as jnp
from jax import lax
from jax.experimental import pallas as pl
from jax.experimental.pallas import tpu as pltpu
from jax.sharding import PartitionSpec as P

MESH = pl.DeviceIdType.MESH

def place(na):
    me = lax.axis_index("fsdp"); p = lax.axis_index("dp")
    a = me // 4; b = (me // 2) % 2; c = me % 2
    par = p % 2
    f2 = lambda aa, bb, cc: (aa, bb + (1 - 2*bb)*(1 - par), cc + (1 - 2*cc)*par)
    f3 = lambda aa, bb, cc: (aa, bb + (1 - 2*bb)*par, cc + (1 - 2*cc)*(1 - par))
    idx = lambda t: (t[0]*2 + t[1])*2 + t[2]
    return me, p, (a, b, c), f2, f3, idx

def barrier_all(na, ndp):
    me, p, (a, b, c), f2, f3, idx = place(na)
    sem = pltpu.get_barrier_semaphore()
    n = 0
    def sig(f, q):
        pl.semaphore_signal(sem, inc=1, device_id=(f, q), device_id_type=MESH)
    for k in range(1, na):
        sig(idx(((a + k) % na, b, c)), p); n += 1
    sig(idx(f2(a, b, c)), p); n += 1
    sig(idx(f3(a, b, c)), p); n += 1
    for k in range(1, ndp):
        sig(me, (p + k) % ndp); n += 1
    pl.semaphore_wait(sem, n)

def ag_kernel(na, ndp, *refs):
    narr = 2
    shards = refs[:narr]; ex = refs[narr]; outs = refs[narr+1:2*narr+1]; exo = refs[2*narr+1]
    scr = refs[2*narr+2:]
    me, p, (a, b, c), f2, f3, idx = place(na)
    barrier_all(na, ndp)
    casts = scr[:narr]; lsem = scr[narr]; sems = scr[narr+1:]
    xss, xrs = sems[2*narr], sems[2*narr+1]
    exo[me] = ex[...].astype(jnp.bfloat16).astype(jnp.float32)
    pend = []
    locs = []
    st = []
    for i in range(narr):
        C = shards[i].shape[1]; w = C // ndp
        casts[i][...] = shards[i][...].astype(jnp.bfloat16)
        loc = pltpu.make_async_copy(casts[i], outs[i].at[me], lsem.at[i])
        loc.start(); locs.append(loc)
        ssem, rsem = sems[2*i], sems[2*i+1]
        cols = pl.ds(pl.multiple_of(p*w, 128), w)
        def rc(src, f, dst_dev, j, i=i, cols=cols, ssem=ssem, rsem=rsem):
            return pltpu.make_async_remote_copy(src_ref=src, dst_ref=outs[i].at[f, :, cols],
                send_sem=ssem.at[j], recv_sem=rsem.at[j], device_id=dst_dev, device_id_type=MESH)
        own = casts[i].at[:, cols]
        st.append((rc, own, cols))
    NS = (na - 1) + na + 2*na + (ndp - 1)*(4*na - 1)
    p2 = idx(f2(a, b, c)); p3 = idx(f3(a, b, c))
    sends = []
    recvs = [dict() for _ in range(narr)]
    def send(i, src, f, dev, j):
        d = st[i][0](src, f, dev, j); d.start(); sends.append(d)
    def wait(i, f, j):
        d = st[i][0](outs[i].at[f, :, st[i][2]], f, (me, p), j); d.wait_recv()
    J2 = na - 1; J3 = J2 + na; JD = J3 + 2*na
    def xsend(f, dev, j):
        d = pltpu.make_async_remote_copy(src_ref=exo.at[f], dst_ref=exo.at[f], send_sem=xss.at[j], recv_sem=xrs.at[j], device_id=dev, device_id_type=MESH)
        d.start(); sends.append(d)
    def xwait(f, j):
        pltpu.make_async_remote_copy(src_ref=exo.at[f], dst_ref=exo.at[f], send_sem=xss.at[j], recv_sem=xrs.at[j], device_id=(me, p), device_id_type=MESH).wait_recv()
    for k in range(1, na):
        xsend(me, (idx(((a + k) % na, b, c)), p), k - 1)
    xsend(me, (p2, p), J2)
    xsend(me, (p3, p), J3)
    for i in range(narr):
        for k in range(1, na):
            send(i, st[i][1], me, (idx(((a + k) % na, b, c)), p), k - 1)
        send(i, st[i][1], me, (p2, p), J2)
        send(i, st[i][1], me, (p3, p), J3)
    for i in range(narr):
        at = lambda f, i=i: outs[i].at[f, :, st[i][2]]
        def dp(f, m):
            for q in range(1, ndp):
                send(i, at(f), f, (me, (p + q) % ndp), JD + (q-1)*(4*na-1) + m)
        A = [(a + na - k) % na for k in range(na)]
        own = [idx((A[k], b, c)) for k in range(na)]
        col2 = [idx(f2(A[k], b, c)) for k in range(na)]
        col3 = [idx(f3(A[k], b, c)) for k in range(na)]
        t = f2(a, b, c)
        col23 = [idx(f3(A[k], t[1], t[2])) for k in range(na)]
        for k in range(na):
            if k > 0:
                wait(i, own[k], k - 1)
                if i == 0:
                    xwait(own[k], k - 1)
                    xsend(own[k], (p2, p), J2 + k)
                    xsend(own[k], (p3, p), J3 + k)
                send(i, at(own[k]), own[k], (p2, p), J2 + k)
                send(i, at(own[k]), own[k], (p3, p), J3 + k)
                dp(own[k], k - 1)
            wait(i, col2[k], J2 + k)
            if i == 0:
                xwait(col2[k], J2 + k)
                xsend(col2[k], (p3, p), J3 + na + k)
            send(i, at(col2[k]), col2[k], (p3, p), J3 + na + k)
            dp(col2[k], na - 1 + k)
            wait(i, col3[k], J3 + k)
            if i == 0: xwait(col3[k], J3 + k)
            dp(col3[k], 2*na - 1 + k)
        for k in range(na):
            wait(i, col23[k], J3 + na + k)
            if i == 0: xwait(col23[k], J3 + na + k)
            dp(col23[k], 3*na - 1 + k)
    for i in range(narr):
        w = st[i][2].size
        for q in range(1, ndp):
            src_p = (p + ndp - q) % ndp
            for m in range(4*na - 1):
                cols = pl.ds(pl.multiple_of(src_p*w, 128), w)
                rsem = sems[2*i+1]; ssem = sems[2*i]
                j = JD + (q-1)*(4*na-1) + m
                r = outs[i].at[me, :, cols]
                pltpu.make_async_remote_copy(src_ref=r, dst_ref=r, send_sem=ssem.at[j], recv_sem=rsem.at[j], device_id=(me, p), device_id_type=MESH).wait_recv()
    for d in sends: d.wait_send()
    for l in locs: l.wait()

def all_gather(mesh_shape, shards, ex, cid):
    F, ndp = mesh_shape
    na = F // 4
    NS = (na - 1) + na + 2*na + (ndp - 1)*(4*na - 1)
    scr = [pltpu.VMEM(s.shape, jnp.bfloat16) for s in shards] + [pltpu.SemaphoreType.DMA((len(shards),))]
    for s in list(shards) + [ex]:
        scr += [pltpu.SemaphoreType.DMA((NS,)), pltpu.SemaphoreType.DMA((NS,))]
    V = pl.BlockSpec(memory_space=pltpu.VMEM)
    return pl.pallas_call(
        functools.partial(ag_kernel, na, ndp),
        out_shape=[jax.ShapeDtypeStruct((F,) + s.shape, jnp.bfloat16) for s in shards] + [jax.ShapeDtypeStruct((F,) + ex.shape, jnp.float32)],
        in_specs=[V]*(len(shards) + 1),
        out_specs=[pl.BlockSpec(memory_space=pl.ANY)]*len(shards) + [V],
        scratch_shapes=scr,
        compiler_params=pltpu.CompilerParams(collective_id=cid, has_side_effects=True),
    )(*shards, ex)

def rs_kernel(na, ndp, narr, *refs):
    grads = refs[:narr]; ex = refs[narr]
    outs = refs[narr+1:2*narr+1]; exo = refs[2*narr+1]
    scr = refs[2*narr+2:]
    me, p, (a, b, c), f2, f3, idx = place(na)
    barrier_all(na, ndp)
    exb, exs, exr = scr[0:3]
    lsem = scr[3]
    bufs = [scr[4+7*i:4+7*i+7] for i in range(narr)]
    t2 = f2(a, b, c); t3 = f3(a, b, c); p2 = idx(t2); p3 = idx(t3)
    t23 = f2(*t3)
    R = grads[0].shape[1]
    sends = []; locs = []
    def rc(src, dst, ss, rs, dev):
        return pltpu.make_async_remote_copy(src_ref=src, dst_ref=dst, send_sem=ss, recv_sem=rs, device_id=dev, device_id_type=MESH)
    def start(*x):
        d = rc(*x); d.start(); sends.append(d)
    def waitr(dst, rs):
        rc(dst, dst, rs, rs, (me, p)).wait_recv()
    order_a = [(a + 1 + k) % na for k in range(na)]
    def shard(aa, flip2, flip3):
        t = (aa, b, c)
        if flip2: t = f2(*t)
        if flip3: t = f3(*t)
        return idx(t)
    seq = [(k, 1, 1) for k in range(na)] + [(k, 0, 1) for k in range(na)] + [(k, 1, 0) for k in range(na)] + [(k, 0, 0) for k in range(na)]
    for i in range(narr):
        own, rD, r3, r2, r1, ss, rs = bufs[i]
        w = grads[i].shape[2] // ndp
        cols = pl.ds(pl.multiple_of(p*w, 128), w)
        for m, (k, y2, y3) in enumerate(seq):
            for q in range(1, ndp):
                f = shard(order_a[k], y2, y3) if q % 2 == 0 else shard(order_a[k], y3, y2)
                dq = (p + q) % ndp
                qc = pl.ds(pl.multiple_of(dq*w, 128), w)
                start(grads[i].at[f, :, qc], rD.at[q-1, f], ss.at[(q-1)*4*na + m], rs.at[(q-1)*4*na + f], (me, dq))
        l = pltpu.make_async_copy(grads[i].at[:, :, cols], own, lsem.at[i])
        l.start(); locs.append(l)
    NX = (ndp - 1) + 2 + (na - 1)
    xs, xr = scr[4+7*narr], scr[4+7*narr+1]
    exb[...] = ex[...]
    for q in range(1, ndp):
        start(exb, exr.at[q-1], xs.at[q-1], xr.at[q-1], (me, (p + q) % ndp))
    def add_into(i, f, srcs, dst):
        own = bufs[i][0]
        w = own.shape[2]; CH = 512 if w % 512 == 0 else (384 if w % 384 == 0 else 128)
        def body(j, _):
            s = pl.ds(pl.multiple_of(j*CH, 128), CH)
            v = own[f, :, s].astype(jnp.float32)
            for r in srcs:
                v = v + r[:, s].astype(jnp.float32)
            dst[:, s] = v.astype(dst.dtype)
            return 0
        lax.fori_loop(0, w // CH, body, 0)
    B2 = (ndp - 1)*4*na
    B3 = B2 + 2*na; B1 = B3 + na
    for l in locs: l.wait()
    def wD(i, f):
        for q in range(1, ndp):
            waitr(bufs[i][1].at[q-1, f], bufs[i][6].at[(q-1)*4*na + f])
        return [bufs[i][1].at[q-1, f] for q in range(1, ndp)]
    par = p % 2
    bit2 = b*(1 - par) + c*par
    for i in range(narr):
        own, rD, r3, r2, r1, ss, rs = bufs[i]
        for x2 in (1, 0):
            for k in range(na):
                f = shard(order_a[k], x2, 1)
                srcs = wD(i, f)
                add_into(i, f, srcs, own.at[f])
                b2 = bit2 + (1 - 2*bit2)*x2
                slot = order_a[k]*2 + b2
                m = (1 - x2)*na + k
                start(own.at[f], r3.at[slot], ss.at[B2 + m], rs.at[B2 + slot], (p3, p))
    for i in range(narr):
        own, rD, r3, r2, r1, ss, rs = bufs[i]
        for k in range(na):
            f = shard(order_a[k], 1, 0)
            slot = order_a[k]*2 + (1 - bit2)
            srcs = wD(i, f)
            waitr(r3.at[slot], rs.at[B2 + slot])
            add_into(i, f, srcs + [r3.at[slot]], own.at[f])
            start(own.at[f], r2.at[order_a[k]], ss.at[B3 + k], rs.at[B3 + order_a[k]], (p2, p))
    for i in range(narr):
        own, rD, r3, r2, r1, ss, rs = bufs[i]
        for k in range(na - 1):
            f = shard(order_a[k], 0, 0)
            slot = order_a[k]*2 + bit2
            srcs = wD(i, f)
            waitr(r3.at[slot], rs.at[B2 + slot])
            waitr(r2.at[order_a[k]], rs.at[B3 + order_a[k]])
            add_into(i, f, srcs + [r3.at[slot], r2.at[order_a[k]]], own.at[f])
            start(own.at[f], r1.at[k], ss.at[B1 + k], rs.at[B1 + k], (f, p))
    for q in range(1, ndp):
        waitr(exr.at[q-1], xr.at[q-1])
    def exsum(n0, n):
        v = exs[0]
    if ndp == 2:
        exs[0] = exb[...] + exr[0]
    else:
        def pick(j):
            v = exb[...]
            for q in range(1, ndp):
                v = jnp.where((p + ndp - q) % ndp == j, exr[q-1], v)
            return v
        v = pick(0)
        for j in range(1, ndp): v = v + pick(j)
        exs[0] = v
    X2 = ndp - 1
    start(exs.at[0], exr.at[X2], xs.at[X2], xr.at[X2], (idx((a, b, 1 - c)), p))
    waitr(exr.at[X2], xr.at[X2])
    exs[1] = exs[0] + exr[X2]
    start(exs.at[1], exr.at[X2+1], xs.at[X2+1], xr.at[X2+1], (idx((a, 1 - b, c)), p))
    waitr(exr.at[X2+1], xr.at[X2+1])
    exs[2] = exs[1] + exr[X2+1]
    for k in range(1, na):
        start(exs.at[2], exr.at[X2+1+k], xs.at[X2+1+k], xr.at[X2+1+k], (idx(((a + k) % na, b, c)), p))
    for k in range(1, na):
        waitr(exr.at[X2+1+k], xr.at[X2+1+k])
    def picka(j):
        v = exs[2]
        for k in range(1, na):
            v = jnp.where((a + na - k) % na == j, exr[X2+1+k], v)
        return v
    v = picka(0)
    for j in range(1, na): v = v + picka(j)
    exo[...] = v
    B0 = B1 + na - 1
    for i in range(narr):
        own, rD, r3, r2, r1, ss, rs = bufs[i]
        w = own.shape[2]
        f = me
        slot = a*2 + bit2
        srcs = wD(i, f)
        waitr(r3.at[slot], rs.at[B2 + slot])
        waitr(r2.at[a], rs.at[B3 + a])
        for k in range(na - 1): waitr(r1.at[k], rs.at[B1 + k])
        cols = pl.ds(pl.multiple_of(p*w, 128), w)
        dst = outs[i].at[:, cols]
        add_into(i, f, srcs + [r3.at[slot], r2.at[a]] + [r1.at[k] for k in range(na - 1)], dst)
        for q in range(1, ndp):
            start(dst, dst, ss.at[B0 + q - 1], rs.at[B0 + q - 1], (me, (p + q) % ndp))
    for i in range(narr):
        own, rD, r3, r2, r1, ss, rs = bufs[i]
        w = own.shape[2]
        for q in range(1, ndp):
            src_p = (p + ndp - q) % ndp
            waitr(outs[i].at[:, pl.ds(pl.multiple_of(src_p*w, 128), w)], rs.at[B0 + q - 1])
    for d in sends: d.wait_send()

def reduce_scatter(mesh_shape, grads, ex, cid):
    F, ndp = mesh_shape
    na = F // 4
    narr = len(grads)
    NX = (ndp - 1) + 2 + (na - 1)
    scr = [pltpu.VMEM(ex.shape, jnp.float32), pltpu.VMEM((3,) + ex.shape, jnp.float32), pltpu.VMEM((NX,) + ex.shape, jnp.float32), pltpu.SemaphoreType.DMA((narr,))]
    for g in grads:
        w = g.shape[2] // ndp; R = g.shape[1]
        NS = (ndp - 1)*4*na + 2*na + na + na - 1 + ndp - 1
        scr += [pltpu.VMEM((F, R, w), jnp.bfloat16), pltpu.VMEM((ndp - 1, F, R, w), jnp.bfloat16), pltpu.VMEM((2*na, R, w), jnp.bfloat16),
                pltpu.VMEM((na, R, w), jnp.bfloat16), pltpu.VMEM((na - 1, R, w), jnp.bfloat16), pltpu.SemaphoreType.DMA((NS,)), pltpu.SemaphoreType.DMA((NS,))]
    scr += [pltpu.SemaphoreType.DMA((NX,)), pltpu.SemaphoreType.DMA((NX,))]
    V = pl.BlockSpec(memory_space=pltpu.VMEM)
    return pl.pallas_call(
        functools.partial(rs_kernel, na, ndp, narr),
        out_shape=[jax.ShapeDtypeStruct(g.shape[1:], jnp.float32) for g in grads] + [jax.ShapeDtypeStruct(ex.shape, jnp.float32)],
        in_specs=[pl.BlockSpec(memory_space=pl.ANY)]*narr + [V],
        out_specs=[V]*(narr + 1),
        scratch_shapes=scr,
        compiler_params=pltpu.CompilerParams(collective_id=cid, has_side_effects=True, vmem_limit_bytes=50 << 20),
    )(*grads, ex)


D = 768; HEADS = 12; HEAD = 64; FF = 3072; LMAX = 512
NN = (((1,), (0,)), ((), ()))
NT = (((1,), (1,)), ((), ()))
TN = (((0,), (0,)), ((), ()))
F32 = jnp.float32; BF16 = jnp.bfloat16
QC = 256

def mm(a, b, dims=NN):
    return lax.dot_general(a, b, dims, preferred_element_type=F32)

def attend_fwd_kernel(lens_ref, tok_ref, wq_ref, wk_ref, wv_ref, vec_ref, q_ref, k_ref, v_ref, o_ref, lse_ref, ot_ref):
    n = lens_ref[pl.program_id(0)]
    x = tok_ref[...]
    q_ref[...] = ((mm(x, wq_ref[...]) + vec_ref[0:1, :]).astype(BF16) * 0.125).astype(BF16)
    k_ref[...] = mm(x, wk_ref[...]).astype(BF16)
    v_ref[...] = (mm(x, wv_ref[...]) + vec_ref[1:2, :]).astype(BF16)
    lane = lax.broadcasted_iota(jnp.int32, (LMAX, 128), 1)
    row = lax.broadcasted_iota(jnp.int32, (LMAX, 128), 0)
    bar = jnp.where(row < n, 0.0, -1e30).astype(BF16)
    one = jnp.ones((LMAX, 128), BF16); zero = jnp.zeros((LMAX, 128), BF16)

    def pair(j, _):
        ls = pl.ds(pl.multiple_of(j * 128, 128), 128)
        q2 = q_ref[:, ls]; k2 = k_ref[:, ls]
        vt = v_ref[:, ls].T
        for e in range(2):
            other = 64 * (1 - e)
            ka = jnp.where((lane >= 64) == (e == 1), k2, jnp.where(lane == other, bar, zero))
            qa = jnp.where(lane == other, one, q2)
            for c in range(LMAX // QC):
                s = mm(ka, qa[c*QC:(c+1)*QC], NT)
                top = jnp.max(s, axis=0, keepdims=True)
                p = jnp.exp(s - top)
                tot = jnp.sum(p, axis=0, keepdims=True)
                o = mm(vt[64*e:64*e+64], p.astype(BF16))
                ot_ref[64*e:64*e+64, c*QC:(c+1)*QC] = o / tot
                lse_ref[pl.ds(2*j + e, 1), c*QC:(c+1)*QC] = top + jnp.log(tot)
        o_ref[:, ls] = ot_ref[...].T.astype(BF16)
        return 0
    lax.fori_loop(0, HEADS // 2, pair, 0)

def attend_fwd(tokens, wa, vec8, lens):
    S = tokens.shape[0] // LMAX
    row = pl.BlockSpec((LMAX, D), lambda s, l: (s, 0))
    w = lambda i: pl.BlockSpec((D, D), lambda s, l, i=i: (0, i))
    return pl.pallas_call(
        attend_fwd_kernel,
        out_shape=[jax.ShapeDtypeStruct((S*LMAX, D), BF16)]*4 + [jax.ShapeDtypeStruct((S*16, LMAX), F32)],
        grid_spec=pltpu.PrefetchScalarGridSpec(num_scalar_prefetch=1, grid=(S,),
            in_specs=[row, w(0), w(1), w(2), pl.BlockSpec((8, D), lambda s, l: (0, 0))],
            out_specs=[row]*4 + [pl.BlockSpec((16, LMAX), lambda s, l: (s, 0))],
            scratch_shapes=[pltpu.VMEM((128, LMAX), F32)]),
        name="attend_fwd",
    )(lens, tokens, wa, wa, wa, vec8)

def attend_bwd_kernel(lens_ref, q_ref, k_ref, v_ref, do_ref, lse_ref, tok_ref, dz_ref, wq_ref, wk_ref, wv_ref, dx_ref, dw_ref, small_ref,
                      dq_s, dk_s, dv_s, xt_s, dqt_s, acck, accv, lse_s):
    S = tok_ref.shape[0] // LMAX
    lane = lax.broadcasted_iota(jnp.int32, (LMAX, 128), 1)
    row = lax.broadcasted_iota(jnp.int32, (LMAX, 128), 0)
    one = jnp.ones((LMAX, 128), BF16); zero = jnp.zeros((LMAX, 128), BF16)
    xt_s[...] = tok_ref[...].T

    def task(t, _):
        sl = t // (HEADS // 2); j = t % (HEADS // 2)
        rs = pl.ds(pl.multiple_of(sl * LMAX, LMAX), LMAX)
        ls = pl.ds(pl.multiple_of(j * 128, 128), 128)
        bar = jnp.where(row < lens_ref[sl], 0.0, -1e30).astype(BF16)
        q2 = q_ref[rs, ls]; k2 = k_ref[rs, ls]; v2 = v_ref[rs, ls]; do2 = do_ref[rs, ls]
        kt = k2.T
        for e in range(2):
            other = 64 * (1 - e)
            mine = (lane >= 64) == (e == 1)
            ka = jnp.where(mine, k2, jnp.where(lane == other, bar, zero))
            va = jnp.where(mine, v2, zero)
            qa = jnp.where(lane == other, one, q2)
            lse_row = lse_ref[pl.ds(sl * 16 + 2*j + e, 1), :]
            for c in range(LMAX // QC):
                cs = slice(c*QC, (c+1)*QC)
                s = mm(ka, qa[cs], NT)
                p = jnp.exp(s - lse_row[:, cs])
                dp = mm(va, do2[cs], NT)
                pd = p * dp
                dsum = jnp.sum(pd, axis=0, keepdims=True)
                ds = (pd - p * dsum).astype(BF16)
                dvc = mm(p.astype(BF16), do2[cs])
                dkc = mm(ds, q2[cs])
                if c == 0:
                    dva, dka = dvc, dkc
                else:
                    dva, dka = dva + dvc, dka + dkc
                dqt_s[64*e:64*e+64, cs] = mm(kt[64*e:64*e+64], ds)
            if e == 0:
                accv[...] = dva; acck[...] = dka
            else:
                dv_s[rs, ls] = jnp.where(mine, dva, accv[...]).astype(BF16)
                dk_s[rs, ls] = jnp.where(mine, dka, acck[...]).astype(BF16)
        dq_s[rs, ls] = (dqt_s[...].T * 0.125).astype(BF16)
        return 0
    lax.fori_loop(0, S * (HEADS // 2), task, 0)
    small_ref[...] = jnp.zeros_like(small_ref)
    small_ref[0:1, :] = jnp.sum(dq_s[...].astype(F32), axis=0, keepdims=True)
    small_ref[1:2, :] = jnp.sum(dv_s[...].astype(F32), axis=0, keepdims=True)
    def rows(r, _):
        rr = pl.ds(pl.multiple_of(r * 256, 256), 256)
        dx_ref[rr, :] = dz_ref[rr, :] + mm(dq_s[rr, :], wq_ref[...], NT) + mm(dk_s[rr, :], wk_ref[...], NT) + mm(dv_s[rr, :], wv_ref[...], NT)
        return 0
    lax.fori_loop(0, S * LMAX // 256, rows, 0)
    for i, g in enumerate((dq_s, dk_s, dv_s)):
        def wg(r, _, g=g, i=i):
            rr = pl.ds(pl.multiple_of(r * 256, 256), 256)
            dw_ref[rr, i*D:(i+1)*D] = mm(xt_s[rr, :], g[...]).astype(BF16)
            return 0
        lax.fori_loop(0, D // 256, wg, 0)

def attend_bwd(q, k, v, do, lse, tokens, dz, wa, lens):
    T = tokens.shape[0]
    V = pl.BlockSpec(memory_space=pltpu.VMEM)
    w = lambda i: pl.BlockSpec((D, D), lambda s, l, i=i: (0, i))
    full = lambda a: pl.BlockSpec(a.shape, lambda s, l: (0, 0))
    o = lambda sh: pl.BlockSpec(sh, lambda s, l: (0, 0))
    return pl.pallas_call(
        attend_bwd_kernel,
        out_shape=[jax.ShapeDtypeStruct((T, D), F32), jax.ShapeDtypeStruct((D, 3*D), BF16), jax.ShapeDtypeStruct((8, D), F32)],
        grid_spec=pltpu.PrefetchScalarGridSpec(num_scalar_prefetch=1, grid=(1,),
            in_specs=[full(q)]*4 + [full(lse), full(tokens), full(dz), w(0), w(1), w(2)],
            out_specs=[o((T, D)), o((D, 3*D)), o((8, D))],
            scratch_shapes=[pltpu.VMEM((T, D), BF16)]*3 + [pltpu.VMEM((D, T), BF16), pltpu.VMEM((128, LMAX), F32), pltpu.VMEM((LMAX, 128), F32), pltpu.VMEM((LMAX, 128), F32), pltpu.VMEM((8, 128), F32)]),
        name="attend_bwd",
    )(lens, q, k, v, do, lse, tokens, dz, wa, wa, wa)


M = 256
CF = 512
ERF_P = 0.47 * 0.7071067811865476
ERF_C = [0.26618060444990516, 0.2492263717857657, 0.33168688252906103, -0.11731296726838297, 0.5981763964403582, -0.41518397881696706, 0.08722668027552141]

def gelu_pair(u):
    au = jnp.abs(u)
    t = 1.0 / (1.0 + ERF_P * au)
    e = jnp.exp(-0.5 * (u * u))
    acc = ERF_C[-1] * 0.5
    for cf in ERF_C[-2::-1]:
        acc = acc * t + 0.5 * cf
    h = acc * t * e
    phi = jnp.where(u < 0, h, 1.0 - h)
    return u * phi, phi + u * (e * 0.3989422804014327)

def norm_stats(z):
    mean = jnp.mean(z, axis=-1, keepdims=True)
    c = z - mean
    var = jnp.mean(c * c, axis=-1, keepdims=True)
    r = lax.rsqrt(var + 1e-5)
    return c * r, r

def norm_back(dxh, xh, r):
    return r * (dxh - jnp.mean(dxh, axis=-1, keepdims=True) - xh * jnp.mean(dxh * xh, axis=-1, keepdims=True))

def colsum(x):
    return jnp.sum(x, axis=0, keepdims=True)

def ffn_kernel(lens_ref, o_ref, tok_ref, cot_ref, wo_ref, w1_ref, w2_ref, vec_ref, b1_ref,
               out_ref, dz_ref, do_ref, ot_ref, da_ref, ht_ref, dft_ref, g_ref, du_ref, small_ref,
               gp_s, facc, hacc):
    t = pl.program_id(0); per = LMAX // M
    sl = t // per; base = (t % per) * M
    n = lens_ref[sl] - base

    @pl.when(t == 0)
    def _():
        small_ref[...] = jnp.zeros_like(small_ref)

    @pl.when(n <= 0)
    def _():
        for r in (out_ref, dz_ref, do_ref, ot_ref, da_ref, ht_ref, dft_ref, g_ref, du_ref):
            r[...] = jnp.zeros_like(r)

    @pl.when(n > 0)
    def _():
        v = lambda i: vec_ref[i:i+1, :]
        o = o_ref[...]
        z1 = tok_ref[...].astype(F32) + (mm(o, wo_ref[...]) + v(2))
        xh1, r1 = norm_stats(z1)
        h = xh1 * v(3) + v(4)
        hb = h.astype(BF16)
        facc[...] = jnp.zeros_like(facc)
        def up(j, _):
            cs = pl.ds(pl.multiple_of(j * CF, 128), CF)
            u = mm(hb, w1_ref[:, cs]) + b1_ref[:, cs]
            g, gp = gelu_pair(u)
            gb = g.astype(BF16)
            g_ref[:, cs] = gb
            gp_s[:, cs] = gp
            facc[...] += mm(gb, w2_ref[:, cs], NT)
            return 0
        lax.fori_loop(0, FF // CF, up, 0)
        z2 = h + (facc[...] + v(5))
        xh2, r2 = norm_stats(z2)
        keep = lax.broadcasted_iota(jnp.int32, (M, 1), 0) < n
        out_ref[...] = jnp.where(keep, xh2 * v(6) + v(7), 0.0).astype(BF16)
        dy = jnp.where(keep, cot_ref[...].astype(F32), 0.0)
        small_ref[7:8, :] += colsum(dy)
        small_ref[6:7, :] += colsum(dy * xh2)
        dz2 = norm_back(dy * v(6), xh2, r2)
        df = dz2.astype(BF16)
        small_ref[5:6, :] += colsum(df.astype(F32))
        hacc[...] = dz2
        def down(j, _):
            cs = pl.ds(pl.multiple_of(j * CF, 128), CF)
            dg = mm(df, w2_ref[:, cs])
            du = (gp_s[:, cs] * dg).astype(BF16)
            du_ref[:, cs] = du
            b1g_ref = small_ref
            gp_s[0:1, cs] = colsum(du.astype(F32))
            hacc[...] += mm(du, w1_ref[:, cs], NT)
            return 0
        lax.fori_loop(0, FF // CF, down, 0)
        for i in range(4):
            small_ref[8+i:9+i, :] += gp_s[0:1, i*D:(i+1)*D]
        dh = hacc[...]
        small_ref[4:5, :] += colsum(dh)
        small_ref[3:4, :] += colsum(dh * xh1)
        dz1 = norm_back(dh * v(3), xh1, r1)
        da = dz1.astype(BF16)
        small_ref[2:3, :] += colsum(da.astype(F32))
        dz_ref[...] = dz1
        da_ref[...] = da
        do_ref[...] = mm(da, wo_ref[...], NT).astype(BF16)
        ot_ref[...] = o.T
        ht_ref[...] = hb.T
        dft_ref[...] = df.T

def tile_order(lens, T):
    per = LMAX // M
    tiles = T // M
    live = (jnp.arange(tiles) % per) * M < lens[jnp.arange(tiles) // per]
    nl = jnp.sum(live.astype(jnp.int32))
    before = jnp.cumsum(live.astype(jnp.int32)) - live
    dead = jnp.arange(tiles) - before
    return jnp.where(live, before, nl + dead).astype(jnp.int32), nl

def ffn_rows(o, tokens, cot, wa, wf, vec8, b1, lens, order):
    T = tokens.shape[0]
    row = pl.BlockSpec((M, D), lambda t, l, q: (t, 0))
    one = lambda sh, i: pl.BlockSpec(sh, lambda t, l, q: (0, i), pipeline_mode=pl.Buffered(1))
    comp = lambda w: pl.BlockSpec((M, w), lambda t, l, q: (q[t], 0))
    compT = pl.BlockSpec((D, M), lambda t, l, q: (0, q[t]))
    S = jax.ShapeDtypeStruct
    def kern(lens_ref, order_ref, *refs): return ffn_kernel(lens_ref, *refs)
    return pl.pallas_call(
        kern,
        out_shape=[S((T, D), BF16), S((T, D), F32), S((T, D), BF16), S((D, T), BF16), S((T, D), BF16), S((D, T), BF16), S((D, T), BF16), S((T, FF), BF16), S((T, FF), BF16), S((16, D), F32)],
        grid_spec=pltpu.PrefetchScalarGridSpec(num_scalar_prefetch=2, grid=(T // M,),
            in_specs=[row, row, row, one((D, D), 3), one((D, FF), 0), one((D, FF), 1), one((8, D), 0), one((1, FF), 0)],
            out_specs=[row, row, row, compT, comp(D), compT, compT, comp(FF), comp(FF), pl.BlockSpec((16, D), lambda t, l, q: (0, 0))],
            scratch_shapes=[pltpu.VMEM((M, FF), F32), pltpu.VMEM((M, D), F32), pltpu.VMEM((M, D), F32)]),
        name="ffn_rows",
    )(lens, order, o, tokens, cot, wa, wf, wf, vec8, b1)

NB = 512
def ffn_grads_kernel(nl_ref, ht_ref, dft_ref, du_ref, g_ref, out_ref):
    i = pl.program_id(0)
    half = FF // NB
    T = ht_ref.shape[1]
    k4 = (nl_ref[0] * M + 255) // 256
    for s in range(2):
        lt, r = ((ht_ref, du_ref), (dft_ref, g_ref))[s]
        for kk in range(1, T // 256 + 1):
            @pl.when(((i < half) == (s == 0)) & (k4 == kk))
            def _(lt=lt, r=r, K=kk*256):
                out_ref[...] = mm(lt[:, :K], r[:K, :]).astype(BF16)

def ffn_grads(ht, dft, du, g, nl):
    T = ht.shape[1]; half = FF // NB
    full = pl.BlockSpec((D, T), lambda i, n: (0, 0), pipeline_mode=pl.Buffered(1))
    return pl.pallas_call(
        ffn_grads_kernel,
        out_shape=jax.ShapeDtypeStruct((D, 2*FF), BF16),
        grid_spec=pltpu.PrefetchScalarGridSpec(num_scalar_prefetch=1, grid=(2*half,),
            in_specs=[full, full, pl.BlockSpec((T, NB), lambda i, n: (0, jnp.minimum(i, half-1))), pl.BlockSpec((T, NB), lambda i, n: (0, jnp.maximum(i-half, 0)))],
            out_specs=pl.BlockSpec((D, NB), lambda i, n: (0, i))),
        name="ffn_grads",
    )(nl, ht, dft, du, g)


class Spot:
    def __init__(self, na, ndp):
        self.na, self.ndp = na, ndp
        self.me = lax.axis_index("fsdp"); self.p = lax.axis_index("dp")
        self.a = self.me // 4; self.b = (self.me // 2) % 2; self.c = self.me % 2
        self.par = self.p % 2
        self.b2 = self.b + (1 - 2*self.b)*(1 - self.par); self.c2 = self.c + (1 - 2*self.c)*self.par
        self.b3 = self.b + (1 - 2*self.b)*self.par; self.c3 = self.c + (1 - 2*self.c)*(1 - self.par)

    def at(self, a, flip2=0, flip3=0):
        if flip2 and flip3:
            b, c = 1 - self.b, 1 - self.c
        elif flip2:
            b, c = self.b2, self.c2
        elif flip3:
            b, c = self.b3, self.c3
        else:
            b, c = self.b, self.c
        return (a*2 + b)*2 + c

    def dev(self, a, flip2=0, flip3=0):
        return (self.at(a, flip2, flip3), self.p)

    def barrier(self):
        sem = pltpu.get_barrier_semaphore()
        up, down = self.a < self.na - 1, self.a > 0
        def sig(dev):
            pl.semaphore_signal(sem, inc=1, device_id=dev, device_id_type=MESH)
        @pl.when(up)
        def _(): sig(self.dev(self.a + 1))
        @pl.when(down)
        def _(): sig(self.dev(self.a - 1))
        sig(self.dev(self.a, 1, 0)); sig(self.dev(self.a, 0, 1))
        for q in range(1, self.ndp): sig((self.me, (self.p + q) % self.ndp))
        pl.semaphore_wait(sem, 1 + self.ndp + up.astype(jnp.int32) + down.astype(jnp.int32))

class Gather:
    def __init__(self, spot, own, view, ssem, rsem, dp_view=None):
        self.s, self.own, self.view, self.ss, self.rs, self.dp_view = spot, own, view, ssem, rsem, dp_view
        na = spot.na
        self.JU, self.JD = 0, na - 1
        self.J2 = 2*(na - 1); self.J3 = self.J2 + na; self.JP = self.J3 + 2*na
        self.log = []

    @staticmethod
    def slots(na, ndp):
        return 2*(na - 1) + na + 2*na + (ndp - 1)*4*na

    def copy(self, f, dev, j, r=None, src=None):
        v = self.view(f)
        return pltpu.make_async_remote_copy(src_ref=v if src is None else src, dst_ref=v, send_sem=self.ss.at[j],
                                            recv_sem=self.rs.at[j if r is None else r], device_id=dev, device_id_type=MESH)

    def send(self, cond, make):
        make().start()
        self.log.append((cond, make))

    def wait(self, f, j):
        self.copy(f, (self.s.me, self.s.p), j).wait_recv()

    def dp(self, cond, f):
        if self.dp_view is None: return
        s = self.s
        for q in range(1, s.ndp):
            self.send(cond, lambda q=q: self.copy(f(), (s.me, (s.p + q) % s.ndp), self.JP + (q-1)*4*s.na + f()))

    def start(self):
        s = self.s; na = s.na
        up, down = s.a < na - 1, s.a > 0
        @pl.when(up)
        def _(): self.send(up, lambda: self.copy(s.me, s.dev(s.a + 1), self.JU, src=self.own))
        @pl.when(down)
        def _(): self.send(down, lambda: self.copy(s.me, s.dev(s.a - 1), self.JD, src=self.own))
        self.send(None, lambda: self.copy(s.me, s.dev(s.a, 1, 0), self.J2 + s.a, src=self.own))
        self.send(None, lambda: self.copy(s.me, s.dev(s.a, 0, 1), self.J3 + s.a*2, src=self.own))

    def events(self):
        s = self.s; na = s.na
        def chain(up, k):
            a = s.a - 1 - k if up else s.a + 1 + k
            cond = a >= 0 if up else a < na
            fwd = s.a < na - 1 if up else s.a > 0
            both = cond & fwd
            j = (self.JU if up else self.JD) + k
            def go():
                self.wait(s.at(a), j)
                if k < na - 2:
                    @pl.when(fwd)
                    def _(): self.send(both, lambda: self.copy(s.at(a), s.dev(s.a + 1 if up else s.a - 1), j + 1))
                self.send(cond, lambda: self.copy(s.at(a), s.dev(s.a, 1, 0), self.J2 + a))
                self.send(cond, lambda: self.copy(s.at(a), s.dev(s.a, 0, 1), self.J3 + a*2))
                self.dp(cond, lambda: s.at(a))
            return cond, go
        def second(a, cond):
            def go():
                self.wait(s.at(a, 1, 0), self.J2 + a)
                self.send(cond, lambda: self.copy(s.at(a, 1, 0), s.dev(s.a, 0, 1), self.J3 + a*2 + 1))
                self.dp(cond, lambda: s.at(a, 1, 0))
            return cond, go
        def third(a, cond, x):
            def go():
                self.wait(s.at(a, x, 1), self.J3 + a*2 + x)
                self.dp(cond, lambda: s.at(a, x, 1))
            return cond, go
        levels = [[(s.a, None)]]
        for k in range(na - 1):
            levels.append([(s.a - 1 - k, s.a - 1 - k >= 0), (s.a + 1 + k, s.a + 1 + k < na)])
        out = []
        for k in range(na + 2):
            if k < na - 1: out += [chain(True, k), chain(False, k)]
            if k < na:
                out += [second(a, cd) for a, cd in levels[k]]
                out += [third(a, cd, 0) for a, cd in levels[k]]
            if 0 < k <= na:
                out += [third(a, cd, 1) for a, cd in levels[k-1]]
        return out

    def finish(self):
        s = self.s
        if self.dp_view is not None:
            for q in range(1, s.ndp):
                def body(f, _):
                    @pl.when(f != s.me)
                    def _():
                        j = self.JP + (q-1)*4*s.na + f
                        v = self.dp_view(f, (s.p + s.ndp - q) % s.ndp)
                        pltpu.make_async_remote_copy(src_ref=v, dst_ref=v, send_sem=self.ss.at[j], recv_sem=self.rs.at[j], device_id=(s.me, s.p), device_id_type=MESH).wait_recv()
                    return 0
                lax.fori_loop(0, 4*s.na, body, 0)
        self.drain()

    def drain(self):
        for cond, make in self.log:
            if cond is None:
                make().wait_send()
            else:
                @pl.when(cond)
                def _(): make().wait_send()

def run_event(ev):
    cond, go = ev
    if cond is None: go()
    else: pl.when(cond)(go)

def forward_kernel(na, ndp, wa_sh, wf_sh, vecs, bff, lens_ref, tok_ref,
                   wa_out, wf_out, vec8, bias, q_ref, k_ref, v_ref, o_ref, lse_ref,
                   wa_c, wf_c, ex, wqkv, ot_s, tr_s, lsem, *sems):
    s = Spot(na, ndp)
    R = wa_sh.shape[0]
    tr_s[...] = jnp.zeros_like(tr_s)
    tr_s[0:R, 0:8] = vecs[...]
    ex[s.me, 0:8, :] = tr_s[...].T[0:8, :].astype(BF16).astype(F32)
    for j in range(4):
        ex[s.me, 8+j:9+j, 0:R] = bff[0:1, j*R:(j+1)*R].astype(BF16).astype(F32)
    wa_c[...] = wa_sh[...].astype(BF16)
    gs = []
    for i, (c, out) in enumerate(((wa_c, wa_out), (wf_c, wf_out))):
        w = c.shape[1] // ndp
        cols = lambda q, w=w: pl.ds(pl.multiple_of(q*w, 128), w)
        gs.append(Gather(s, c.at[:, cols(s.p)], lambda f, out=out, cols=cols: out.at[f, :, cols(s.p)], sems[2*i], sems[2*i+1],
                         lambda f, q, out=out, cols=cols: out.at[f, :, cols(q)]))
    gx = Gather(s, ex.at[s.me], lambda f: ex.at[f], sems[4], sems[5])
    ga, gf = gs
    s.barrier()
    gx.start(); ga.start()
    locs = [pltpu.make_async_copy(wa_c, wa_out.at[s.me], lsem.at[0])]
    locs[0].start()
    wf_c[...] = wf_sh[...].astype(BF16)
    locs.append(pltpu.make_async_copy(wf_c, wf_out.at[s.me], lsem.at[1]))
    locs[1].start()
    ea, exv, ef = ga.events(), gx.events(), gf.events()
    cut = 2 + 2*2
    started = False
    for n, (u, v) in enumerate(zip(ea, exv)):
        run_event(v); run_event(u)
        if n == len(ea)*2//5:
            gf.start(); started = True
    for q in range(1, ndp):
        def body(f, _, q=q):
            @pl.when(f != s.me)
            def _():
                j = ga.JP + (q-1)*4*na + f
                v = ga.dp_view(f, (s.p + ndp - q) % ndp)
                pltpu.make_async_remote_copy(src_ref=v, dst_ref=v, send_sem=ga.ss.at[j], recv_sem=ga.rs.at[j], device_id=(s.me, s.p), device_id_type=MESH).wait_recv()
            return 0
        lax.fori_loop(0, 4*na, body, 0)
    locs[0].wait()
    load = pltpu.make_async_copy(wa_out.at[:, :, 0:3*D], wqkv, lsem.at[2])
    load.start()
    for f in range(4*na):
        vec8[:, f*R:(f+1)*R] = ex[f, 0:8, 0:R]
        for j in range(4):
            bias[0:1, (f*4+j)*R:(f*4+j+1)*R] = ex[f, 8+j:9+j, 0:R]
    load.wait()
    S = tok_ref.shape[0] // LMAX
    lane = lax.broadcasted_iota(jnp.int32, (LMAX, 128), 1)
    row = lax.broadcasted_iota(jnp.int32, (LMAX, 128), 0)
    one = jnp.ones((LMAX, 128), BF16); zero = jnp.zeros((LMAX, 128), BF16)
    PAIRS = HEADS // 2
    ntask = S*(3 + PAIRS)
    per = -(-len(ef) // ntask)
    def events_after(i, first, last):
        for t in range(first, last):
            evs = ef[t*per:(t+1)*per]
            if evs:
                @pl.when(i == t)
                def _():
                    for e in evs: run_event(e)
    w3 = wqkv.shape
    def proj(sl, which):
        rs = pl.ds(pl.multiple_of(sl*LMAX, LMAX), LMAX)
        x = tok_ref[rs, :]
        y = mm(x, wqkv[:, :, which*D:(which+1)*D].reshape(4*na*R, D))
        if which == 0: q_ref[rs, :] = ((y + vec8[0:1, :]).astype(BF16) * 0.125).astype(BF16)
        elif which == 1: k_ref[rs, :] = y.astype(BF16)
        else: v_ref[rs, :] = (y + vec8[1:2, :]).astype(BF16)
    def step1(i, _):
        for which in range(3):
            @pl.when(i % 3 == which)
            def _(): proj(i // 3, which)
        events_after(i, 0, 3*S)
        return 0
    lax.fori_loop(0, 3*S, step1, 0)
    def step2(i, _):
        sl = i // PAIRS; j = i % PAIRS
        rs = pl.ds(pl.multiple_of(sl*LMAX, LMAX), LMAX)
        ls = pl.ds(pl.multiple_of(j * 128, 128), 128)
        bar = jnp.where(row < lens_ref[sl], 0.0, -1e30).astype(BF16)
        q2 = q_ref[rs, ls]; k2 = k_ref[rs, ls]
        vt = v_ref[rs, ls].T
        for e in range(2):
            other = 64 * (1 - e)
            ka = jnp.where((lane >= 64) == (e == 1), k2, jnp.where(lane == other, bar, zero))
            qa = jnp.where(lane == other, one, q2)
            for c in range(LMAX // QC):
                sc = mm(ka, qa[c*QC:(c+1)*QC], NT)
                top = jnp.max(sc, axis=0, keepdims=True)
                p = jnp.exp(sc - top)
                tot = jnp.sum(p, axis=0, keepdims=True)
                o = mm(vt[64*e:64*e+64], p.astype(BF16))
                ot_s[64*e:64*e+64, c*QC:(c+1)*QC] = o / tot
                lse_ref[pl.ds(sl*16 + 2*j + e, 1), c*QC:(c+1)*QC] = top + jnp.log(tot)
        o_ref[rs, ls] = ot_s[...].T.astype(BF16)
        events_after(i + 3*S, 3*S, ntask)
        return 0
    lax.fori_loop(0, S*PAIRS, step2, 0)
    gf.finish(); gx.finish()
    ga.drain()
    locs[1].wait()

def forward(mesh_shape, wa_sh, wf_sh, vecs, bff, lens, tokens, cid):
    F, ndp = mesh_shape
    na = F // 4; R = vecs.shape[0]; T = tokens.shape[0]
    NS = Gather.slots(na, ndp)
    S = jax.ShapeDtypeStruct
    V = pl.BlockSpec(memory_space=pltpu.VMEM); A = pl.BlockSpec(memory_space=pl.ANY)
    DMA = pltpu.SemaphoreType.DMA
    return pl.pallas_call(
        functools.partial(forward_kernel, na, ndp),
        out_shape=[S((F, R, 4*D), BF16), S((F, R, 2*FF), BF16), S((8, D), F32), S((1, FF), F32)] + [S((T, D), BF16)]*4 + [S((T//LMAX*16, LMAX), F32)],
        in_specs=[V, V, V, V, pl.BlockSpec(memory_space=pltpu.SMEM), V],
        out_specs=[A, A] + [V]*7,
        scratch_shapes=[pltpu.VMEM((R, 4*D), BF16), pltpu.VMEM((R, 2*FF), BF16), pltpu.VMEM((F, 16, 128), F32), pltpu.VMEM((F, R, 3*D), BF16),
                        pltpu.VMEM((128, LMAX), F32), pltpu.VMEM((128, 128), F32), DMA((3,))] + [DMA((NS,))]*6,
        compiler_params=pltpu.CompilerParams(collective_id=cid, has_side_effects=True, vmem_limit_bytes=56 << 20),
        name="gather_attend",
    )(wa_sh, wf_sh, vecs, bff, lens, tokens)


def adam_update(gradient, moment, second, master, adam_step, learn_rate):
    count = adam_step[0].astype(jnp.float32)
    moment_new = 0.9 * moment + 0.1 * gradient
    second_new = 0.98 * second + 0.02 * gradient * gradient
    first_fix = moment_new / (1.0 - jnp.power(0.9, count))
    second_fix = second_new / (1.0 - jnp.power(0.98, count))
    master_new = master - learn_rate[0] * (
        first_fix / (jnp.sqrt(second_fix) + 1e-06) + 0.01 * master
    )
    return (moment_new, second_new, master_new, master_new.astype(jnp.bfloat16))


def local(mesh_shape, tokens, cotangent, lengths, adam_step, learn_rate, attn_w, attn_m, attn_v, ffn_w, ffn_m, ffn_v,
          vecs, vecs_m, vecs_v, b_ff, bff_m, bff_v):
    shards, rows = mesh_shape[0], vecs.shape[0]
    T = tokens.shape[0]
    attn_low, ffn_low, vec8, bias, q, k, v, o, lse = forward(
        mesh_shape, attn_w, ffn_w, vecs, b_ff.reshape(1, 4 * rows), lengths, tokens, 1)
    attn_low = attn_low.reshape(D, 4 * D)
    ffn_low = ffn_low.reshape(D, 2 * FF)
    order, live = tile_order(lengths, T)
    outputs, dz1, do, ot, da, ht, dft, g, du, small_ffn = ffn_rows(
        o, tokens, cotangent, attn_low, ffn_low, vec8, bias, lengths, order)
    grad_ffn = ffn_grads(ht, dft, du, g, live[None])
    grad_wo = mm(ot, da).astype(BF16)
    input_grad, grad_qkv, small_attn = attend_bwd(q, k, v, do, lse, tokens, dz1, attn_low, lengths)
    grad_attn = jnp.concatenate([grad_qkv, grad_wo], axis=1)
    small = jnp.concatenate([small_attn[:2], small_ffn[2:]], axis=0)
    summed_attn, summed_ffn, summed_small = reduce_scatter(
        mesh_shape, [grad_attn.reshape(shards, rows, 4 * D), grad_ffn.reshape(shards, rows, 2 * FF)], small, 2)
    mine = lax.axis_index("fsdp")
    summed_vecs = lax.dynamic_slice(summed_small, (0, mine * rows), (8, rows)).T
    summed_bias = lax.dynamic_slice(summed_small[8:12].reshape(FF), (mine * 4 * rows,), (4 * rows,))
    attn_new = adam_update(summed_attn, attn_m, attn_v, attn_w, adam_step, learn_rate)
    ffn_new = adam_update(summed_ffn, ffn_m, ffn_v, ffn_w, adam_step, learn_rate)
    vecs_new = adam_update(summed_vecs, vecs_m, vecs_v, vecs, adam_step, learn_rate)
    bff_new = adam_update(summed_bias, bff_m, bff_v, b_ff, adam_step, learn_rate)
    return (outputs, input_grad, summed_attn, *attn_new, summed_ffn, *ffn_new, summed_vecs, *vecs_new, summed_bias, *bff_new)


def solution(mesh):
    both, rows, whole = P(("fsdp", "dp")), P("fsdp"), P()
    return jax.shard_map(
        functools.partial(local, (mesh.shape["fsdp"], mesh.shape["dp"])),
        mesh=mesh,
        in_specs=(both, both, both, whole, whole) + (rows,) * 12,
        out_specs=(both, both) + (rows,) * 20,
        check_vma=False,
    )
```

```python
import functools

import jax
import jax.numpy as jnp
from jax import lax
from jax.experimental import pallas as pl
from jax.experimental.pallas import tpu as pltpu
from jax.sharding import PartitionSpec as P

MESH = pl.DeviceIdType.MESH

D = 768; HEADS = 12; HEAD = 64; FF = 3072; LMAX = 512
NN = (((1,), (0,)), ((), ()))
NT = (((1,), (1,)), ((), ()))
TN = (((0,), (0,)), ((), ()))
F32 = jnp.float32; BF16 = jnp.bfloat16
QC = 256

def mm(a, b, dims=NN):
    return lax.dot_general(a, b, dims, preferred_element_type=F32)

def attend_fwd_kernel(lens_ref, tok_ref, wq_ref, wk_ref, wv_ref, vec_ref, q_ref, k_ref, v_ref, o_ref, lse_ref, ot_ref):
    n = lens_ref[pl.program_id(0)]
    x = tok_ref[...]
    q_ref[...] = ((mm(x, wq_ref[...]) + vec_ref[0:1, :]).astype(BF16) * 0.125).astype(BF16)
    k_ref[...] = mm(x, wk_ref[...]).astype(BF16)
    v_ref[...] = (mm(x, wv_ref[...]) + vec_ref[1:2, :]).astype(BF16)
    lane = lax.broadcasted_iota(jnp.int32, (LMAX, 128), 1)
    row = lax.broadcasted_iota(jnp.int32, (LMAX, 128), 0)
    bar = jnp.where(row < n, 0.0, -1e30).astype(BF16)
    one = jnp.ones((LMAX, 128), BF16); zero = jnp.zeros((LMAX, 128), BF16)

    def pair(j, _):
        ls = pl.ds(pl.multiple_of(j * 128, 128), 128)
        q2 = q_ref[:, ls]; k2 = k_ref[:, ls]
        vt = v_ref[:, ls].T
        for e in range(2):
            other = 64 * (1 - e)
            ka = jnp.where((lane >= 64) == (e == 1), k2, jnp.where(lane == other, bar, zero))
            qa = jnp.where(lane == other, one, q2)
            for c in range(LMAX // QC):
                s = mm(ka, qa[c*QC:(c+1)*QC], NT)
                top = jnp.max(s, axis=0, keepdims=True)
                p = jnp.exp(s - top)
                tot = jnp.sum(p, axis=0, keepdims=True)
                o = mm(vt[64*e:64*e+64], p.astype(BF16))
                ot_ref[64*e:64*e+64, c*QC:(c+1)*QC] = o / tot
                lse_ref[pl.ds(2*j + e, 1), c*QC:(c+1)*QC] = top + jnp.log(tot)
        o_ref[:, ls] = ot_ref[...].T.astype(BF16)
        return 0
    lax.fori_loop(0, HEADS // 2, pair, 0)

def attend_fwd(tokens, wa, vec8, lens):
    S = tokens.shape[0] // LMAX
    row = pl.BlockSpec((LMAX, D), lambda s, l: (s, 0))
    w = lambda i: pl.BlockSpec((D, D), lambda s, l, i=i: (0, i))
    return pl.pallas_call(
        attend_fwd_kernel,
        out_shape=[jax.ShapeDtypeStruct((S*LMAX, D), BF16)]*4 + [jax.ShapeDtypeStruct((S*16, LMAX), F32)],
        grid_spec=pltpu.PrefetchScalarGridSpec(num_scalar_prefetch=1, grid=(S,),
            in_specs=[row, w(0), w(1), w(2), pl.BlockSpec((8, D), lambda s, l: (0, 0))],
            out_specs=[row]*4 + [pl.BlockSpec((16, LMAX), lambda s, l: (s, 0))],
            scratch_shapes=[pltpu.VMEM((128, LMAX), F32)]),
        name="attend_fwd",
    )(lens, tokens, wa, wa, wa, vec8)

def attend_bwd_kernel(lens_ref, q_ref, k_ref, v_ref, do_ref, lse_ref, tok_ref, dz_ref, wq_ref, wk_ref, wv_ref, dx_ref, dw_ref, small_ref,
                      dq_s, dk_s, dv_s, xt_s, dqt_s, acck, accv, lse_s):
    S = tok_ref.shape[0] // LMAX
    lane = lax.broadcasted_iota(jnp.int32, (LMAX, 128), 1)
    row = lax.broadcasted_iota(jnp.int32, (LMAX, 128), 0)
    one = jnp.ones((LMAX, 128), BF16); zero = jnp.zeros((LMAX, 128), BF16)
    xt_s[...] = tok_ref[...].T

    def task(t, _):
        sl = t // (HEADS // 2); j = t % (HEADS // 2)
        rs = pl.ds(pl.multiple_of(sl * LMAX, LMAX), LMAX)
        ls = pl.ds(pl.multiple_of(j * 128, 128), 128)
        bar = jnp.where(row < lens_ref[sl], 0.0, -1e30).astype(BF16)
        q2 = q_ref[rs, ls]; k2 = k_ref[rs, ls]; v2 = v_ref[rs, ls]; do2 = do_ref[rs, ls]
        kt = k2.T
        for e in range(2):
            other = 64 * (1 - e)
            mine = (lane >= 64) == (e == 1)
            ka = jnp.where(mine, k2, jnp.where(lane == other, bar, zero))
            va = jnp.where(mine, v2, zero)
            qa = jnp.where(lane == other, one, q2)
            lse_row = lse_ref[pl.ds(sl * 16 + 2*j + e, 1), :]
            for c in range(LMAX // QC):
                cs = slice(c*QC, (c+1)*QC)
                s = mm(ka, qa[cs], NT)
                p = jnp.exp(s - lse_row[:, cs])
                dp = mm(va, do2[cs], NT)
                pd = p * dp
                dsum = jnp.sum(pd, axis=0, keepdims=True)
                ds = (pd - p * dsum).astype(BF16)
                dvc = mm(p.astype(BF16), do2[cs])
                dkc = mm(ds, q2[cs])
                if c == 0:
                    dva, dka = dvc, dkc
                else:
                    dva, dka = dva + dvc, dka + dkc
                dqt_s[64*e:64*e+64, cs] = mm(kt[64*e:64*e+64], ds)
            if e == 0:
                accv[...] = dva; acck[...] = dka
            else:
                dv_s[rs, ls] = jnp.where(mine, dva, accv[...]).astype(BF16)
                dk_s[rs, ls] = jnp.where(mine, dka, acck[...]).astype(BF16)
        dq_s[rs, ls] = (dqt_s[...].T * 0.125).astype(BF16)
        return 0
    lax.fori_loop(0, S * (HEADS // 2), task, 0)
    small_ref[...] = jnp.zeros_like(small_ref)
    small_ref[0:1, :] = jnp.sum(dq_s[...].astype(F32), axis=0, keepdims=True)
    small_ref[1:2, :] = jnp.sum(dv_s[...].astype(F32), axis=0, keepdims=True)
    def rows(r, _):
        rr = pl.ds(pl.multiple_of(r * 256, 256), 256)
        dx_ref[rr, :] = dz_ref[rr, :] + mm(dq_s[rr, :], wq_ref[...], NT) + mm(dk_s[rr, :], wk_ref[...], NT) + mm(dv_s[rr, :], wv_ref[...], NT)
        return 0
    lax.fori_loop(0, S * LMAX // 256, rows, 0)
    for i, g in enumerate((dq_s, dk_s, dv_s)):
        def wg(r, _, g=g, i=i):
            rr = pl.ds(pl.multiple_of(r * 256, 256), 256)
            dw_ref[rr, i*D:(i+1)*D] = mm(xt_s[rr, :], g[...]).astype(BF16)
            return 0
        lax.fori_loop(0, D // 256, wg, 0)

def attend_bwd(q, k, v, do, lse, tokens, dz, wa, lens):
    T = tokens.shape[0]
    V = pl.BlockSpec(memory_space=pltpu.VMEM)
    w = lambda i: pl.BlockSpec((D, D), lambda s, l, i=i: (0, i))
    full = lambda a: pl.BlockSpec(a.shape, lambda s, l: (0, 0))
    o = lambda sh: pl.BlockSpec(sh, lambda s, l: (0, 0))
    return pl.pallas_call(
        attend_bwd_kernel,
        out_shape=[jax.ShapeDtypeStruct((T, D), F32), jax.ShapeDtypeStruct((D, 3*D), BF16), jax.ShapeDtypeStruct((8, D), F32)],
        grid_spec=pltpu.PrefetchScalarGridSpec(num_scalar_prefetch=1, grid=(1,),
            in_specs=[full(q)]*4 + [full(lse), full(tokens), full(dz), w(0), w(1), w(2)],
            out_specs=[o((T, D)), o((D, 3*D)), o((8, D))],
            scratch_shapes=[pltpu.VMEM((T, D), BF16)]*3 + [pltpu.VMEM((D, T), BF16), pltpu.VMEM((128, LMAX), F32), pltpu.VMEM((LMAX, 128), F32), pltpu.VMEM((LMAX, 128), F32), pltpu.VMEM((8, 128), F32)]),
        name="attend_bwd",
    )(lens, q, k, v, do, lse, tokens, dz, wa, wa, wa)


M = 256
NB = 768


def gelu_pair(u):
    phi = 0.5 * (1.0 + lax.erf(u * 0.7071067811865476))
    e = jnp.exp(-0.5 * (u * u))
    return u * phi, phi + u * (e * 0.3989422804014327)

def norm_stats(z):
    mean = jnp.mean(z, axis=-1, keepdims=True)
    c = z - mean
    var = jnp.mean(c * c, axis=-1, keepdims=True)
    r = lax.rsqrt(var + 1e-5)
    return c * r, r

def norm_back(dxh, xh, r):
    return r * (dxh - jnp.mean(dxh, axis=-1, keepdims=True) - xh * jnp.mean(dxh * xh, axis=-1, keepdims=True))

def colsum(x):
    return jnp.sum(x, axis=0, keepdims=True)

def ffn_kernel(tiles, lens_ref, o_ref, tok_ref, cot_ref, wa_h, wf_h, vec_ref, b1_ref,
               out_ref, dz_ref, do_ref, gf_ref, small_ref,
               wo_ref, w1_ref, w2_ref, gp_s, ot_s, da_s, ht_s, dft_s, g_s, du_s, sem):
    t = pl.program_id(0); per = LMAX // M
    live = [(lens_ref[u // per] > (u % per) * M).astype(jnp.int32) for u in range(tiles)]
    count = sum(live)
    loads = [pltpu.make_async_copy(wa_h.at[:, 3*D:4*D], wo_ref, sem.at[0]), pltpu.make_async_copy(wf_h.at[:, 0:FF], w1_ref, sem.at[1]), pltpu.make_async_copy(wf_h.at[:, FF:2*FF], w2_ref, sem.at[2])]
    def arrived(i):
        @pl.when(t == 0)
        def _(): loads[i].wait()

    @pl.when(t == 0)
    def _():
        for l in loads: l.start()
        small_ref[...] = jnp.zeros_like(small_ref)

    n = lens_ref[jnp.minimum(t, tiles - 1) // per] - (t % per) * M

    @pl.when((t < tiles) & (n <= 0))
    def _():
        for r in (out_ref, dz_ref, do_ref):
            r[...] = jnp.zeros_like(r)

    @pl.when((t < tiles) & (n > 0))
    def _():
        pos = sum(live[u] * (u < t).astype(jnp.int32) for u in range(tiles))
        rs = pl.ds(pl.multiple_of(pos * M, M), M)
        v = lambda i: vec_ref[i:i+1, :]
        o = o_ref[...]
        arrived(0)
        z1 = tok_ref[...].astype(F32) + (mm(o, wo_ref[...]) + v(2))
        ot_s[:, rs] = o.T
        xh1, r1 = norm_stats(z1)
        h = xh1 * v(3) + v(4)
        hb = h.astype(BF16)
        ht_s[:, rs] = hb.T
        arrived(1)
        arrived(2)
        f = None
        CF = 512
        cuts = [slice(c, c + CF) for c in range(0, FF, CF)]
        u = mm(hb, w1_ref[:, cuts[0]]) + b1_ref[:, cuts[0]]
        for j, cs in enumerate(cuts):
            nxt = mm(hb, w1_ref[:, cuts[j+1]]) + b1_ref[:, cuts[j+1]] if j + 1 < len(cuts) else None
            g, gp = gelu_pair(u)
            gb = g.astype(BF16)
            g_s[rs, cs] = gb
            gp_s[:, cs] = gp
            part = mm(gb, w2_ref[:, cs], NT)
            f = part if f is None else f + part
            u = nxt
        z2 = h + (f + v(5))
        xh2, r2 = norm_stats(z2)
        keep = lax.broadcasted_iota(jnp.int32, (M, 1), 0) < n
        out_ref[...] = jnp.where(keep, xh2 * v(6) + v(7), 0.0).astype(BF16)
        dy = jnp.where(keep, cot_ref[...].astype(F32), 0.0)
        small_ref[7:8, :] += colsum(dy)
        small_ref[6:7, :] += colsum(dy * xh2)
        dz2 = norm_back(dy * v(6), xh2, r2)
        df = dz2.astype(BF16)
        dft_s[:, rs] = df.T
        small_ref[5:6, :] += colsum(df.astype(F32))
        du = (gp_s[...] * mm(df, w2_ref[...])).astype(BF16)
        du_s[rs, :] = du
        db1 = colsum(du.astype(F32))
        for i in range(4):
            small_ref[8+i:9+i, :] += db1[:, i*D:(i+1)*D]
        dh = dz2 + mm(du, w1_ref[...], NT)
        small_ref[4:5, :] += colsum(dh)
        small_ref[3:4, :] += colsum(dh * xh1)
        dz1 = norm_back(dh * v(3), xh1, r1)
        da = dz1.astype(BF16)
        small_ref[2:3, :] += colsum(da.astype(F32))
        dz_ref[...] = dz1
        da_s[rs, :] = da
        do_ref[...] = mm(da, wo_ref[...], NT).astype(BF16)

    i = t - tiles
    half = FF // NB
    for kk in range(1, tiles + 1):
        K = kk*M
        for lt, r, c0, n0, n1 in ((ht_s, du_s, 0, 0, half), (dft_s, g_s, half, half, 2*half), (ot_s, da_s, 2*half, 2*half, 2*half + 1)):
            @pl.when((count == kk) & (i >= n0) & (i < n1))
            def _(lt=lt, r=r, K=K, c0=c0):
                cs = pl.ds(pl.multiple_of((i - c0) * NB, NB), NB)
                gf_ref[...] = mm(lt[:, :K], r[:K, cs]).astype(BF16)

def ffn(o, tokens, cot, wa, wf, vec8, b1, lens):
    T = tokens.shape[0]; tiles = T // M; chunks = 2*FF // NB + 1
    row = pl.BlockSpec((M, D), lambda t, l: (jnp.minimum(t, tiles - 1), 0))
    one = lambda sh: pl.BlockSpec(sh, lambda t, l: (0, 0))
    A = pl.BlockSpec(memory_space=pl.ANY)
    S = jax.ShapeDtypeStruct
    B = lambda *sh: pltpu.VMEM(sh, BF16)
    return pl.pallas_call(
        functools.partial(ffn_kernel, tiles),
        out_shape=[S((T, D), BF16), S((T, D), F32), S((T, D), BF16), S((D, chunks*NB), BF16), S((16, D), F32)],
        grid_spec=pltpu.PrefetchScalarGridSpec(num_scalar_prefetch=1, grid=(tiles + chunks,),
            in_specs=[row, row, row, A, A, one((8, D)), one((1, FF))],
            out_specs=[row, row, row, pl.BlockSpec((D, NB), lambda t, l: (0, jnp.maximum(t - tiles, 0))), one((16, D))],
            scratch_shapes=[B(D, D), B(D, FF), B(D, FF), pltpu.VMEM((M, FF), F32), B(D, T), B(T, D), B(D, T), B(D, T), B(T, FF), B(T, FF), pltpu.SemaphoreType.DMA((3,))]),
        compiler_params=pltpu.CompilerParams(vmem_limit_bytes=60 << 20),
        name="ffn",
    )(lens, o, tokens, cot, wa, wf, vec8, b1)


class Spot:
    def __init__(self, na, ndp):
        self.na, self.ndp = na, ndp
        self.me = lax.axis_index("fsdp"); self.p = lax.axis_index("dp")
        self.a = self.me // 4; self.b = (self.me // 2) % 2; self.c = self.me % 2
        self.par = self.p % 2
        self.b2 = self.b + (1 - 2*self.b)*(1 - self.par); self.c2 = self.c + (1 - 2*self.c)*self.par
        self.b3 = self.b + (1 - 2*self.b)*self.par; self.c3 = self.c + (1 - 2*self.c)*(1 - self.par)

    def at(self, a, flip2=0, flip3=0):
        if flip2 and flip3:
            b, c = 1 - self.b, 1 - self.c
        elif flip2:
            b, c = self.b2, self.c2
        elif flip3:
            b, c = self.b3, self.c3
        else:
            b, c = self.b, self.c
        return (a*2 + b)*2 + c

    def dev(self, a, flip2=0, flip3=0):
        return (self.at(a, flip2, flip3), self.p)

    def barrier(self):
        sem = pltpu.get_barrier_semaphore()
        up, down = self.a < self.na - 1, self.a > 0
        def sig(dev):
            pl.semaphore_signal(sem, inc=1, device_id=dev, device_id_type=MESH)
        @pl.when(up)
        def _(): sig(self.dev(self.a + 1))
        @pl.when(down)
        def _(): sig(self.dev(self.a - 1))
        sig(self.dev(self.a, 1, 0)); sig(self.dev(self.a, 0, 1))
        for q in range(1, self.ndp): sig((self.me, (self.p + q) % self.ndp))
        pl.semaphore_wait(sem, 1 + self.ndp + up.astype(jnp.int32) + down.astype(jnp.int32))

class Gather:
    def __init__(self, spot, own, view, ssem, rsem, dp_view=None):
        self.s, self.own, self.view, self.ss, self.rs, self.dp_view = spot, own, view, ssem, rsem, dp_view
        na = spot.na
        self.JU, self.JD = 0, na - 1
        self.J2 = 2*(na - 1); self.J3 = self.J2 + na; self.JP = self.J3 + 2*na
        self.log = []

    @staticmethod
    def slots(na, ndp):
        return 2*(na - 1) + na + 2*na + (ndp - 1)*4*na

    def copy(self, f, dev, j, r=None, src=None):
        v = self.view(f)
        return pltpu.make_async_remote_copy(src_ref=v if src is None else src, dst_ref=v, send_sem=self.ss.at[j],
                                            recv_sem=self.rs.at[j if r is None else r], device_id=dev, device_id_type=MESH)

    def send(self, cond, make):
        make().start()
        self.log.append((cond, make))

    def wait(self, f, j):
        self.copy(f, (self.s.me, self.s.p), j).wait_recv()

    def dp(self, cond, f):
        if self.dp_view is None: return
        s = self.s
        for q in range(1, s.ndp):
            self.send(cond, lambda q=q: self.copy(f(), (s.me, (s.p + q) % s.ndp), self.JP + (q-1)*4*s.na + f()))

    def start(self):
        s = self.s; na = s.na
        up, down = s.a < na - 1, s.a > 0
        @pl.when(up)
        def _(): self.send(up, lambda: self.copy(s.me, s.dev(s.a + 1), self.JU, src=self.own))
        @pl.when(down)
        def _(): self.send(down, lambda: self.copy(s.me, s.dev(s.a - 1), self.JD, src=self.own))
        self.send(None, lambda: self.copy(s.me, s.dev(s.a, 1, 0), self.J2 + s.a, src=self.own))
        self.send(None, lambda: self.copy(s.me, s.dev(s.a, 0, 1), self.J3 + s.a*2, src=self.own))

    def events(self):
        s = self.s; na = s.na
        def chain(up, k):
            a = s.a - 1 - k if up else s.a + 1 + k
            cond = a >= 0 if up else a < na
            fwd = s.a < na - 1 if up else s.a > 0
            both = cond & fwd
            j = (self.JU if up else self.JD) + k
            def go():
                self.wait(s.at(a), j)
                if k < na - 2:
                    @pl.when(fwd)
                    def _(): self.send(both, lambda: self.copy(s.at(a), s.dev(s.a + 1 if up else s.a - 1), j + 1))
                self.send(cond, lambda: self.copy(s.at(a), s.dev(s.a, 1, 0), self.J2 + a))
                self.send(cond, lambda: self.copy(s.at(a), s.dev(s.a, 0, 1), self.J3 + a*2))
                self.dp(cond, lambda: s.at(a))
            return cond, go
        def second(a, cond):
            def go():
                self.wait(s.at(a, 1, 0), self.J2 + a)
                self.send(cond, lambda: self.copy(s.at(a, 1, 0), s.dev(s.a, 0, 1), self.J3 + a*2 + 1))
                self.dp(cond, lambda: s.at(a, 1, 0))
            return cond, go
        def third(a, cond, x):
            def go():
                self.wait(s.at(a, x, 1), self.J3 + a*2 + x)
                self.dp(cond, lambda: s.at(a, x, 1))
            return cond, go
        levels = [[(s.a, None)]]
        for k in range(na - 1):
            levels.append([(s.a - 1 - k, s.a - 1 - k >= 0), (s.a + 1 + k, s.a + 1 + k < na)])
        out = []
        for k in range(na + 2):
            if k < na - 1: out += [chain(True, k), chain(False, k)]
            if k < na:
                out += [second(a, cd) for a, cd in levels[k]]
                out += [third(a, cd, 0) for a, cd in levels[k]]
            if 0 < k <= na:
                out += [third(a, cd, 1) for a, cd in levels[k-1]]
        return out

    def finish(self):
        s = self.s
        if self.dp_view is not None:
            for q in range(1, s.ndp):
                def body(f, _):
                    @pl.when(f != s.me)
                    def _():
                        j = self.JP + (q-1)*4*s.na + f
                        v = self.dp_view(f, (s.p + s.ndp - q) % s.ndp)
                        pltpu.make_async_remote_copy(src_ref=v, dst_ref=v, send_sem=self.ss.at[j], recv_sem=self.rs.at[j], device_id=(s.me, s.p), device_id_type=MESH).wait_recv()
                    return 0
                lax.fori_loop(0, 4*s.na, body, 0)
        self.drain()

    def drain(self):
        for cond, make in self.log:
            if cond is None:
                make().wait_send()
            else:
                @pl.when(cond)
                def _(): make().wait_send()

def run_event(ev):
    cond, go = ev
    if cond is None: go()
    else: pl.when(cond)(go)

def forward_kernel(na, ndp, wa_sh, wf_sh, vecs, bff, lens_ref, tok_ref,
                   wa_out, wf_out, vec8, bias, q_ref, k_ref, v_ref, o_ref, lse_ref,
                   wa_c, wf_c, ex, wqkv, ot_s, tr_s, lsem, *sems):
    s = Spot(na, ndp)
    R = wa_sh.shape[0]
    tr_s[...] = jnp.zeros_like(tr_s)
    tr_s[0:R, 0:8] = vecs[...]
    ex[s.me, 0:8, :] = tr_s[...].T[0:8, :].astype(BF16).astype(F32)
    for j in range(4):
        ex[s.me, 8+j:9+j, 0:R] = bff[0:1, j*R:(j+1)*R].astype(BF16).astype(F32)
    wa_c[...] = wa_sh[...].astype(BF16)
    gs = []
    for i, (c, out) in enumerate(((wa_c, wa_out), (wf_c, wf_out))):
        w = c.shape[1] // ndp
        cols = lambda q, w=w: pl.ds(pl.multiple_of(q*w, 128), w)
        gs.append(Gather(s, c.at[:, cols(s.p)], lambda f, out=out, cols=cols: out.at[f, :, cols(s.p)], sems[2*i], sems[2*i+1],
                         lambda f, q, out=out, cols=cols: out.at[f, :, cols(q)]))
    gx = Gather(s, ex.at[s.me], lambda f: ex.at[f], sems[4], sems[5])
    ga, gf = gs
    s.barrier()
    gx.start(); ga.start()
    locs = [pltpu.make_async_copy(wa_c, wa_out.at[s.me], lsem.at[0])]
    locs[0].start()
    wf_c[...] = wf_sh[...].astype(BF16)
    locs.append(pltpu.make_async_copy(wf_c, wf_out.at[s.me], lsem.at[1]))
    locs[1].start()
    ea, exv, ef = ga.events(), gx.events(), gf.events()
    cut = 2 + 2*2
    started = False
    for n, (u, v) in enumerate(zip(ea, exv)):
        run_event(v); run_event(u)
        if n == len(ea)*2//5:
            gf.start(); started = True
    for q in range(1, ndp):
        def body(f, _, q=q):
            @pl.when(f != s.me)
            def _():
                j = ga.JP + (q-1)*4*na + f
                v = ga.dp_view(f, (s.p + ndp - q) % ndp)
                pltpu.make_async_remote_copy(src_ref=v, dst_ref=v, send_sem=ga.ss.at[j], recv_sem=ga.rs.at[j], device_id=(s.me, s.p), device_id_type=MESH).wait_recv()
            return 0
        lax.fori_loop(0, 4*na, body, 0)
    locs[0].wait()
    load = pltpu.make_async_copy(wa_out.at[:, :, 0:3*D], wqkv, lsem.at[2])
    load.start()
    for f in range(4*na):
        vec8[:, f*R:(f+1)*R] = ex[f, 0:8, 0:R]
        for j in range(4):
            bias[0:1, (f*4+j)*R:(f*4+j+1)*R] = ex[f, 8+j:9+j, 0:R]
    load.wait()
    S = tok_ref.shape[0] // LMAX
    lane = lax.broadcasted_iota(jnp.int32, (LMAX, 128), 1)
    row = lax.broadcasted_iota(jnp.int32, (LMAX, 128), 0)
    one = jnp.ones((LMAX, 128), BF16); zero = jnp.zeros((LMAX, 128), BF16)
    PAIRS = HEADS // 2
    ntask = S*(3 + PAIRS)
    per = -(-len(ef) // ntask)
    def events_after(i, first, last):
        for t in range(first, last):
            evs = ef[t*per:(t+1)*per]
            if evs:
                @pl.when(i == t)
                def _():
                    for e in evs: run_event(e)
    w3 = wqkv.shape
    def proj(sl, which):
        rs = pl.ds(pl.multiple_of(sl*LMAX, LMAX), LMAX)
        x = tok_ref[rs, :]
        y = mm(x, wqkv[:, :, which*D:(which+1)*D].reshape(4*na*R, D))
        if which == 0: q_ref[rs, :] = ((y + vec8[0:1, :]).astype(BF16) * 0.125).astype(BF16)
        elif which == 1: k_ref[rs, :] = y.astype(BF16)
        else: v_ref[rs, :] = (y + vec8[1:2, :]).astype(BF16)
    def step1(i, _):
        for which in range(3):
            @pl.when(i % 3 == which)
            def _(): proj(i // 3, which)
        events_after(i, 0, 3*S)
        return 0
    lax.fori_loop(0, 3*S, step1, 0)
    def step2(i, _):
        sl = i // PAIRS; j = i % PAIRS
        rs = pl.ds(pl.multiple_of(sl*LMAX, LMAX), LMAX)
        ls = pl.ds(pl.multiple_of(j * 128, 128), 128)
        bar = jnp.where(row < lens_ref[sl], 0.0, -1e30).astype(BF16)
        q2 = q_ref[rs, ls]; k2 = k_ref[rs, ls]
        vt = v_ref[rs, ls].T
        for e in range(2):
            other = 64 * (1 - e)
            ka = jnp.where((lane >= 64) == (e == 1), k2, jnp.where(lane == other, bar, zero))
            qa = jnp.where(lane == other, one, q2)
            for c in range(LMAX // QC):
                sc = mm(ka, qa[c*QC:(c+1)*QC], NT)
                top = jnp.max(sc, axis=0, keepdims=True)
                p = jnp.exp(sc - top)
                tot = jnp.sum(p, axis=0, keepdims=True)
                o = mm(vt[64*e:64*e+64], p.astype(BF16))
                ot_s[64*e:64*e+64, c*QC:(c+1)*QC] = o / tot
                lse_ref[pl.ds(sl*16 + 2*j + e, 1), c*QC:(c+1)*QC] = top + jnp.log(tot)
        o_ref[rs, ls] = ot_s[...].T.astype(BF16)
        events_after(i + 3*S, 3*S, ntask)
        return 0
    lax.fori_loop(0, S*PAIRS, step2, 0)
    gf.finish(); gx.finish()
    ga.drain()
    locs[1].wait()

def forward(mesh_shape, wa_sh, wf_sh, vecs, bff, lens, tokens, cid):
    F, ndp = mesh_shape
    na = F // 4; R = vecs.shape[0]; T = tokens.shape[0]
    NS = Gather.slots(na, ndp)
    S = jax.ShapeDtypeStruct
    V = pl.BlockSpec(memory_space=pltpu.VMEM); A = pl.BlockSpec(memory_space=pl.ANY)
    DMA = pltpu.SemaphoreType.DMA
    return pl.pallas_call(
        functools.partial(forward_kernel, na, ndp),
        out_shape=[S((F, R, 4*D), BF16), S((F, R, 2*FF), BF16), S((8, D), F32), S((1, FF), F32)] + [S((T, D), BF16)]*4 + [S((T//LMAX*16, LMAX), F32)],
        in_specs=[V, V, V, V, pl.BlockSpec(memory_space=pltpu.SMEM), V],
        out_specs=[A, A] + [V]*7,
        scratch_shapes=[pltpu.VMEM((R, 4*D), BF16), pltpu.VMEM((R, 2*FF), BF16), pltpu.VMEM((F, 16, 128), F32), pltpu.VMEM((F, R, 3*D), BF16),
                        pltpu.VMEM((128, LMAX), F32), pltpu.VMEM((128, 128), F32), DMA((3,))] + [DMA((NS,))]*6,
        compiler_params=pltpu.CompilerParams(collective_id=cid, has_side_effects=True, vmem_limit_bytes=56 << 20),
        name="gather_attend",
    )(wa_sh, wf_sh, vecs, bff, lens, tokens)


def as_int(cond):
    return cond.astype(jnp.int32)

class Reduce:
    def __init__(self, spot, src, mine, rd, r3, r2, cu, cd, ss, rs, out, load=None):
        self.s = spot
        self.src, self.mine = src, mine
        self.rd, self.r3, self.r2, self.cu, self.cd = rd, r3, r2, cu, cd
        self.ss, self.rs, self.out, self.load = ss, rs, out, load
        s = spot; na = s.na; F = 4*na
        self.B3 = (s.ndp - 1)*F; self.B2 = self.B3 + 2*na; self.BU = self.B2 + na; self.BD = self.BU + na; self.BO = self.BD + na
        self.log = []
        z = s.a; lower = as_int(z < na // 2)
        self.order = []
        for k in range(na):
            c1 = as_int(k < na - 1 - z); c2 = as_int(k < z)
            lo = c1*(na - 1 - k) + (1 - c1)*(k - (na - 1 - z))
            hi = c2*k + (1 - c2)*(na - 1 - (k - z))
            self.order.append(lower*lo + (1 - lower)*hi)
        self.bit2 = s.b*(1 - s.par) + s.c*s.par

    @staticmethod
    def slots(na, ndp):
        return (ndp - 1)*4*na + 5*na + ndp - 1

    def rc(self, src, dst, j, r, dev):
        return pltpu.make_async_remote_copy(src_ref=src, dst_ref=dst, send_sem=self.ss.at[j], recv_sem=self.rs.at[r], device_id=dev, device_id_type=MESH)

    def send(self, cond, make):
        make().start()
        self.log.append((cond, make))

    def wait(self, dst, r):
        self.rc(dst, dst, r, r, (self.s.me, self.s.p)).wait_recv()

    def start(self):
        s = self.s; na = s.na
        if self.load is not None:
            for y3, y2 in ((1, 1), (1, 0), (0, 1), (0, 0)):
                for k in range(na): self.load(s.at(self.order[k], y2, y3)).start()
        for y3, y2 in ((1, 1), (1, 0), (0, 1), (0, 0)):
            for k in range(na):
                for q in range(1, s.ndp):
                    x2, x3 = (y2, y3) if q % 2 == 0 else (y3, y2)
                    f = s.at(self.order[k], x2, x3)
                    dq = (s.p + q) % s.ndp
                    self.send(None, lambda f=f, q=q, dq=dq: self.rc(self.src(f, dq), self.rd.at[q-1, f], (q-1)*4*na + f, (q-1)*4*na + f, (s.me, dq)))

    def add(self, f, srcs, dst=None):
        s = self.s
        for q in range(1, s.ndp):
            self.wait(self.rd.at[q-1, f], (q-1)*4*s.na + f)
        if self.load is not None: self.load(f).wait()
        own = self.mine(f)
        dst = own if dst is None else dst
        srcs = [self.rd.at[q-1, f] for q in range(1, s.ndp)] + srcs
        w = own.shape[-1]
        CH = next(c for c in (512, 384, 256, 128) if w % c == 0)
        def body(j, _):
            cs = pl.ds(pl.multiple_of(j*CH, 128), CH)
            v = own[:, cs].astype(F32)
            for r in srcs: v = v + r[:, cs].astype(F32)
            dst[:, cs] = v.astype(dst.dtype)
            return 0
        lax.fori_loop(0, w // CH, body, 0)

    def events(self):
        s = self.s; na = s.na
        out = []
        for x2 in (1, 0):
            for k in range(na):
                def go(x2=x2, k=k):
                    a = self.order[k]; f = lambda: s.at(a, x2, 1)
                    slot = lambda: a*2 + self.bit2 + (1 - 2*self.bit2)*x2
                    self.add(f(), [])
                    self.send(None, lambda: self.rc(self.mine(f()), self.r3.at[slot()], self.B3 + slot(), self.B3 + slot(), s.dev(s.a, 0, 1)))
                out.append((None, go))
        for k in range(na):
            def go(k=k):
                a = self.order[k]; f = lambda: s.at(a, 1, 0)
                slot = a*2 + 1 - self.bit2
                self.wait(self.r3.at[slot], self.B3 + slot)
                self.add(f(), [self.r3.at[slot]])
                self.send(None, lambda: self.rc(self.mine(f()), self.r2.at[a], self.B2 + a, self.B2 + a, s.dev(s.a, 1, 0)))
            out.append((None, go))
        for k in range(na - 1, 0, -1):
            for up in (True, False):
                a = s.a + k if up else s.a - k
                cond = a < na if up else a >= 0
                more = s.a > 0 if up else s.a < na - 1
                buf, B = (self.cu, self.BU) if up else (self.cd, self.BD)
                def go(a=a, cond=cond, more=more, buf=buf, B=B, up=up):
                    slot = a*2 + self.bit2
                    f = lambda: s.at(a)
                    self.wait(self.r3.at[slot], self.B3 + slot)
                    self.wait(self.r2.at[a], self.B2 + a)
                    base = [self.r3.at[slot], self.r2.at[a]]
                    @pl.when(more)
                    def _():
                        self.wait(buf.at[a], B + a)
                        self.add(f(), base + [buf.at[a]])
                    @pl.when(jnp.logical_not(more))
                    def _(): self.add(f(), base)
                    self.send(cond, lambda: self.rc(self.mine(f()), buf.at[a], B + a, B + a, s.dev(s.a + 1 if up else s.a - 1)))
                out.append((cond, go))
        def last():
            a = s.a; slot = a*2 + self.bit2
            self.wait(self.r3.at[slot], self.B3 + slot)
            self.wait(self.r2.at[a], self.B2 + a)
            base = [self.r3.at[slot], self.r2.at[a]]
            dst = self.out(s.p)
            @pl.when(a == 0)
            def _():
                self.wait(self.cd.at[a], self.BD + a)
                self.add(s.me, base + [self.cd.at[a]], dst)
            @pl.when(a == na - 1)
            def _():
                self.wait(self.cu.at[a], self.BU + a)
                self.add(s.me, base + [self.cu.at[a]], dst)
            @pl.when((a > 0) & (a < na - 1))
            def _():
                self.wait(self.cd.at[a], self.BD + a)
                self.wait(self.cu.at[a], self.BU + a)
                self.add(s.me, base + [self.cd.at[a], self.cu.at[a]], dst)
            for q in range(1, s.ndp):
                self.send(None, lambda q=q: self.rc(self.out(s.p), self.out(s.p), self.BO + q - 1, self.BO + q - 1, (s.me, (s.p + q) % s.ndp)))
        out.append((None, last))
        return out

    def finish(self):
        s = self.s
        for q in range(1, s.ndp):
            self.wait(self.out((s.p + s.ndp - q) % s.ndp), self.BO + q - 1)
        for cond, make in self.log:
            if cond is None: make().wait_send()
            else:
                @pl.when(cond)
                def _(): make().wait_send()

    @staticmethod
    def scratch(na, ndp, R, w):
        F = 4*na
        B = lambda *sh: pltpu.VMEM(sh + (R, w), BF16)
        NS = Reduce.slots(na, ndp)
        return [B(ndp - 1, F), B(2*na), B(na), B(na), B(na), pltpu.SemaphoreType.DMA((NS,)), pltpu.SemaphoreType.DMA((NS,))]

class SmallSum:
    def __init__(self, spot, buf, got, ss, rs):
        self.s, self.buf, self.got, self.ss, self.rs = spot, buf, got, ss, rs
        self.sent = []

    @staticmethod
    def scratch(na, ndp, shape):
        NX = ndp + 1 + na - 1
        return [pltpu.VMEM((4,) + shape, F32), pltpu.VMEM((NX,) + shape, F32), pltpu.SemaphoreType.DMA((NX,)), pltpu.SemaphoreType.DMA((NX,))]

    def go(self, i, j, dev):
        d = pltpu.make_async_remote_copy(src_ref=self.buf.at[i], dst_ref=self.got.at[j], send_sem=self.ss.at[j], recv_sem=self.rs.at[j], device_id=dev, device_id_type=MESH)
        d.start(); self.sent.append(d)

    def wait(self, j):
        pltpu.make_async_remote_copy(src_ref=self.got.at[j], dst_ref=self.got.at[j], send_sem=self.ss.at[j], recv_sem=self.rs.at[j], device_id=(self.s.me, self.s.p), device_id_type=MESH).wait_recv()

    def ordered(self, i, here, n, j0):
        def pick(m):
            v = self.buf[i]
            for q in range(1, n):
                v = jnp.where((here + n - q) % n == m, self.got[j0 + q - 1], v)
            return v
        v = pick(0)
        for m in range(1, n): v = v + pick(m)
        return v

    def start(self):
        s = self.s
        for q in range(1, s.ndp): self.go(0, q - 1, (s.me, (s.p + q) % s.ndp))

    def steps(self, out):
        s = self.s; X = s.ndp - 1
        def one():
            for q in range(1, s.ndp): self.wait(q - 1)
            self.buf[1] = self.ordered(0, s.p, s.ndp, 0)
            self.go(1, X, ((s.a*2 + s.b)*2 + 1 - s.c, s.p))
        def two():
            self.wait(X)
            self.buf[2] = self.buf[1] + self.got[X]
            self.go(2, X + 1, ((s.a*2 + 1 - s.b)*2 + s.c, s.p))
        def three():
            self.wait(X + 1)
            self.buf[3] = self.buf[2] + self.got[X + 1]
            for k in range(1, s.na): self.go(3, X + 1 + k, s.dev((s.a + k) % s.na))
        def four():
            for k in range(1, s.na): self.wait(X + 1 + k)
            out[...] = self.ordered(3, s.a, s.na, X + 2)
        return [one, two, three, four]

    def finish(self):
        for d in self.sent: d.wait_send()

def barrier_full(s):
    sem = pltpu.get_barrier_semaphore()
    def sig(dev): pl.semaphore_signal(sem, inc=1, device_id=dev, device_id_type=MESH)
    for k in range(1, s.na): sig(s.dev((s.a + k) % s.na))
    sig(s.dev(s.a, 1, 0)); sig(s.dev(s.a, 0, 1))
    for q in range(1, s.ndp): sig((s.me, (s.p + q) % s.ndp))
    pl.semaphore_wait(sem, s.na + s.ndp)

def backward_kernel(na, ndp, lens_ref, q_h, k_h, v_h, do_h, lse_ref, tok_h, dz_h, wa_h, gf_h, small_in,
                    dx_ref, of_ref, oq_ref, small_out,
                    q_ref, k_ref, v_ref, do_ref, tok_ref, wqkv, g_s, xt_s, dqt_s, acck, accv, wg, ownf, lsem, fsem, *sc):
    s = Spot(na, ndp)
    R = gf_h.shape[1]; T = tok_ref.shape[0]; S = T // LMAX
    PAIRS = HEADS // 2
    loads = []
    for i, (h, r) in enumerate(((q_h, q_ref), (k_h, k_ref), (v_h, v_ref), (do_h, do_ref))):
        loads.append(pltpu.make_async_copy(h, r, lsem.at[i]))
    late = [pltpu.make_async_copy(tok_h, tok_ref, lsem.at[4]), pltpu.make_async_copy(wa_h.at[:, :, 0:3*D], wqkv, lsem.at[5]), pltpu.make_async_copy(dz_h, dx_ref, lsem.at[6])]
    wf = gf_h.shape[2] // ndp; wq = wg.shape[2] // ndp
    def cols(q, w): return pl.ds(pl.multiple_of(q*w, 128), w)
    cf = lambda f: pltpu.make_async_copy(gf_h.at[f, :, cols(s.p, wf)], ownf.at[f], fsem.at[f])
    rf = Reduce(s, lambda f, q: gf_h.at[f, :, cols(q, wf)], lambda f: ownf.at[f], *sc[0:7], lambda q: of_ref.at[:, cols(q, wf)], cf)
    rq = Reduce(s, lambda f, q: wg.at[f, :, cols(q, wq)], lambda f: wg.at[f, :, cols(s.p, wq)], *sc[7:14], lambda q: oq_ref.at[:, cols(q, wq)])
    xs = SmallSum(s, *sc[14:18])
    barrier_full(s)
    rf.start()
    for l in loads + late: l.start()
    both = rf.events()
    ntask = S*PAIRS
    n3, n2 = 2*na, na
    plan = [[] for _ in range(ntask)]
    quick, half = max(1, ntask // 4), ntask // 2
    for i, e in enumerate(both[:n3 + n2]):
        t = i*quick // n3 if i < n3 else half + (i - n3)*(ntask - half) // n2
        plan[t].append(e)
    chain_f, last_f = both[n3 + n2:-1], both[-1]

    lane = lax.broadcasted_iota(jnp.int32, (LMAX, 128), 1)
    row = lax.broadcasted_iota(jnp.int32, (LMAX, 128), 0)
    one = jnp.ones((LMAX, 128), BF16); zero = jnp.zeros((LMAX, 128), BF16)
    for l in loads: l.wait()
    def task(t, _):
        sl = t // PAIRS; j = t % PAIRS
        rs = pl.ds(pl.multiple_of(sl * LMAX, LMAX), LMAX)
        ls = pl.ds(pl.multiple_of(j * 128, 128), 128)
        bar = jnp.where(row < lens_ref[sl], 0.0, -1e30).astype(BF16)
        q2 = q_ref[rs, ls]; k2 = k_ref[rs, ls]; v2 = v_ref[rs, ls]; do2 = do_ref[rs, ls]
        kt = k2.T
        for e in range(2):
            other = 64 * (1 - e)
            mine = (lane >= 64) == (e == 1)
            ka = jnp.where(mine, k2, jnp.where(lane == other, bar, zero))
            va = jnp.where(mine, v2, zero)
            qa = jnp.where(lane == other, one, q2)
            lse_row = lse_ref[pl.ds(sl * 16 + 2*j + e, 1), :]
            for c in range(LMAX // QC):
                cs = slice(c*QC, (c+1)*QC)
                sc_ = mm(ka, qa[cs], NT)
                p = jnp.exp(sc_ - lse_row[:, cs])
                dp = mm(va, do2[cs], NT)
                pd = p * dp
                dsum = jnp.sum(pd, axis=0, keepdims=True)
                ds = (pd - p * dsum).astype(BF16)
                dvc = mm(p.astype(BF16), do2[cs])
                dkc = mm(ds, q2[cs])
                if c == 0: dva, dka = dvc, dkc
                else: dva, dka = dva + dvc, dka + dkc
                dqt_s[64*e:64*e+64, cs] = mm(kt[64*e:64*e+64], ds)
            if e == 0:
                accv[...] = dva; acck[...] = dka
            else:
                g_s[rs, pl.ds(pl.multiple_of(2*D + j*128, 128), 128)] = jnp.where(mine, dva, accv[...]).astype(BF16)
                g_s[rs, pl.ds(pl.multiple_of(D + j*128, 128), 128)] = jnp.where(mine, dka, acck[...]).astype(BF16)
        g_s[rs, ls] = (dqt_s[...].T * 0.125).astype(BF16)
        for n in range(ntask):
            if plan[n]:
                @pl.when(t == n)
                def _():
                    for e in plan[n]: run_event(e)
        return 0
    lax.fori_loop(0, ntask, task, 0)
    late[0].wait()
    xt_s[...] = tok_ref[...].T
    if wg.shape[2] > 3*D: wg[:, :, 3*D:] = jnp.zeros(wg.shape[:2] + (wg.shape[2] - 3*D,), BF16)
    def wgr(r, _):
        cs = pl.ds(pl.multiple_of(r * 256, 256), 256)
        wg[:, :, cs] = mm(xt_s[...], g_s[:, cs]).reshape(4*na, R, 256).astype(BF16)
        return 0
    lax.fori_loop(0, 3*D // 256, wgr, 0)
    rq.start()
    xs.buf[0] = small_in[...]
    xs.buf[0, 0:1, :] = jnp.sum(g_s[:, 0:D].astype(F32), axis=0, keepdims=True)
    xs.buf[0, 1:2, :] = jnp.sum(g_s[:, 2*D:3*D].astype(F32), axis=0, keepdims=True)
    xs.start()
    eq = rq.events(); small = xs.steps(small_out)
    for e in eq[:n3]: run_event(e)
    late[1].wait(); late[2].wait()
    def rows(r):
        rr = slice(r*256, (r+1)*256)
        dx_ref[rr, :] += mm(g_s[rr, :], wqkv[...].reshape(D, 3*D), NT)
    steps = [lambda r=r: rows(r) for r in range(T // 256)]
    rest = list(chain_f) + eq[n3:n3 + n2]
    gap = -(-len(rest) // len(steps))
    for i, step in enumerate(steps):
        for e in rest[i*gap:(i+1)*gap]: run_event(e)
        if i < 4: small[i]()
        step()
    for e in rest[len(steps)*gap:]: run_event(e)
    for f in small[len(steps):]: f()
    run_event(last_f)
    for e in eq[n3 + n2:]: run_event(e)
    rf.finish(); rq.finish(); xs.finish()

def backward(mesh_shape, lens, q, k, v, do, lse, tokens, dz, wa3, gf, small, cid):
    F, ndp = mesh_shape
    na = F // 4; R = gf.shape[1]; T = tokens.shape[0]
    S = jax.ShapeDtypeStruct
    V = pl.BlockSpec(memory_space=pltpu.VMEM); A = pl.BlockSpec(memory_space=pl.ANY)
    up = lambda n: -(-n // (128*ndp)) * 128*ndp
    CQ = up(3*D)
    B = lambda *sh: pltpu.VMEM(sh, BF16)
    return pl.pallas_call(
        functools.partial(backward_kernel, na, ndp),
        out_shape=[S((T, D), F32), S((R, gf.shape[2]), F32), S((R, CQ), F32), S(small.shape, F32)],
        in_specs=[pl.BlockSpec(memory_space=pltpu.SMEM), A, A, A, A, V, A, A, A, A, V],
        out_specs=[V]*4,
        scratch_shapes=[B(T, D)]*5 + [B(F, R, 3*D)] + [B(T, 3*D), B(D, T), pltpu.VMEM((128, LMAX), F32), pltpu.VMEM((LMAX, 128), F32), pltpu.VMEM((LMAX, 128), F32),
                        B(F, R, CQ), B(F, R, gf.shape[2]//ndp), pltpu.SemaphoreType.DMA((7,)), pltpu.SemaphoreType.DMA((F,))]
                       + Reduce.scratch(na, ndp, R, gf.shape[2]//ndp) + Reduce.scratch(na, ndp, R, CQ//ndp)
                       + SmallSum.scratch(na, ndp, small.shape),
        compiler_params=pltpu.CompilerParams(collective_id=cid, has_side_effects=True, vmem_limit_bytes=60 << 20),
        name="reduce_attend",
    )(lens, q, k, v, do, lse, tokens, dz, wa3, gf, small)


def adam_update(gradient, moment, second, master, adam_step, learn_rate):
    count = adam_step[0].astype(jnp.float32)
    moment_new = 0.9 * moment + 0.1 * gradient
    second_new = 0.98 * second + 0.02 * gradient * gradient
    first_fix = moment_new / (1.0 - jnp.power(0.9, count))
    second_fix = second_new / (1.0 - jnp.power(0.98, count))
    master_new = master - learn_rate[0] * (
        first_fix / (jnp.sqrt(second_fix) + 1e-06) + 0.01 * master
    )
    return (moment_new, second_new, master_new, master_new.astype(jnp.bfloat16))


def local(mesh_shape, tokens, cotangent, lengths, adam_step, learn_rate, attn_w, attn_m, attn_v, ffn_w, ffn_m, ffn_v,
          vecs, vecs_m, vecs_v, b_ff, bff_m, bff_v):
    shards, rows = mesh_shape[0], vecs.shape[0]
    T = tokens.shape[0]
    attn_low, ffn_low, vec8, bias, q, k, v, o, lse = forward(
        mesh_shape, attn_w, ffn_w, vecs, b_ff.reshape(1, 4 * rows), lengths, tokens, 1)
    attn_low = attn_low.reshape(D, 4 * D)
    ffn_low = ffn_low.reshape(D, 2 * FF)
    outputs, dz1, do, grads, small_ffn = ffn(o, tokens, cotangent, attn_low, ffn_low, vec8, bias, lengths)
    grads = jnp.pad(grads, ((0, 0), (0, -grads.shape[1] % (128 * mesh_shape[1]))))
    input_grad, summed, summed_qkv, summed_small = backward(
        mesh_shape, lengths, q, k, v, do, lse, tokens, dz1, attn_low.reshape(shards, rows, 4 * D),
        grads.reshape(shards, rows, grads.shape[1]), small_ffn, 2)
    summed_ffn = summed[:, : 2 * FF]
    summed_attn = jnp.concatenate([summed_qkv[:, : 3 * D], summed[:, 2 * FF : 2 * FF + D]], axis=1)
    mine = lax.axis_index("fsdp")
    summed_vecs = lax.dynamic_slice(summed_small, (0, mine * rows), (8, rows)).T
    summed_bias = lax.dynamic_slice(summed_small[8:12].reshape(FF), (mine * 4 * rows,), (4 * rows,))
    attn_new = adam_update(summed_attn, attn_m, attn_v, attn_w, adam_step, learn_rate)
    ffn_new = adam_update(summed_ffn, ffn_m, ffn_v, ffn_w, adam_step, learn_rate)
    vecs_new = adam_update(summed_vecs, vecs_m, vecs_v, vecs, adam_step, learn_rate)
    bff_new = adam_update(summed_bias, bff_m, bff_v, b_ff, adam_step, learn_rate)
    return (outputs, input_grad, summed_attn, *attn_new, summed_ffn, *ffn_new, summed_vecs, *vecs_new, summed_bias, *bff_new)


def solution(mesh):
    both, rows, whole = P(("fsdp", "dp")), P("fsdp"), P()
    return jax.shard_map(
        functools.partial(local, (mesh.shape["fsdp"], mesh.shape["dp"])),
        mesh=mesh,
        in_specs=(both, both, both, whole, whole) + (rows,) * 12,
        out_specs=(both, both) + (rows,) * 20,
        check_vma=False,
    )
```

```python
import functools

import jax
import jax.numpy as jnp
from jax import lax
from jax.experimental import pallas as pl
from jax.experimental.pallas import tpu as pltpu
from jax.sharding import PartitionSpec as P

MESH = pl.DeviceIdType.MESH

D = 768; HEADS = 12; HEAD = 64; FF = 3072; LMAX = 512
NN = (((1,), (0,)), ((), ()))
NT = (((1,), (1,)), ((), ()))
TN = (((0,), (0,)), ((), ()))
F32 = jnp.float32; BF16 = jnp.bfloat16
QC = 256

def mm(a, b, dims=NN):
    return lax.dot_general(a, b, dims, preferred_element_type=F32)

def attend_fwd_kernel(lens_ref, tok_ref, wq_ref, wk_ref, wv_ref, vec_ref, q_ref, k_ref, v_ref, o_ref, lse_ref, ot_ref):
    n = lens_ref[pl.program_id(0)]
    x = tok_ref[...]
    q_ref[...] = ((mm(x, wq_ref[...]) + vec_ref[0:1, :]).astype(BF16) * 0.125).astype(BF16)
    k_ref[...] = mm(x, wk_ref[...]).astype(BF16)
    v_ref[...] = (mm(x, wv_ref[...]) + vec_ref[1:2, :]).astype(BF16)
    lane = lax.broadcasted_iota(jnp.int32, (LMAX, 128), 1)
    row = lax.broadcasted_iota(jnp.int32, (LMAX, 128), 0)
    bar = jnp.where(row < n, 0.0, -1e30).astype(BF16)
    one = jnp.ones((LMAX, 128), BF16); zero = jnp.zeros((LMAX, 128), BF16)

    def pair(j, _):
        ls = pl.ds(pl.multiple_of(j * 128, 128), 128)
        q2 = q_ref[:, ls]; k2 = k_ref[:, ls]
        vt = v_ref[:, ls].T
        for e in range(2):
            other = 64 * (1 - e)
            ka = jnp.where((lane >= 64) == (e == 1), k2, jnp.where(lane == other, bar, zero))
            qa = jnp.where(lane == other, one, q2)
            for c in range(LMAX // QC):
                s = mm(ka, qa[c*QC:(c+1)*QC], NT)
                top = jnp.max(s, axis=0, keepdims=True)
                p = jnp.exp(s - top)
                tot = jnp.sum(p, axis=0, keepdims=True)
                o = mm(vt[64*e:64*e+64], p.astype(BF16))
                ot_ref[64*e:64*e+64, c*QC:(c+1)*QC] = o / tot
                lse_ref[pl.ds(2*j + e, 1), c*QC:(c+1)*QC] = top + jnp.log(tot)
        o_ref[:, ls] = ot_ref[...].T.astype(BF16)
        return 0
    lax.fori_loop(0, HEADS // 2, pair, 0)

def attend_fwd(tokens, wa, vec8, lens):
    S = tokens.shape[0] // LMAX
    row = pl.BlockSpec((LMAX, D), lambda s, l: (s, 0))
    w = lambda i: pl.BlockSpec((D, D), lambda s, l, i=i: (0, i))
    return pl.pallas_call(
        attend_fwd_kernel,
        out_shape=[jax.ShapeDtypeStruct((S*LMAX, D), BF16)]*4 + [jax.ShapeDtypeStruct((S*16, LMAX), F32)],
        grid_spec=pltpu.PrefetchScalarGridSpec(num_scalar_prefetch=1, grid=(S,),
            in_specs=[row, w(0), w(1), w(2), pl.BlockSpec((8, D), lambda s, l: (0, 0))],
            out_specs=[row]*4 + [pl.BlockSpec((16, LMAX), lambda s, l: (s, 0))],
            scratch_shapes=[pltpu.VMEM((128, LMAX), F32)]),
        name="attend_fwd",
    )(lens, tokens, wa, wa, wa, vec8)

def attend_bwd_kernel(lens_ref, q_ref, k_ref, v_ref, do_ref, lse_ref, tok_ref, dz_ref, wq_ref, wk_ref, wv_ref, dx_ref, dw_ref, small_ref,
                      dq_s, dk_s, dv_s, xt_s, dqt_s, acck, accv, lse_s):
    S = tok_ref.shape[0] // LMAX
    lane = lax.broadcasted_iota(jnp.int32, (LMAX, 128), 1)
    row = lax.broadcasted_iota(jnp.int32, (LMAX, 128), 0)
    one = jnp.ones((LMAX, 128), BF16); zero = jnp.zeros((LMAX, 128), BF16)
    xt_s[...] = tok_ref[...].T

    def task(t, _):
        sl = t // (HEADS // 2); j = t % (HEADS // 2)
        rs = pl.ds(pl.multiple_of(sl * LMAX, LMAX), LMAX)
        ls = pl.ds(pl.multiple_of(j * 128, 128), 128)
        bar = jnp.where(row < lens_ref[sl], 0.0, -1e30).astype(BF16)
        q2 = q_ref[rs, ls]; k2 = k_ref[rs, ls]; v2 = v_ref[rs, ls]; do2 = do_ref[rs, ls]
        kt = k2.T
        for e in range(2):
            other = 64 * (1 - e)
            mine = (lane >= 64) == (e == 1)
            ka = jnp.where(mine, k2, jnp.where(lane == other, bar, zero))
            va = jnp.where(mine, v2, zero)
            qa = jnp.where(lane == other, one, q2)
            lse_row = lse_ref[pl.ds(sl * 16 + 2*j + e, 1), :]
            for c in range(LMAX // QC):
                cs = slice(c*QC, (c+1)*QC)
                s = mm(ka, qa[cs], NT)
                p = jnp.exp(s - lse_row[:, cs])
                dp = mm(va, do2[cs], NT)
                pd = p * dp
                dsum = jnp.sum(pd, axis=0, keepdims=True)
                ds = (pd - p * dsum).astype(BF16)
                dvc = mm(p.astype(BF16), do2[cs])
                dkc = mm(ds, q2[cs])
                if c == 0:
                    dva, dka = dvc, dkc
                else:
                    dva, dka = dva + dvc, dka + dkc
                dqt_s[64*e:64*e+64, cs] = mm(kt[64*e:64*e+64], ds)
            if e == 0:
                accv[...] = dva; acck[...] = dka
            else:
                dv_s[rs, ls] = jnp.where(mine, dva, accv[...]).astype(BF16)
                dk_s[rs, ls] = jnp.where(mine, dka, acck[...]).astype(BF16)
        dq_s[rs, ls] = (dqt_s[...].T * 0.125).astype(BF16)
        return 0
    lax.fori_loop(0, S * (HEADS // 2), task, 0)
    small_ref[...] = jnp.zeros_like(small_ref)
    small_ref[0:1, :] = jnp.sum(dq_s[...].astype(F32), axis=0, keepdims=True)
    small_ref[1:2, :] = jnp.sum(dv_s[...].astype(F32), axis=0, keepdims=True)
    def rows(r, _):
        rr = pl.ds(pl.multiple_of(r * 256, 256), 256)
        dx_ref[rr, :] = dz_ref[rr, :] + mm(dq_s[rr, :], wq_ref[...], NT) + mm(dk_s[rr, :], wk_ref[...], NT) + mm(dv_s[rr, :], wv_ref[...], NT)
        return 0
    lax.fori_loop(0, S * LMAX // 256, rows, 0)
    for i, g in enumerate((dq_s, dk_s, dv_s)):
        def wg(r, _, g=g, i=i):
            rr = pl.ds(pl.multiple_of(r * 256, 256), 256)
            dw_ref[rr, i*D:(i+1)*D] = mm(xt_s[rr, :], g[...]).astype(BF16)
            return 0
        lax.fori_loop(0, D // 256, wg, 0)

def attend_bwd(q, k, v, do, lse, tokens, dz, wa, lens):
    T = tokens.shape[0]
    V = pl.BlockSpec(memory_space=pltpu.VMEM)
    w = lambda i: pl.BlockSpec((D, D), lambda s, l, i=i: (0, i))
    full = lambda a: pl.BlockSpec(a.shape, lambda s, l: (0, 0))
    o = lambda sh: pl.BlockSpec(sh, lambda s, l: (0, 0))
    return pl.pallas_call(
        attend_bwd_kernel,
        out_shape=[jax.ShapeDtypeStruct((T, D), F32), jax.ShapeDtypeStruct((D, 3*D), BF16), jax.ShapeDtypeStruct((8, D), F32)],
        grid_spec=pltpu.PrefetchScalarGridSpec(num_scalar_prefetch=1, grid=(1,),
            in_specs=[full(q)]*4 + [full(lse), full(tokens), full(dz), w(0), w(1), w(2)],
            out_specs=[o((T, D)), o((D, 3*D)), o((8, D))],
            scratch_shapes=[pltpu.VMEM((T, D), BF16)]*3 + [pltpu.VMEM((D, T), BF16), pltpu.VMEM((128, LMAX), F32), pltpu.VMEM((LMAX, 128), F32), pltpu.VMEM((LMAX, 128), F32), pltpu.VMEM((8, 128), F32)]),
        name="attend_bwd",
    )(lens, q, k, v, do, lse, tokens, dz, wa, wa, wa)


M = 256
NB = 768


def gelu_pair(u):
    phi = 0.5 * (1.0 + lax.erf(u * 0.7071067811865476))
    e = jnp.exp(-0.5 * (u * u))
    return u * phi, phi + u * (e * 0.3989422804014327)

def norm_stats(z):
    mean = jnp.mean(z, axis=-1, keepdims=True)
    c = z - mean
    var = jnp.mean(c * c, axis=-1, keepdims=True)
    r = lax.rsqrt(var + 1e-5)
    return c * r, r

def norm_back(dxh, xh, r):
    return r * (dxh - jnp.mean(dxh, axis=-1, keepdims=True) - xh * jnp.mean(dxh * xh, axis=-1, keepdims=True))

def colsum(x):
    return jnp.sum(x, axis=0, keepdims=True)

def ffn_kernel(tiles, lens_ref, o_ref, tok_ref, cot_ref, wa_h, wf_h, vec_ref, b1_ref,
               out_ref, dz_ref, do_ref, gf_ref, small_ref,
               wo_ref, w1_ref, w2_ref, gp_s, ot_s, da_s, ht_s, dft_s, g_s, du_s, sem):
    t = pl.program_id(0); per = LMAX // M
    live = [(lens_ref[u // per] > (u % per) * M).astype(jnp.int32) for u in range(tiles)]
    count = sum(live)
    loads = [pltpu.make_async_copy(wa_h.at[:, 3*D:4*D], wo_ref, sem.at[0]), pltpu.make_async_copy(wf_h.at[:, 0:FF], w1_ref, sem.at[1]), pltpu.make_async_copy(wf_h.at[:, FF:2*FF], w2_ref, sem.at[2])]
    def arrived(i):
        @pl.when(t == 0)
        def _(): loads[i].wait()

    @pl.when(t == 0)
    def _():
        for l in loads: l.start()
        small_ref[...] = jnp.zeros_like(small_ref)

    n = lens_ref[jnp.minimum(t, tiles - 1) // per] - (t % per) * M

    @pl.when((t < tiles) & (n <= 0))
    def _():
        for r in (out_ref, dz_ref, do_ref):
            r[...] = jnp.zeros_like(r)

    @pl.when((t < tiles) & (n > 0))
    def _():
        pos = sum(live[u] * (u < t).astype(jnp.int32) for u in range(tiles))
        rs = pl.ds(pl.multiple_of(pos * M, M), M)
        v = lambda i: vec_ref[i:i+1, :]
        o = o_ref[...]
        arrived(0)
        z1 = tok_ref[...].astype(F32) + (mm(o, wo_ref[...]) + v(2))
        ot_s[:, rs] = o.T
        xh1, r1 = norm_stats(z1)
        h = xh1 * v(3) + v(4)
        hb = h.astype(BF16)
        ht_s[:, rs] = hb.T
        arrived(1)
        arrived(2)
        f = None
        CF = 512
        cuts = [slice(c, c + CF) for c in range(0, FF, CF)]
        u = mm(hb, w1_ref[:, cuts[0]]) + b1_ref[:, cuts[0]]
        for j, cs in enumerate(cuts):
            nxt = mm(hb, w1_ref[:, cuts[j+1]]) + b1_ref[:, cuts[j+1]] if j + 1 < len(cuts) else None
            g, gp = gelu_pair(u)
            gb = g.astype(BF16)
            g_s[rs, cs] = gb
            gp_s[:, cs] = gp
            part = mm(gb, w2_ref[:, cs], NT)
            f = part if f is None else f + part
            u = nxt
        z2 = h + (f + v(5))
        xh2, r2 = norm_stats(z2)
        keep = lax.broadcasted_iota(jnp.int32, (M, 1), 0) < n
        out_ref[...] = jnp.where(keep, xh2 * v(6) + v(7), 0.0).astype(BF16)
        dy = jnp.where(keep, cot_ref[...].astype(F32), 0.0)
        small_ref[7:8, :] += colsum(dy)
        small_ref[6:7, :] += colsum(dy * xh2)
        dz2 = norm_back(dy * v(6), xh2, r2)
        df = dz2.astype(BF16)
        dft_s[:, rs] = df.T
        small_ref[5:6, :] += colsum(df.astype(F32))
        du = (gp_s[...] * mm(df, w2_ref[...])).astype(BF16)
        du_s[rs, :] = du
        db1 = colsum(du.astype(F32))
        for i in range(4):
            small_ref[8+i:9+i, :] += db1[:, i*D:(i+1)*D]
        dh = dz2 + mm(du, w1_ref[...], NT)
        small_ref[4:5, :] += colsum(dh)
        small_ref[3:4, :] += colsum(dh * xh1)
        dz1 = norm_back(dh * v(3), xh1, r1)
        da = dz1.astype(BF16)
        small_ref[2:3, :] += colsum(da.astype(F32))
        dz_ref[...] = dz1
        da_s[rs, :] = da
        do_ref[...] = mm(da, wo_ref[...], NT).astype(BF16)

    i = t - tiles
    half = FF // NB
    for kk in range(1, tiles + 1):
        K = kk*M
        for lt, r, c0, n0, n1 in ((ht_s, du_s, 0, 0, half), (dft_s, g_s, half, half, 2*half), (ot_s, da_s, 2*half, 2*half, 2*half + 1)):
            @pl.when((count == kk) & (i >= n0) & (i < n1))
            def _(lt=lt, r=r, K=K, c0=c0):
                cs = pl.ds(pl.multiple_of((i - c0) * NB, NB), NB)
                gf_ref[...] = mm(lt[:, :K], r[:K, cs]).astype(BF16)

def ffn(o, tokens, cot, wa, wf, vec8, b1, lens):
    T = tokens.shape[0]; tiles = T // M; chunks = 2*FF // NB + 1
    row = pl.BlockSpec((M, D), lambda t, l: (jnp.minimum(t, tiles - 1), 0))
    one = lambda sh: pl.BlockSpec(sh, lambda t, l: (0, 0))
    A = pl.BlockSpec(memory_space=pl.ANY)
    S = jax.ShapeDtypeStruct
    B = lambda *sh: pltpu.VMEM(sh, BF16)
    return pl.pallas_call(
        functools.partial(ffn_kernel, tiles),
        out_shape=[S((T, D), BF16), S((T, D), F32), S((T, D), BF16), S((D, chunks*NB), BF16), S((16, D), F32)],
        grid_spec=pltpu.PrefetchScalarGridSpec(num_scalar_prefetch=1, grid=(tiles + chunks,),
            in_specs=[row, row, row, A, A, one((8, D)), one((1, FF))],
            out_specs=[row, row, row, pl.BlockSpec((D, NB), lambda t, l: (0, jnp.maximum(t - tiles, 0))), one((16, D))],
            scratch_shapes=[B(D, D), B(D, FF), B(D, FF), pltpu.VMEM((M, FF), F32), B(D, T), B(T, D), B(D, T), B(D, T), B(T, FF), B(T, FF), pltpu.SemaphoreType.DMA((3,))]),
        compiler_params=pltpu.CompilerParams(vmem_limit_bytes=60 << 20),
        name="ffn",
    )(lens, o, tokens, cot, wa, wf, vec8, b1)


RATE = 1.0

class Spot:
    def __init__(self, na, ndp):
        self.na, self.ndp = na, ndp
        self.me = lax.axis_index("fsdp"); self.p = lax.axis_index("dp")
        self.a = self.me // 4; self.b = (self.me // 2) % 2; self.c = self.me % 2
        self.par = self.p % 2
        self.b2 = self.b + (1 - 2*self.b)*(1 - self.par); self.c2 = self.c + (1 - 2*self.c)*self.par
        self.b3 = self.b + (1 - 2*self.b)*self.par; self.c3 = self.c + (1 - 2*self.c)*(1 - self.par)

    def at(self, a, flip2=0, flip3=0):
        if flip2 and flip3:
            b, c = 1 - self.b, 1 - self.c
        elif flip2:
            b, c = self.b2, self.c2
        elif flip3:
            b, c = self.b3, self.c3
        else:
            b, c = self.b, self.c
        return (a*2 + b)*2 + c

    def dev(self, a, flip2=0, flip3=0):
        return (self.at(a, flip2, flip3), self.p)

    def barrier(self):
        sem = pltpu.get_barrier_semaphore()
        up, down = self.a < self.na - 1, self.a > 0
        def sig(dev):
            pl.semaphore_signal(sem, inc=1, device_id=dev, device_id_type=MESH)
        @pl.when(up)
        def _(): sig(self.dev(self.a + 1))
        @pl.when(down)
        def _(): sig(self.dev(self.a - 1))
        sig(self.dev(self.a, 1, 0)); sig(self.dev(self.a, 0, 1))
        for q in range(1, self.ndp): sig((self.me, (self.p + q) % self.ndp))
        pl.semaphore_wait(sem, 1 + self.ndp + up.astype(jnp.int32) + down.astype(jnp.int32))

class Gather:
    def __init__(self, spot, own, view, ssem, rsem, dp_view=None):
        self.s, self.own, self.view, self.ss, self.rs, self.dp_view = spot, own, view, ssem, rsem, dp_view
        na = spot.na
        self.JU, self.JD = 0, na - 1
        self.J2 = 2*(na - 1); self.J3 = self.J2 + na; self.JP = self.J3 + 2*na
        self.log = []

    @staticmethod
    def slots(na, ndp):
        return 2*(na - 1) + na + 2*na + (ndp - 1)*4*na

    def copy(self, f, dev, j, r=None, src=None):
        v = self.view(f)
        return pltpu.make_async_remote_copy(src_ref=v if src is None else src, dst_ref=v, send_sem=self.ss.at[j],
                                            recv_sem=self.rs.at[j if r is None else r], device_id=dev, device_id_type=MESH)

    def send(self, cond, make):
        make().start()
        self.log.append((cond, make))

    def wait(self, f, j):
        self.copy(f, (self.s.me, self.s.p), j).wait_recv()

    def dp(self, cond, f):
        if self.dp_view is None: return
        s = self.s
        for q in range(1, s.ndp):
            self.send(cond, lambda q=q: self.copy(f(), (s.me, (s.p + q) % s.ndp), self.JP + (q-1)*4*s.na + f()))

    def start(self):
        s = self.s; na = s.na
        up, down = s.a < na - 1, s.a > 0
        @pl.when(up)
        def _(): self.send(up, lambda: self.copy(s.me, s.dev(s.a + 1), self.JU, src=self.own))
        @pl.when(down)
        def _(): self.send(down, lambda: self.copy(s.me, s.dev(s.a - 1), self.JD, src=self.own))
        self.send(None, lambda: self.copy(s.me, s.dev(s.a, 1, 0), self.J2 + s.a, src=self.own))
        self.send(None, lambda: self.copy(s.me, s.dev(s.a, 0, 1), self.J3 + s.a*2, src=self.own))

    def events(self):
        s = self.s; na = s.na
        def chain(up, k):
            a = s.a - 1 - k if up else s.a + 1 + k
            cond = a >= 0 if up else a < na
            fwd = s.a < na - 1 if up else s.a > 0
            both = cond & fwd
            j = (self.JU if up else self.JD) + k
            def go():
                self.wait(s.at(a), j)
                if k < na - 2:
                    @pl.when(fwd)
                    def _(): self.send(both, lambda: self.copy(s.at(a), s.dev(s.a + 1 if up else s.a - 1), j + 1))
                self.send(cond, lambda: self.copy(s.at(a), s.dev(s.a, 1, 0), self.J2 + a))
                self.send(cond, lambda: self.copy(s.at(a), s.dev(s.a, 0, 1), self.J3 + a*2))
                self.dp(cond, lambda: s.at(a))
            return cond, go
        def second(a, cond):
            def go():
                self.wait(s.at(a, 1, 0), self.J2 + a)
                self.send(cond, lambda: self.copy(s.at(a, 1, 0), s.dev(s.a, 0, 1), self.J3 + a*2 + 1))
                self.dp(cond, lambda: s.at(a, 1, 0))
            return cond, go
        def third(a, cond, x):
            def go():
                self.wait(s.at(a, x, 1), self.J3 + a*2 + x)
                self.dp(cond, lambda: s.at(a, x, 1))
            return cond, go
        levels = [[(s.a, None)]]
        for k in range(na - 1):
            levels.append([(s.a - 1 - k, s.a - 1 - k >= 0), (s.a + 1 + k, s.a + 1 + k < na)])
        out = []
        for k in range(na + 2):
            if k < na - 1: out += [chain(True, k), chain(False, k)]
            if k < na:
                out += [second(a, cd) for a, cd in levels[k]]
                out += [third(a, cd, 0) for a, cd in levels[k]]
            if 0 < k <= na:
                out += [third(a, cd, 1) for a, cd in levels[k-1]]
        return out

    def finish(self):
        s = self.s
        if self.dp_view is not None:
            for q in range(1, s.ndp):
                def body(f, _):
                    @pl.when(f != s.me)
                    def _():
                        j = self.JP + (q-1)*4*s.na + f
                        v = self.dp_view(f, (s.p + s.ndp - q) % s.ndp)
                        pltpu.make_async_remote_copy(src_ref=v, dst_ref=v, send_sem=self.ss.at[j], recv_sem=self.rs.at[j], device_id=(s.me, s.p), device_id_type=MESH).wait_recv()
                    return 0
                lax.fori_loop(0, 4*s.na, body, 0)
        self.drain()

    def drain(self):
        for cond, make in self.log:
            if cond is None:
                make().wait_send()
            else:
                @pl.when(cond)
                def _(): make().wait_send()

def run_event(ev):
    cond, go = ev
    if cond is None: go()
    else: pl.when(cond)(go)

def forward_kernel(na, ndp, wa_sh, wf_sh, vecs, bff, lens_ref, tok_ref,
                   wa_out, wf_out, vec8, bias, q_ref, k_ref, v_ref, o_ref, lse_ref,
                   wa_c, wf_c, ex, wqkv, ot_s, tr_s, lsem, *sems):
    s = Spot(na, ndp)
    R = wa_sh.shape[0]
    tr_s[...] = jnp.zeros_like(tr_s)
    tr_s[0:R, 0:8] = vecs[...]
    ex[s.me, 0:8, :] = tr_s[...].T[0:8, :].astype(BF16).astype(F32)
    for j in range(4):
        ex[s.me, 8+j:9+j, 0:R] = bff[0:1, j*R:(j+1)*R].astype(BF16).astype(F32)
    wa_c[...] = wa_sh[...].astype(BF16)
    gs = []
    for i, (c, out) in enumerate(((wa_c, wa_out), (wf_c, wf_out))):
        w = c.shape[1] // ndp
        cols = lambda q, w=w: pl.ds(pl.multiple_of(q*w, 128), w)
        gs.append(Gather(s, c.at[:, cols(s.p)], lambda f, out=out, cols=cols: out.at[f, :, cols(s.p)], sems[2*i], sems[2*i+1],
                         lambda f, q, out=out, cols=cols: out.at[f, :, cols(q)]))
    gx = Gather(s, ex.at[s.me], lambda f: ex.at[f], sems[4], sems[5])
    ga, gf = gs
    s.barrier()
    gx.start(); ga.start()
    locs = [pltpu.make_async_copy(wa_c, wa_out.at[s.me], lsem.at[0])]
    locs[0].start()
    wf_c[...] = wf_sh[...].astype(BF16)
    locs.append(pltpu.make_async_copy(wf_c, wf_out.at[s.me], lsem.at[1]))
    locs[1].start()
    ea, exv, ef = ga.events(), gx.events(), gf.events()
    gf.start()
    for u, v in zip(ea, exv):
        run_event(v); run_event(u)
    for q in range(1, ndp):
        def body(f, _, q=q):
            @pl.when(f != s.me)
            def _():
                j = ga.JP + (q-1)*4*na + f
                v = ga.dp_view(f, (s.p + ndp - q) % ndp)
                pltpu.make_async_remote_copy(src_ref=v, dst_ref=v, send_sem=ga.ss.at[j], recv_sem=ga.rs.at[j], device_id=(s.me, s.p), device_id_type=MESH).wait_recv()
            return 0
        lax.fori_loop(0, 4*na, body, 0)
    locs[0].wait()
    load = pltpu.make_async_copy(wa_out.at[:, :, 0:3*D], wqkv, lsem.at[2])
    load.start()
    for f in range(4*na):
        vec8[:, f*R:(f+1)*R] = ex[f, 0:8, 0:R]
        for j in range(4):
            bias[0:1, (f*4+j)*R:(f*4+j+1)*R] = ex[f, 8+j:9+j, 0:R]
    load.wait()
    S = tok_ref.shape[0] // LMAX
    lane = lax.broadcasted_iota(jnp.int32, (LMAX, 128), 1)
    row = lax.broadcasted_iota(jnp.int32, (LMAX, 128), 0)
    one = jnp.ones((LMAX, 128), BF16); zero = jnp.zeros((LMAX, 128), BF16)
    PAIRS = HEADS // 2
    ntask = S*(3 + PAIRS)
    cut = [min(len(ef), int(RATE*t)) for t in range(ntask + 1)]
    def events_after(i, first, last):
        for t in range(first, last):
            evs = ef[cut[t]:cut[t+1]]
            if evs:
                @pl.when(i == t)
                def _():
                    for e in evs: run_event(e)
    w3 = wqkv.shape
    def proj(sl, which):
        rs = pl.ds(pl.multiple_of(sl*LMAX, LMAX), LMAX)
        x = tok_ref[rs, :]
        y = mm(x, wqkv[:, :, which*D:(which+1)*D].reshape(4*na*R, D))
        if which == 0: q_ref[rs, :] = ((y + vec8[0:1, :]).astype(BF16) * 0.125).astype(BF16)
        elif which == 1: k_ref[rs, :] = y.astype(BF16)
        else: v_ref[rs, :] = (y + vec8[1:2, :]).astype(BF16)
    def step1(i, _):
        for which in range(3):
            @pl.when(i % 3 == which)
            def _(): proj(i // 3, which)
        events_after(i, 0, 3*S)
        return 0
    lax.fori_loop(0, 3*S, step1, 0)
    def step2(i, _):
        sl = i // PAIRS; j = i % PAIRS
        rs = pl.ds(pl.multiple_of(sl*LMAX, LMAX), LMAX)
        ls = pl.ds(pl.multiple_of(j * 128, 128), 128)
        bar = jnp.where(row < lens_ref[sl], 0.0, -1e30).astype(BF16)
        q2 = q_ref[rs, ls]; k2 = k_ref[rs, ls]
        vt = v_ref[rs, ls].T
        raw = []
        for e in range(2):
            other = 64 * (1 - e)
            ka = jnp.where((lane >= 64) == (e == 1), k2, jnp.where(lane == other, bar, zero))
            qa = jnp.where(lane == other, one, q2)
            raw.append(mm(ka, qa, NT))
        for e in range(2):
            top = jnp.max(raw[e], axis=0, keepdims=True)
            p = jnp.exp(raw[e] - top)
            tot = jnp.sum(p, axis=0, keepdims=True)
            ot_s[64*e:64*e+64, :] = mm(vt[64*e:64*e+64], p.astype(BF16)) / tot
            lse_ref[pl.ds(sl*16 + 2*j + e, 1), :] = top + jnp.log(tot)
        o_ref[rs, ls] = ot_s[...].T.astype(BF16)
        events_after(i + 3*S, 3*S, ntask)
        return 0
    lax.fori_loop(0, S*PAIRS, step2, 0)
    for e in ef[cut[ntask]:]: run_event(e)
    gf.finish(); gx.finish()
    ga.drain()
    locs[1].wait()

def forward(mesh_shape, wa_sh, wf_sh, vecs, bff, lens, tokens, cid):
    F, ndp = mesh_shape
    na = F // 4; R = vecs.shape[0]; T = tokens.shape[0]
    NS = Gather.slots(na, ndp)
    S = jax.ShapeDtypeStruct
    V = pl.BlockSpec(memory_space=pltpu.VMEM); A = pl.BlockSpec(memory_space=pl.ANY)
    DMA = pltpu.SemaphoreType.DMA
    return pl.pallas_call(
        functools.partial(forward_kernel, na, ndp),
        out_shape=[S((F, R, 4*D), BF16), S((F, R, 2*FF), BF16), S((8, D), F32), S((1, FF), F32)] + [S((T, D), BF16)]*4 + [S((T//LMAX*16, LMAX), F32)],
        in_specs=[V, V, V, V, pl.BlockSpec(memory_space=pltpu.SMEM), V],
        out_specs=[A, A] + [V]*7,
        scratch_shapes=[pltpu.VMEM((R, 4*D), BF16), pltpu.VMEM((R, 2*FF), BF16), pltpu.VMEM((F, 16, 128), F32), pltpu.VMEM((F, R, 3*D), BF16),
                        pltpu.VMEM((128, LMAX), F32), pltpu.VMEM((128, 128), F32), DMA((3,))] + [DMA((NS,))]*6,
        compiler_params=pltpu.CompilerParams(collective_id=cid, has_side_effects=True, vmem_limit_bytes=56 << 20),
        name="gather_attend",
    )(wa_sh, wf_sh, vecs, bff, lens, tokens)


def as_int(cond):
    return cond.astype(jnp.int32)

class Reduce:
    def __init__(self, spot, src, mine, rd, r3, r2, c1, ss, rs, out, load=None):
        self.s = spot
        self.src, self.mine = src, mine
        self.rd, self.r3, self.r2, self.c1 = rd, r3, r2, c1
        self.ss, self.rs, self.out, self.load = ss, rs, out, load
        s = spot; na = s.na; F = 4*na
        self.B3 = (s.ndp - 1)*F; self.B2 = self.B3 + 2*na; self.B1 = self.B2 + na; self.BO = self.B1 + na
        self.log = []
        z = s.a; lower = as_int(z < na // 2)
        self.order = []
        for k in range(na):
            c1 = as_int(k < na - 1 - z); c2 = as_int(k < z)
            lo = c1*(na - 1 - k) + (1 - c1)*(k - (na - 1 - z))
            hi = c2*k + (1 - c2)*(na - 1 - (k - z))
            self.order.append(lower*lo + (1 - lower)*hi)
        self.bit2 = s.b*(1 - s.par) + s.c*s.par

    @staticmethod
    def slots(na, ndp):
        return (ndp - 1)*4*na + 4*na + ndp - 1

    def rc(self, src, dst, j, r, dev):
        return pltpu.make_async_remote_copy(src_ref=src, dst_ref=dst, send_sem=self.ss.at[j], recv_sem=self.rs.at[r], device_id=dev, device_id_type=MESH)

    def send(self, cond, make):
        make().start()
        self.log.append((cond, make))

    def wait(self, dst, r):
        self.rc(dst, dst, r, r, (self.s.me, self.s.p)).wait_recv()

    def start(self):
        s = self.s; na = s.na
        if self.load is not None:
            for y3, y2 in ((1, 1), (1, 0), (0, 1), (0, 0)):
                for k in range(na): self.load(s.at(self.order[k], y2, y3)).start()
        for y3, y2 in ((1, 1), (1, 0), (0, 1), (0, 0)):
            for k in range(na):
                for q in range(1, s.ndp):
                    x2, x3 = (y2, y3) if q % 2 == 0 else (y3, y2)
                    f = s.at(self.order[k], x2, x3)
                    dq = (s.p + q) % s.ndp
                    self.send(None, lambda f=f, q=q, dq=dq: self.rc(self.src(f, dq), self.rd.at[q-1, f], (q-1)*4*na + f, (q-1)*4*na + f, (s.me, dq)))

    def add(self, f, srcs, dst=None):
        s = self.s
        for q in range(1, s.ndp):
            self.wait(self.rd.at[q-1, f], (q-1)*4*s.na + f)
        if self.load is not None: self.load(f).wait()
        own = self.mine(f)
        dst = own if dst is None else dst
        srcs = [self.rd.at[q-1, f] for q in range(1, s.ndp)] + srcs
        w = own.shape[-1]
        CH = next(c for c in (512, 384, 256, 128) if w % c == 0)
        def body(j, _):
            cs = pl.ds(pl.multiple_of(j*CH, 128), CH)
            v = own[:, cs].astype(F32)
            for r in srcs: v = v + r[:, cs].astype(F32)
            dst[:, cs] = v.astype(dst.dtype)
            return 0
        lax.fori_loop(0, w // CH, body, 0)

    def events(self):
        s = self.s; na = s.na
        out = []
        for x2 in (1, 0):
            for k in range(na):
                def go(x2=x2, k=k):
                    a = self.order[k]; f = lambda: s.at(a, x2, 1)
                    slot = lambda: a*2 + self.bit2 + (1 - 2*self.bit2)*x2
                    self.add(f(), [])
                    self.send(None, lambda: self.rc(self.mine(f()), self.r3.at[slot()], self.B3 + slot(), self.B3 + slot(), s.dev(s.a, 0, 1)))
                out.append((None, go))
        for k in range(na):
            def go(k=k):
                a = self.order[k]; f = lambda: s.at(a, 1, 0)
                slot = a*2 + 1 - self.bit2
                self.wait(self.r3.at[slot], self.B3 + slot)
                self.add(f(), [self.r3.at[slot]])
                self.send(None, lambda: self.rc(self.mine(f()), self.r2.at[a], self.B2 + a, self.B2 + a, s.dev(s.a, 1, 0)))
            out.append((None, go))
        for k in range(na - 1):
            def go(k=k):
                a = self.order[k]; f = lambda: s.at(a)
                slot = a*2 + self.bit2
                self.wait(self.r3.at[slot], self.B3 + slot)
                self.wait(self.r2.at[a], self.B2 + a)
                self.add(f(), [self.r3.at[slot], self.r2.at[a]])
                self.send(None, lambda: self.rc(self.mine(f()), self.c1.at[s.a], self.B1 + k, self.B1 + s.a, s.dev(a)))
            out.append((None, go))
        def last():
            a = s.a; slot = a*2 + self.bit2
            self.wait(self.r3.at[slot], self.B3 + slot)
            self.wait(self.r2.at[a], self.B2 + a)
            others = [(a + k) % na for k in range(1, na)]
            for r in others: self.wait(self.c1.at[r], self.B1 + r)
            self.add(s.me, [self.r3.at[slot], self.r2.at[a]] + [self.c1.at[r] for r in others], self.out(s.p))
            for q in range(1, s.ndp):
                self.send(None, lambda q=q: self.rc(self.out(s.p), self.out(s.p), self.BO + q - 1, self.BO + q - 1, (s.me, (s.p + q) % s.ndp)))
        out.append((None, last))
        return out

    def finish(self):
        s = self.s
        for q in range(1, s.ndp):
            self.wait(self.out((s.p + s.ndp - q) % s.ndp), self.BO + q - 1)
        for cond, make in self.log:
            if cond is None: make().wait_send()
            else:
                @pl.when(cond)
                def _(): make().wait_send()

    @staticmethod
    def scratch(na, ndp, R, w):
        F = 4*na
        B = lambda *sh: pltpu.VMEM(sh + (R, w), BF16)
        NS = Reduce.slots(na, ndp)
        return [B(ndp - 1, F), B(2*na), B(na), B(na), pltpu.SemaphoreType.DMA((NS,)), pltpu.SemaphoreType.DMA((NS,))]

class SmallSum:
    def __init__(self, spot, buf, got, ss, rs):
        self.s, self.buf, self.got, self.ss, self.rs = spot, buf, got, ss, rs
        self.sent = []

    @staticmethod
    def scratch(na, ndp, shape):
        NX = ndp + 1 + na - 1
        return [pltpu.VMEM((4,) + shape, F32), pltpu.VMEM((NX,) + shape, F32), pltpu.SemaphoreType.DMA((NX,)), pltpu.SemaphoreType.DMA((NX,))]

    def go(self, i, j, dev):
        d = pltpu.make_async_remote_copy(src_ref=self.buf.at[i], dst_ref=self.got.at[j], send_sem=self.ss.at[j], recv_sem=self.rs.at[j], device_id=dev, device_id_type=MESH)
        d.start(); self.sent.append(d)

    def wait(self, j):
        pltpu.make_async_remote_copy(src_ref=self.got.at[j], dst_ref=self.got.at[j], send_sem=self.ss.at[j], recv_sem=self.rs.at[j], device_id=(self.s.me, self.s.p), device_id_type=MESH).wait_recv()

    def ordered(self, i, here, n, j0):
        def pick(m):
            v = self.buf[i]
            for q in range(1, n):
                v = jnp.where((here + n - q) % n == m, self.got[j0 + q - 1], v)
            return v
        v = pick(0)
        for m in range(1, n): v = v + pick(m)
        return v

    def start(self):
        s = self.s
        for q in range(1, s.ndp): self.go(0, q - 1, (s.me, (s.p + q) % s.ndp))

    def steps(self, out):
        s = self.s; X = s.ndp - 1
        def one():
            for q in range(1, s.ndp): self.wait(q - 1)
            self.buf[1] = self.ordered(0, s.p, s.ndp, 0)
            self.go(1, X, ((s.a*2 + s.b)*2 + 1 - s.c, s.p))
        def two():
            self.wait(X)
            self.buf[2] = self.buf[1] + self.got[X]
            self.go(2, X + 1, ((s.a*2 + 1 - s.b)*2 + s.c, s.p))
        def three():
            self.wait(X + 1)
            self.buf[3] = self.buf[2] + self.got[X + 1]
            for k in range(1, s.na): self.go(3, X + 1 + k, s.dev((s.a + k) % s.na))
        def four():
            for k in range(1, s.na): self.wait(X + 1 + k)
            out[...] = self.ordered(3, s.a, s.na, X + 2)
        return [one, two, three, four]

    def finish(self):
        for d in self.sent: d.wait_send()

def barrier_full(s):
    sem = pltpu.get_barrier_semaphore()
    def sig(dev): pl.semaphore_signal(sem, inc=1, device_id=dev, device_id_type=MESH)
    for k in range(1, s.na): sig(s.dev((s.a + k) % s.na))
    sig(s.dev(s.a, 1, 0)); sig(s.dev(s.a, 0, 1))
    for q in range(1, s.ndp): sig((s.me, (s.p + q) % s.ndp))
    pl.semaphore_wait(sem, s.na + s.ndp)

def backward_kernel(na, ndp, lens_ref, q_h, k_h, v_h, do_h, lse_ref, tok_h, dz_h, wa_h, gf_h, small_in,
                    dx_ref, of_ref, oq_ref, small_out,
                    q_ref, k_ref, v_ref, do_ref, tok_ref, wqkv, g_s, xt_s, dqt_s, wg, ownf, lsem, fsem, *sc):
    s = Spot(na, ndp)
    R = gf_h.shape[1]; T = tok_ref.shape[0]; S = T // LMAX
    PAIRS = HEADS // 2
    loads = []
    for i, (h, r) in enumerate(((q_h, q_ref), (k_h, k_ref), (v_h, v_ref), (do_h, do_ref))):
        loads.append(pltpu.make_async_copy(h, r, lsem.at[i]))
    late = [pltpu.make_async_copy(tok_h, tok_ref, lsem.at[4]), pltpu.make_async_copy(wa_h.at[:, :, 0:3*D], wqkv, lsem.at[5]), pltpu.make_async_copy(dz_h, dx_ref, lsem.at[6])]
    wf = gf_h.shape[2] // ndp; wq = wg.shape[2] // ndp
    def cols(q, w): return pl.ds(pl.multiple_of(q*w, 128), w)
    cf = lambda f: pltpu.make_async_copy(gf_h.at[f, :, cols(s.p, wf)], ownf.at[f], fsem.at[f])
    rf = Reduce(s, lambda f, q: gf_h.at[f, :, cols(q, wf)], lambda f: ownf.at[f], *sc[0:6], lambda q: of_ref.at[:, cols(q, wf)], cf)
    rq = Reduce(s, lambda f, q: wg.at[f, :, cols(q, wq)], lambda f: wg.at[f, :, cols(s.p, wq)], *sc[6:12], lambda q: oq_ref.at[:, cols(q, wq)])
    xs = SmallSum(s, *sc[12:16])
    barrier_full(s)
    rf.start()
    for l in loads + late: l.start()
    both = rf.events()
    ntask = S*PAIRS
    n3, n2 = 2*na, na
    plan = [[] for _ in range(ntask)]
    quick, half = max(1, ntask // 4), ntask // 2
    for i, e in enumerate(both[:n3 + n2]):
        t = i*quick // n3 if i < n3 else half + (i - n3)*(ntask - half) // n2
        plan[t].append(e)
    chain_f, last_f = both[n3 + n2:-1], both[-1]

    lane = lax.broadcasted_iota(jnp.int32, (LMAX, 128), 1)
    row = lax.broadcasted_iota(jnp.int32, (LMAX, 128), 0)
    one = jnp.ones((LMAX, 128), BF16); zero = jnp.zeros((LMAX, 128), BF16)
    for l in loads: l.wait()
    def task(t, _):
        sl = t // PAIRS; j = t % PAIRS
        rs = pl.ds(pl.multiple_of(sl * LMAX, LMAX), LMAX)
        ls = pl.ds(pl.multiple_of(j * 128, 128), 128)
        bar = jnp.where(row < lens_ref[sl], 0.0, -1e30).astype(BF16)
        q2 = q_ref[rs, ls]; k2 = k_ref[rs, ls]; v2 = v_ref[rs, ls]; do2 = do_ref[rs, ls]
        kt = k2.T
        raw, dps = [], []
        for e in range(2):
            other = 64 * (1 - e)
            mine = (lane >= 64) == (e == 1)
            ka = jnp.where(mine, k2, jnp.where(lane == other, bar, zero))
            va = jnp.where(mine, v2, zero)
            qa = jnp.where(lane == other, one, q2)
            raw.append(mm(ka, qa, NT)); dps.append(mm(va, do2, NT))
        dvs, dks = [], []
        for e in range(2):
            p = jnp.exp(raw[e] - lse_ref[pl.ds(sl * 16 + 2*j + e, 1), :])
            pd = p * dps[e]
            ds = (pd - p * jnp.sum(pd, axis=0, keepdims=True)).astype(BF16)
            dvs.append(mm(p.astype(BF16), do2)); dks.append(mm(ds, q2))
            dqt_s[64*e:64*e+64, :] = mm(kt[64*e:64*e+64], ds)
        g_s[rs, pl.ds(pl.multiple_of(2*D + j*128, 128), 128)] = jnp.where(lane >= 64, dvs[1], dvs[0]).astype(BF16)
        g_s[rs, pl.ds(pl.multiple_of(D + j*128, 128), 128)] = jnp.where(lane >= 64, dks[1], dks[0]).astype(BF16)
        g_s[rs, ls] = (dqt_s[...].T * 0.125).astype(BF16)
        for n in range(ntask):
            if plan[n]:
                @pl.when(t == n)
                def _():
                    for e in plan[n]: run_event(e)
        return 0
    lax.fori_loop(0, ntask, task, 0)
    late[0].wait()
    xt_s[...] = tok_ref[...].T
    if wg.shape[2] > 3*D: wg[:, :, 3*D:] = jnp.zeros(wg.shape[:2] + (wg.shape[2] - 3*D,), BF16)
    def wgr(r, _):
        cs = pl.ds(pl.multiple_of(r * 256, 256), 256)
        wg[:, :, cs] = mm(xt_s[...], g_s[:, cs]).reshape(4*na, R, 256).astype(BF16)
        return 0
    lax.fori_loop(0, 3*D // 256, wgr, 0)
    rq.start()
    xs.buf[0] = small_in[...]
    xs.buf[0, 0:1, :] = jnp.sum(g_s[:, 0:D].astype(F32), axis=0, keepdims=True)
    xs.buf[0, 1:2, :] = jnp.sum(g_s[:, 2*D:3*D].astype(F32), axis=0, keepdims=True)
    xs.start()
    eq = rq.events(); small = xs.steps(small_out)
    for e in eq[:n3]: run_event(e)
    late[1].wait(); late[2].wait()
    def rows(r):
        rr = slice(r*256, (r+1)*256)
        dx_ref[rr, :] += mm(g_s[rr, :], wqkv[...].reshape(D, 3*D), NT)
    steps = [lambda r=r: rows(r) for r in range(T // 256)]
    chain_q = eq[n3 + n2:-1]
    small[0]()
    for e in chain_f: run_event(e)
    small[1]()
    for f in steps[:1]: f()
    for e in eq[n3:n3 + n2]: run_event(e)
    small[2]()
    run_event(last_f)
    rest = steps[1:]
    gap = -(-len(chain_q) // (len(rest) + 1))
    for i in range(len(rest) + 1):
        for e in chain_q[i*gap:(i+1)*gap]: run_event(e)
        if i < len(rest): rest[i]()
    small[3]()
    run_event(eq[-1])
    rf.finish(); rq.finish(); xs.finish()

def backward(mesh_shape, lens, q, k, v, do, lse, tokens, dz, wa3, gf, small, cid):
    F, ndp = mesh_shape
    na = F // 4; R = gf.shape[1]; T = tokens.shape[0]
    S = jax.ShapeDtypeStruct
    V = pl.BlockSpec(memory_space=pltpu.VMEM); A = pl.BlockSpec(memory_space=pl.ANY)
    up = lambda n: -(-n // (128*ndp)) * 128*ndp
    CQ = up(3*D)
    B = lambda *sh: pltpu.VMEM(sh, BF16)
    return pl.pallas_call(
        functools.partial(backward_kernel, na, ndp),
        out_shape=[S((T, D), F32), S((R, gf.shape[2]), F32), S((R, CQ), F32), S(small.shape, F32)],
        in_specs=[pl.BlockSpec(memory_space=pltpu.SMEM), A, A, A, A, V, A, A, A, A, V],
        out_specs=[V]*4,
        scratch_shapes=[B(T, D)]*5 + [B(F, R, 3*D)] + [B(T, 3*D), B(D, T), pltpu.VMEM((128, LMAX), F32),
                        B(F, R, CQ), B(F, R, gf.shape[2]//ndp), pltpu.SemaphoreType.DMA((7,)), pltpu.SemaphoreType.DMA((F,))]
                       + Reduce.scratch(na, ndp, R, gf.shape[2]//ndp) + Reduce.scratch(na, ndp, R, CQ//ndp)
                       + SmallSum.scratch(na, ndp, small.shape),
        compiler_params=pltpu.CompilerParams(collective_id=cid, has_side_effects=True, vmem_limit_bytes=60 << 20),
        name="reduce_attend",
    )(lens, q, k, v, do, lse, tokens, dz, wa3, gf, small)


def adam_update(gradient, moment, second, master, adam_step, learn_rate):
    count = adam_step[0].astype(jnp.float32)
    moment_new = 0.9 * moment + 0.1 * gradient
    second_new = 0.98 * second + 0.02 * gradient * gradient
    first_fix = moment_new / (1.0 - jnp.power(0.9, count))
    second_fix = second_new / (1.0 - jnp.power(0.98, count))
    master_new = master - learn_rate[0] * (
        first_fix / (jnp.sqrt(second_fix) + 1e-06) + 0.01 * master
    )
    return (moment_new, second_new, master_new, master_new.astype(jnp.bfloat16))


def local(mesh_shape, tokens, cotangent, lengths, adam_step, learn_rate, attn_w, attn_m, attn_v, ffn_w, ffn_m, ffn_v,
          vecs, vecs_m, vecs_v, b_ff, bff_m, bff_v):
    shards, rows = mesh_shape[0], vecs.shape[0]
    T = tokens.shape[0]
    attn_low, ffn_low, vec8, bias, q, k, v, o, lse = forward(
        mesh_shape, attn_w, ffn_w, vecs, b_ff.reshape(1, 4 * rows), lengths, tokens, 1)
    attn_low = attn_low.reshape(D, 4 * D)
    ffn_low = ffn_low.reshape(D, 2 * FF)
    outputs, dz1, do, grads, small_ffn = ffn(o, tokens, cotangent, attn_low, ffn_low, vec8, bias, lengths)
    grads = jnp.pad(grads, ((0, 0), (0, -grads.shape[1] % (128 * mesh_shape[1]))))
    input_grad, summed, summed_qkv, summed_small = backward(
        mesh_shape, lengths, q, k, v, do, lse, tokens, dz1, attn_low.reshape(shards, rows, 4 * D),
        grads.reshape(shards, rows, grads.shape[1]), small_ffn, 2)
    summed_ffn = summed[:, : 2 * FF]
    summed_attn = jnp.concatenate([summed_qkv[:, : 3 * D], summed[:, 2 * FF : 2 * FF + D]], axis=1)
    mine = lax.axis_index("fsdp")
    summed_vecs = lax.dynamic_slice(summed_small, (0, mine * rows), (8, rows)).T
    summed_bias = lax.dynamic_slice(summed_small[8:12].reshape(FF), (mine * 4 * rows,), (4 * rows,))
    attn_new = adam_update(summed_attn, attn_m, attn_v, attn_w, adam_step, learn_rate)
    ffn_new = adam_update(summed_ffn, ffn_m, ffn_v, ffn_w, adam_step, learn_rate)
    vecs_new = adam_update(summed_vecs, vecs_m, vecs_v, vecs, adam_step, learn_rate)
    bff_new = adam_update(summed_bias, bff_m, bff_v, b_ff, adam_step, learn_rate)
    return (outputs, input_grad, summed_attn, *attn_new, summed_ffn, *ffn_new, summed_vecs, *vecs_new, summed_bias, *bff_new)


def solution(mesh):
    both, rows, whole = P(("fsdp", "dp")), P("fsdp"), P()
    return jax.shard_map(
        functools.partial(local, (mesh.shape["fsdp"], mesh.shape["dp"])),
        mesh=mesh,
        in_specs=(both, both, both, whole, whole) + (rows,) * 12,
        out_specs=(both, both) + (rows,) * 20,
        check_vma=False,
    )
```

```python
import functools

import jax
import jax.numpy as jnp
from jax import lax
from jax.experimental import pallas as pl
from jax.experimental.pallas import tpu as pltpu
from jax.sharding import PartitionSpec as P

MESH = pl.DeviceIdType.MESH

D = 768; HEADS = 12; HEAD = 64; FF = 3072; LMAX = 512
NN = (((1,), (0,)), ((), ()))
NT = (((1,), (1,)), ((), ()))
TN = (((0,), (0,)), ((), ()))
F32 = jnp.float32; BF16 = jnp.bfloat16
QC = 256

def mm(a, b, dims=NN):
    return lax.dot_general(a, b, dims, preferred_element_type=F32)

def attend_fwd_kernel(lens_ref, tok_ref, wq_ref, wk_ref, wv_ref, vec_ref, q_ref, k_ref, v_ref, o_ref, lse_ref, ot_ref):
    n = lens_ref[pl.program_id(0)]
    x = tok_ref[...]
    q_ref[...] = ((mm(x, wq_ref[...]) + vec_ref[0:1, :]).astype(BF16) * 0.125).astype(BF16)
    k_ref[...] = mm(x, wk_ref[...]).astype(BF16)
    v_ref[...] = (mm(x, wv_ref[...]) + vec_ref[1:2, :]).astype(BF16)
    lane = lax.broadcasted_iota(jnp.int32, (LMAX, 128), 1)
    row = lax.broadcasted_iota(jnp.int32, (LMAX, 128), 0)
    bar = jnp.where(row < n, 0.0, -1e30).astype(BF16)
    one = jnp.ones((LMAX, 128), BF16); zero = jnp.zeros((LMAX, 128), BF16)

    def pair(j, _):
        ls = pl.ds(pl.multiple_of(j * 128, 128), 128)
        q2 = q_ref[:, ls]; k2 = k_ref[:, ls]
        vt = v_ref[:, ls].T
        for e in range(2):
            other = 64 * (1 - e)
            ka = jnp.where((lane >= 64) == (e == 1), k2, jnp.where(lane == other, bar, zero))
            qa = jnp.where(lane == other, one, q2)
            for c in range(LMAX // QC):
                s = mm(ka, qa[c*QC:(c+1)*QC], NT)
                top = jnp.max(s, axis=0, keepdims=True)
                p = jnp.exp(s - top)
                tot = jnp.sum(p, axis=0, keepdims=True)
                o = mm(vt[64*e:64*e+64], p.astype(BF16))
                ot_ref[64*e:64*e+64, c*QC:(c+1)*QC] = o / tot
                lse_ref[pl.ds(2*j + e, 1), c*QC:(c+1)*QC] = top + jnp.log(tot)
        o_ref[:, ls] = ot_ref[...].T.astype(BF16)
        return 0
    lax.fori_loop(0, HEADS // 2, pair, 0)

def attend_fwd(tokens, wa, vec8, lens):
    S = tokens.shape[0] // LMAX
    row = pl.BlockSpec((LMAX, D), lambda s, l: (s, 0))
    w = lambda i: pl.BlockSpec((D, D), lambda s, l, i=i: (0, i))
    return pl.pallas_call(
        attend_fwd_kernel,
        out_shape=[jax.ShapeDtypeStruct((S*LMAX, D), BF16)]*4 + [jax.ShapeDtypeStruct((S*16, LMAX), F32)],
        grid_spec=pltpu.PrefetchScalarGridSpec(num_scalar_prefetch=1, grid=(S,),
            in_specs=[row, w(0), w(1), w(2), pl.BlockSpec((8, D), lambda s, l: (0, 0))],
            out_specs=[row]*4 + [pl.BlockSpec((16, LMAX), lambda s, l: (s, 0))],
            scratch_shapes=[pltpu.VMEM((128, LMAX), F32)]),
        name="attend_fwd",
    )(lens, tokens, wa, wa, wa, vec8)

def attend_bwd_kernel(lens_ref, q_ref, k_ref, v_ref, do_ref, lse_ref, tok_ref, dz_ref, wq_ref, wk_ref, wv_ref, dx_ref, dw_ref, small_ref,
                      dq_s, dk_s, dv_s, xt_s, dqt_s, acck, accv, lse_s):
    S = tok_ref.shape[0] // LMAX
    lane = lax.broadcasted_iota(jnp.int32, (LMAX, 128), 1)
    row = lax.broadcasted_iota(jnp.int32, (LMAX, 128), 0)
    one = jnp.ones((LMAX, 128), BF16); zero = jnp.zeros((LMAX, 128), BF16)
    xt_s[...] = tok_ref[...].T

    def task(t, _):
        sl = t // (HEADS // 2); j = t % (HEADS // 2)
        rs = pl.ds(pl.multiple_of(sl * LMAX, LMAX), LMAX)
        ls = pl.ds(pl.multiple_of(j * 128, 128), 128)
        bar = jnp.where(row < lens_ref[sl], 0.0, -1e30).astype(BF16)
        q2 = q_ref[rs, ls]; k2 = k_ref[rs, ls]; v2 = v_ref[rs, ls]; do2 = do_ref[rs, ls]
        kt = k2.T
        for e in range(2):
            other = 64 * (1 - e)
            mine = (lane >= 64) == (e == 1)
            ka = jnp.where(mine, k2, jnp.where(lane == other, bar, zero))
            va = jnp.where(mine, v2, zero)
            qa = jnp.where(lane == other, one, q2)
            lse_row = lse_ref[pl.ds(sl * 16 + 2*j + e, 1), :]
            for c in range(LMAX // QC):
                cs = slice(c*QC, (c+1)*QC)
                s = mm(ka, qa[cs], NT)
                p = jnp.exp(s - lse_row[:, cs])
                dp = mm(va, do2[cs], NT)
                pd = p * dp
                dsum = jnp.sum(pd, axis=0, keepdims=True)
                ds = (pd - p * dsum).astype(BF16)
                dvc = mm(p.astype(BF16), do2[cs])
                dkc = mm(ds, q2[cs])
                if c == 0:
                    dva, dka = dvc, dkc
                else:
                    dva, dka = dva + dvc, dka + dkc
                dqt_s[64*e:64*e+64, cs] = mm(kt[64*e:64*e+64], ds)
            if e == 0:
                accv[...] = dva; acck[...] = dka
            else:
                dv_s[rs, ls] = jnp.where(mine, dva, accv[...]).astype(BF16)
                dk_s[rs, ls] = jnp.where(mine, dka, acck[...]).astype(BF16)
        dq_s[rs, ls] = (dqt_s[...].T * 0.125).astype(BF16)
        return 0
    lax.fori_loop(0, S * (HEADS // 2), task, 0)
    small_ref[...] = jnp.zeros_like(small_ref)
    small_ref[0:1, :] = jnp.sum(dq_s[...].astype(F32), axis=0, keepdims=True)
    small_ref[1:2, :] = jnp.sum(dv_s[...].astype(F32), axis=0, keepdims=True)
    def rows(r, _):
        rr = pl.ds(pl.multiple_of(r * 256, 256), 256)
        dx_ref[rr, :] = dz_ref[rr, :] + mm(dq_s[rr, :], wq_ref[...], NT) + mm(dk_s[rr, :], wk_ref[...], NT) + mm(dv_s[rr, :], wv_ref[...], NT)
        return 0
    lax.fori_loop(0, S * LMAX // 256, rows, 0)
    for i, g in enumerate((dq_s, dk_s, dv_s)):
        def wg(r, _, g=g, i=i):
            rr = pl.ds(pl.multiple_of(r * 256, 256), 256)
            dw_ref[rr, i*D:(i+1)*D] = mm(xt_s[rr, :], g[...]).astype(BF16)
            return 0
        lax.fori_loop(0, D // 256, wg, 0)

def attend_bwd(q, k, v, do, lse, tokens, dz, wa, lens):
    T = tokens.shape[0]
    V = pl.BlockSpec(memory_space=pltpu.VMEM)
    w = lambda i: pl.BlockSpec((D, D), lambda s, l, i=i: (0, i))
    full = lambda a: pl.BlockSpec(a.shape, lambda s, l: (0, 0))
    o = lambda sh: pl.BlockSpec(sh, lambda s, l: (0, 0))
    return pl.pallas_call(
        attend_bwd_kernel,
        out_shape=[jax.ShapeDtypeStruct((T, D), F32), jax.ShapeDtypeStruct((D, 3*D), BF16), jax.ShapeDtypeStruct((8, D), F32)],
        grid_spec=pltpu.PrefetchScalarGridSpec(num_scalar_prefetch=1, grid=(1,),
            in_specs=[full(q)]*4 + [full(lse), full(tokens), full(dz), w(0), w(1), w(2)],
            out_specs=[o((T, D)), o((D, 3*D)), o((8, D))],
            scratch_shapes=[pltpu.VMEM((T, D), BF16)]*3 + [pltpu.VMEM((D, T), BF16), pltpu.VMEM((128, LMAX), F32), pltpu.VMEM((LMAX, 128), F32), pltpu.VMEM((LMAX, 128), F32), pltpu.VMEM((8, 128), F32)]),
        name="attend_bwd",
    )(lens, q, k, v, do, lse, tokens, dz, wa, wa, wa)


M = 256
NB = 768


def gelu_pair(u):
    phi = 0.5 * (1.0 + lax.erf(u * 0.7071067811865476))
    e = jnp.exp(-0.5 * (u * u))
    return u * phi, phi + u * (e * 0.3989422804014327)

def norm_stats(z):
    mean = jnp.mean(z, axis=-1, keepdims=True)
    c = z - mean
    var = jnp.mean(c * c, axis=-1, keepdims=True)
    r = lax.rsqrt(var + 1e-5)
    return c * r, r

def norm_back(dxh, xh, r):
    return r * (dxh - jnp.mean(dxh, axis=-1, keepdims=True) - xh * jnp.mean(dxh * xh, axis=-1, keepdims=True))

def colsum(x):
    return jnp.sum(x, axis=0, keepdims=True)

def ffn_kernel(tiles, lens_ref, o_ref, tok_ref, cot_ref, wa_h, wf_h, vec_ref, b1_ref,
               out_ref, dz_ref, do_ref, gf_ref, small_ref,
               wo_ref, w1_ref, w2_ref, gp_s, ot_s, da_s, ht_s, dft_s, g_s, du_s, sem):
    t = pl.program_id(0); per = LMAX // M
    live = [(lens_ref[u // per] > (u % per) * M).astype(jnp.int32) for u in range(tiles)]
    count = sum(live)
    loads = [pltpu.make_async_copy(wa_h.at[:, 3*D:4*D], wo_ref, sem.at[0]), pltpu.make_async_copy(wf_h.at[:, 0:FF], w1_ref, sem.at[1]), pltpu.make_async_copy(wf_h.at[:, FF:2*FF], w2_ref, sem.at[2])]
    def arrived(i):
        @pl.when(t == 0)
        def _(): loads[i].wait()

    @pl.when(t == 0)
    def _():
        for l in loads: l.start()
        small_ref[...] = jnp.zeros_like(small_ref)

    n = lens_ref[jnp.minimum(t, tiles - 1) // per] - (t % per) * M

    @pl.when((t < tiles) & (n <= 0))
    def _():
        for r in (out_ref, dz_ref, do_ref):
            r[...] = jnp.zeros_like(r)

    @pl.when((t < tiles) & (n > 0))
    def _():
        pos = sum(live[u] * (u < t).astype(jnp.int32) for u in range(tiles))
        rs = pl.ds(pl.multiple_of(pos * M, M), M)
        v = lambda i: vec_ref[i:i+1, :]
        o = o_ref[...]
        arrived(0)
        z1 = tok_ref[...].astype(F32) + (mm(o, wo_ref[...]) + v(2))
        ot_s[:, rs] = o.T
        xh1, r1 = norm_stats(z1)
        h = xh1 * v(3) + v(4)
        hb = h.astype(BF16)
        ht_s[:, rs] = hb.T
        arrived(1)
        arrived(2)
        f = None
        CF = 512
        cuts = [slice(c, c + CF) for c in range(0, FF, CF)]
        u = mm(hb, w1_ref[:, cuts[0]]) + b1_ref[:, cuts[0]]
        for j, cs in enumerate(cuts):
            nxt = mm(hb, w1_ref[:, cuts[j+1]]) + b1_ref[:, cuts[j+1]] if j + 1 < len(cuts) else None
            g, gp = gelu_pair(u)
            gb = g.astype(BF16)
            g_s[rs, cs] = gb
            gp_s[:, cs] = gp
            part = mm(gb, w2_ref[:, cs], NT)
            f = part if f is None else f + part
            u = nxt
        z2 = h + (f + v(5))
        xh2, r2 = norm_stats(z2)
        keep = lax.broadcasted_iota(jnp.int32, (M, 1), 0) < n
        out_ref[...] = jnp.where(keep, xh2 * v(6) + v(7), 0.0).astype(BF16)
        dy = jnp.where(keep, cot_ref[...].astype(F32), 0.0)
        small_ref[7:8, :] += colsum(dy)
        small_ref[6:7, :] += colsum(dy * xh2)
        dz2 = norm_back(dy * v(6), xh2, r2)
        df = dz2.astype(BF16)
        dft_s[:, rs] = df.T
        small_ref[5:6, :] += colsum(df.astype(F32))
        du = (gp_s[...] * mm(df, w2_ref[...])).astype(BF16)
        du_s[rs, :] = du
        db1 = colsum(du.astype(F32))
        for i in range(4):
            small_ref[8+i:9+i, :] += db1[:, i*D:(i+1)*D]
        dh = dz2 + mm(du, w1_ref[...], NT)
        small_ref[4:5, :] += colsum(dh)
        small_ref[3:4, :] += colsum(dh * xh1)
        dz1 = norm_back(dh * v(3), xh1, r1)
        da = dz1.astype(BF16)
        small_ref[2:3, :] += colsum(da.astype(F32))
        dz_ref[...] = dz1
        da_s[rs, :] = da
        do_ref[...] = mm(da, wo_ref[...], NT).astype(BF16)

    i = t - tiles
    half = FF // NB
    for kk in range(1, tiles + 1):
        K = kk*M
        for lt, r, c0, n0, n1 in ((ht_s, du_s, 0, 0, half), (dft_s, g_s, half, half, 2*half), (ot_s, da_s, 2*half, 2*half, 2*half + 1)):
            @pl.when((count == kk) & (i >= n0) & (i < n1))
            def _(lt=lt, r=r, K=K, c0=c0):
                cs = pl.ds(pl.multiple_of((i - c0) * NB, NB), NB)
                gf_ref[...] = mm(lt[:, :K], r[:K, cs]).astype(BF16)

def ffn(o, tokens, cot, wa, wf, vec8, b1, lens):
    T = tokens.shape[0]; tiles = T // M; chunks = 2*FF // NB + 1
    row = pl.BlockSpec((M, D), lambda t, l: (jnp.minimum(t, tiles - 1), 0))
    one = lambda sh: pl.BlockSpec(sh, lambda t, l: (0, 0))
    A = pl.BlockSpec(memory_space=pl.ANY)
    S = jax.ShapeDtypeStruct
    B = lambda *sh: pltpu.VMEM(sh, BF16)
    return pl.pallas_call(
        functools.partial(ffn_kernel, tiles),
        out_shape=[S((T, D), BF16), S((T, D), F32), S((T, D), BF16), S((D, chunks*NB), BF16), S((16, D), F32)],
        grid_spec=pltpu.PrefetchScalarGridSpec(num_scalar_prefetch=1, grid=(tiles + chunks,),
            in_specs=[row, row, row, A, A, one((8, D)), one((1, FF))],
            out_specs=[row, row, row, pl.BlockSpec((D, NB), lambda t, l: (0, jnp.maximum(t - tiles, 0))), one((16, D))],
            scratch_shapes=[B(D, D), B(D, FF), B(D, FF), pltpu.VMEM((M, FF), F32), B(D, T), B(T, D), B(D, T), B(D, T), B(T, FF), B(T, FF), pltpu.SemaphoreType.DMA((3,))]),
        compiler_params=pltpu.CompilerParams(vmem_limit_bytes=60 << 20),
        name="ffn",
    )(lens, o, tokens, cot, wa, wf, vec8, b1)


RATE = 1.0

class Spot:
    def __init__(self, na, ndp):
        self.na, self.ndp = na, ndp
        self.me = lax.axis_index("fsdp"); self.p = lax.axis_index("dp")
        self.a = self.me // 4; self.b = (self.me // 2) % 2; self.c = self.me % 2
        self.par = self.p % 2
        self.b2 = self.b + (1 - 2*self.b)*(1 - self.par); self.c2 = self.c + (1 - 2*self.c)*self.par
        self.b3 = self.b + (1 - 2*self.b)*self.par; self.c3 = self.c + (1 - 2*self.c)*(1 - self.par)

    def at(self, a, flip2=0, flip3=0):
        if flip2 and flip3:
            b, c = 1 - self.b, 1 - self.c
        elif flip2:
            b, c = self.b2, self.c2
        elif flip3:
            b, c = self.b3, self.c3
        else:
            b, c = self.b, self.c
        return (a*2 + b)*2 + c

    def dev(self, a, flip2=0, flip3=0):
        return (self.at(a, flip2, flip3), self.p)

    def barrier(self):
        sem = pltpu.get_barrier_semaphore()
        up, down = self.a < self.na - 1, self.a > 0
        def sig(dev):
            pl.semaphore_signal(sem, inc=1, device_id=dev, device_id_type=MESH)
        @pl.when(up)
        def _(): sig(self.dev(self.a + 1))
        @pl.when(down)
        def _(): sig(self.dev(self.a - 1))
        sig(self.dev(self.a, 1, 0)); sig(self.dev(self.a, 0, 1))
        for q in range(1, self.ndp): sig((self.me, (self.p + q) % self.ndp))
        pl.semaphore_wait(sem, 1 + self.ndp + up.astype(jnp.int32) + down.astype(jnp.int32))

class Gather:
    def __init__(self, spot, own, view, ssem, rsem, dp_view=None):
        self.s, self.own, self.view, self.ss, self.rs, self.dp_view = spot, own, view, ssem, rsem, dp_view
        na = spot.na
        self.JU, self.JD = 0, na - 1
        self.J2 = 2*(na - 1); self.J3 = self.J2 + na; self.JP = self.J3 + 2*na
        self.log = []

    @staticmethod
    def slots(na, ndp):
        return 2*(na - 1) + na + 2*na + (ndp - 1)*4*na

    def copy(self, f, dev, j, r=None, src=None):
        v = self.view(f)
        return pltpu.make_async_remote_copy(src_ref=v if src is None else src, dst_ref=v, send_sem=self.ss.at[j],
                                            recv_sem=self.rs.at[j if r is None else r], device_id=dev, device_id_type=MESH)

    def send(self, cond, make):
        make().start()
        self.log.append((cond, make))

    def wait(self, f, j):
        self.copy(f, (self.s.me, self.s.p), j).wait_recv()

    def dp(self, cond, f):
        if self.dp_view is None: return
        s = self.s
        for q in range(1, s.ndp):
            self.send(cond, lambda q=q: self.copy(f(), (s.me, (s.p + q) % s.ndp), self.JP + (q-1)*4*s.na + f()))

    def start(self):
        s = self.s; na = s.na
        up, down = s.a < na - 1, s.a > 0
        @pl.when(up)
        def _(): self.send(up, lambda: self.copy(s.me, s.dev(s.a + 1), self.JU, src=self.own))
        @pl.when(down)
        def _(): self.send(down, lambda: self.copy(s.me, s.dev(s.a - 1), self.JD, src=self.own))
        self.send(None, lambda: self.copy(s.me, s.dev(s.a, 1, 0), self.J2 + s.a, src=self.own))
        self.send(None, lambda: self.copy(s.me, s.dev(s.a, 0, 1), self.J3 + s.a*2, src=self.own))

    def events(self):
        s = self.s; na = s.na
        def chain(up, k):
            a = s.a - 1 - k if up else s.a + 1 + k
            cond = a >= 0 if up else a < na
            fwd = s.a < na - 1 if up else s.a > 0
            both = cond & fwd
            j = (self.JU if up else self.JD) + k
            def go():
                self.wait(s.at(a), j)
                if k < na - 2:
                    @pl.when(fwd)
                    def _(): self.send(both, lambda: self.copy(s.at(a), s.dev(s.a + 1 if up else s.a - 1), j + 1))
                self.send(cond, lambda: self.copy(s.at(a), s.dev(s.a, 1, 0), self.J2 + a))
                self.send(cond, lambda: self.copy(s.at(a), s.dev(s.a, 0, 1), self.J3 + a*2))
                self.dp(cond, lambda: s.at(a))
            return cond, go
        def second(a, cond):
            def go():
                self.wait(s.at(a, 1, 0), self.J2 + a)
                self.send(cond, lambda: self.copy(s.at(a, 1, 0), s.dev(s.a, 0, 1), self.J3 + a*2 + 1))
                self.dp(cond, lambda: s.at(a, 1, 0))
            return cond, go
        def third(a, cond, x):
            def go():
                self.wait(s.at(a, x, 1), self.J3 + a*2 + x)
                self.dp(cond, lambda: s.at(a, x, 1))
            return cond, go
        levels = [[(s.a, None)]]
        for k in range(na - 1):
            levels.append([(s.a - 1 - k, s.a - 1 - k >= 0), (s.a + 1 + k, s.a + 1 + k < na)])
        out = []
        for k in range(na + 2):
            if k < na - 1: out += [chain(True, k), chain(False, k)]
            if k < na:
                out += [second(a, cd) for a, cd in levels[k]]
                out += [third(a, cd, 0) for a, cd in levels[k]]
            if 0 < k <= na:
                out += [third(a, cd, 1) for a, cd in levels[k-1]]
        return out

    def finish(self):
        s = self.s
        if self.dp_view is not None:
            for q in range(1, s.ndp):
                def body(f, _):
                    @pl.when(f != s.me)
                    def _():
                        j = self.JP + (q-1)*4*s.na + f
                        v = self.dp_view(f, (s.p + s.ndp - q) % s.ndp)
                        pltpu.make_async_remote_copy(src_ref=v, dst_ref=v, send_sem=self.ss.at[j], recv_sem=self.rs.at[j], device_id=(s.me, s.p), device_id_type=MESH).wait_recv()
                    return 0
                lax.fori_loop(0, 4*s.na, body, 0)
        self.drain()

    def drain(self):
        for cond, make in self.log:
            if cond is None:
                make().wait_send()
            else:
                @pl.when(cond)
                def _(): make().wait_send()

def run_event(ev):
    cond, go = ev
    if cond is None: go()
    else: pl.when(cond)(go)

def forward_kernel(na, ndp, wa_sh, wf_sh, vecs, bff, lens_ref, tok_ref,
                   wa_out, wf_out, vec8, bias, q_ref, k_ref, v_ref, o_ref, lse_ref,
                   wa_c, wf_c, ex, wqkv, ot_s, lsem, *sems):
    s = Spot(na, ndp)
    R = wa_sh.shape[0]
    ex[s.me, 0:8, 0:R] = vecs[...].astype(BF16).astype(F32)
    for j in range(4):
        ex[s.me, 8+j:9+j, 0:R] = bff[0:1, j*R:(j+1)*R].astype(BF16).astype(F32)
    wa_c[...] = wa_sh[...].astype(BF16)
    gs = []
    for i, (c, out) in enumerate(((wa_c, wa_out), (wf_c, wf_out))):
        w = c.shape[1] // ndp
        cols = lambda q, w=w: pl.ds(pl.multiple_of(q*w, 128), w)
        gs.append(Gather(s, c.at[:, cols(s.p)], lambda f, out=out, cols=cols: out.at[f, :, cols(s.p)], sems[2*i], sems[2*i+1],
                         lambda f, q, out=out, cols=cols: out.at[f, :, cols(q)]))
    gx = Gather(s, ex.at[s.me], lambda f: ex.at[f], sems[4], sems[5])
    ga, gf = gs
    s.barrier()
    gx.start(); ga.start()
    locs = [pltpu.make_async_copy(wa_c, wa_out.at[s.me], lsem.at[0])]
    locs[0].start()
    wf_c[...] = wf_sh[...].astype(BF16)
    locs.append(pltpu.make_async_copy(wf_c, wf_out.at[s.me], lsem.at[1]))
    locs[1].start()
    ea, exv, ef = ga.events(), gx.events(), gf.events()
    gf.start()
    for u, v in zip(ea, exv):
        run_event(v); run_event(u)
    for q in range(1, ndp):
        def body(f, _, q=q):
            @pl.when(f != s.me)
            def _():
                j = ga.JP + (q-1)*4*na + f
                v = ga.dp_view(f, (s.p + ndp - q) % ndp)
                pltpu.make_async_remote_copy(src_ref=v, dst_ref=v, send_sem=ga.ss.at[j], recv_sem=ga.rs.at[j], device_id=(s.me, s.p), device_id_type=MESH).wait_recv()
            return 0
        lax.fori_loop(0, 4*na, body, 0)
    locs[0].wait()
    load = pltpu.make_async_copy(wa_out.at[:, :, 0:3*D], wqkv, lsem.at[2])
    load.start()
    for f in range(4*na):
        vec8[:, f*R:(f+1)*R] = ex[f, 0:8, 0:R]
        for j in range(4):
            bias[0:1, (f*4+j)*R:(f*4+j+1)*R] = ex[f, 8+j:9+j, 0:R]
    load.wait()
    S = tok_ref.shape[0] // LMAX
    lane = lax.broadcasted_iota(jnp.int32, (LMAX, 128), 1)
    row = lax.broadcasted_iota(jnp.int32, (LMAX, 128), 0)
    one = jnp.ones((LMAX, 128), BF16); zero = jnp.zeros((LMAX, 128), BF16)
    PAIRS = HEADS // 2
    ntask = S*(3 + PAIRS)
    cut = [min(len(ef), int(RATE*t)) for t in range(ntask + 1)]
    def events_after(i, first, last):
        for t in range(first, last):
            evs = ef[cut[t]:cut[t+1]]
            if evs:
                @pl.when(i == t)
                def _():
                    for e in evs: run_event(e)
    w3 = wqkv.shape
    def proj(sl, which):
        rs = pl.ds(pl.multiple_of(sl*LMAX, LMAX), LMAX)
        x = tok_ref[rs, :]
        y = mm(x, wqkv[:, :, which*D:(which+1)*D].reshape(4*na*R, D))
        if which == 0: q_ref[rs, :] = ((y + vec8[0:1, :]).astype(BF16) * 0.125).astype(BF16)
        elif which == 1: k_ref[rs, :] = y.astype(BF16)
        else: v_ref[rs, :] = (y + vec8[1:2, :]).astype(BF16)
    def step1(i, _):
        for which in range(3):
            @pl.when(i % 3 == which)
            def _(): proj(i // 3, which)
        events_after(i, 0, 3*S)
        return 0
    lax.fori_loop(0, 3*S, step1, 0)
    def step2(i, _):
        sl = i // PAIRS; j = i % PAIRS
        rs = pl.ds(pl.multiple_of(sl*LMAX, LMAX), LMAX)
        ls = pl.ds(pl.multiple_of(j * 128, 128), 128)
        bar = jnp.where(row < lens_ref[sl], 0.0, -1e30).astype(BF16)
        q2 = q_ref[rs, ls]; k2 = k_ref[rs, ls]
        vt = v_ref[rs, ls].T
        raw = []
        for e in range(2):
            other = 64 * (1 - e)
            ka = jnp.where((lane >= 64) == (e == 1), k2, jnp.where(lane == other, bar, zero))
            qa = jnp.where(lane == other, one, q2)
            raw.append(mm(ka, qa, NT))
        for e in range(2):
            top = jnp.max(raw[e], axis=0, keepdims=True)
            p = jnp.exp(raw[e] - top)
            tot = jnp.sum(p, axis=0, keepdims=True)
            ot_s[64*e:64*e+64, :] = mm(vt[64*e:64*e+64], p.astype(BF16)) / tot
            lse_ref[pl.ds(sl*16 + 2*j + e, 1), :] = top + jnp.log(tot)
        o_ref[rs, ls] = ot_s[...].T.astype(BF16)
        events_after(i + 3*S, 3*S, ntask)
        return 0
    lax.fori_loop(0, S*PAIRS, step2, 0)
    for e in ef[cut[ntask]:]: run_event(e)
    gf.finish(); gx.finish()
    ga.drain()
    locs[1].wait()

def forward(mesh_shape, wa_sh, wf_sh, vecs, bff, lens, tokens, cid):
    F, ndp = mesh_shape
    na = F // 4; R = vecs.shape[1]; T = tokens.shape[0]
    NS = Gather.slots(na, ndp)
    S = jax.ShapeDtypeStruct
    V = pl.BlockSpec(memory_space=pltpu.VMEM); A = pl.BlockSpec(memory_space=pl.ANY)
    DMA = pltpu.SemaphoreType.DMA
    return pl.pallas_call(
        functools.partial(forward_kernel, na, ndp),
        out_shape=[S((F, R, 4*D), BF16), S((F, R, 2*FF), BF16), S((8, D), F32), S((1, FF), F32)] + [S((T, D), BF16)]*4 + [S((T//LMAX*16, LMAX), F32)],
        in_specs=[V, V, V, V, pl.BlockSpec(memory_space=pltpu.SMEM), V],
        out_specs=[A, A] + [V]*7,
        scratch_shapes=[pltpu.VMEM((R, 4*D), BF16), pltpu.VMEM((R, 2*FF), BF16), pltpu.VMEM((F, 16, 128), F32), pltpu.VMEM((F, R, 3*D), BF16),
                        pltpu.VMEM((128, LMAX), F32), DMA((3,))] + [DMA((NS,))]*6,
        compiler_params=pltpu.CompilerParams(collective_id=cid, has_side_effects=True, vmem_limit_bytes=56 << 20),
        name="gather_attend",
    )(wa_sh, wf_sh, vecs, bff, lens, tokens)


def as_int(cond):
    return cond.astype(jnp.int32)

class Reduce:
    def __init__(self, spot, src, mine, rd, r3, r2, cu, cd, ss, rs, out, load=None):
        self.s = spot
        self.src, self.mine = src, mine
        self.rd, self.r3, self.r2, self.cu, self.cd = rd, r3, r2, cu, cd
        self.ss, self.rs, self.out, self.load = ss, rs, out, load
        s = spot; na = s.na; F = 4*na
        self.B3 = (s.ndp - 1)*F; self.B2 = self.B3 + 2*na; self.BU = self.B2 + na; self.BD = self.BU + na; self.BO = self.BD + na
        self.log = []
        z = s.a; lower = as_int(z < na // 2)
        self.order = []
        for k in range(na):
            c1 = as_int(k < na - 1 - z); c2 = as_int(k < z)
            lo = c1*(na - 1 - k) + (1 - c1)*(k - (na - 1 - z))
            hi = c2*k + (1 - c2)*(na - 1 - (k - z))
            self.order.append(lower*lo + (1 - lower)*hi)
        self.bit2 = s.b*(1 - s.par) + s.c*s.par

    @staticmethod
    def slots(na, ndp):
        return (ndp - 1)*4*na + 5*na + ndp - 1

    def rc(self, src, dst, j, r, dev):
        return pltpu.make_async_remote_copy(src_ref=src, dst_ref=dst, send_sem=self.ss.at[j], recv_sem=self.rs.at[r], device_id=dev, device_id_type=MESH)

    def send(self, cond, make):
        make().start()
        self.log.append((cond, make))

    def wait(self, dst, r):
        self.rc(dst, dst, r, r, (self.s.me, self.s.p)).wait_recv()

    def start(self):
        s = self.s; na = s.na
        if self.load is not None:
            for y3, y2 in ((1, 1), (1, 0), (0, 1), (0, 0)):
                for k in range(na): self.load(s.at(self.order[k], y2, y3)).start()
        for y3, y2 in ((1, 1), (1, 0), (0, 1), (0, 0)):
            for k in range(na):
                for q in range(1, s.ndp):
                    x2, x3 = (y2, y3) if q % 2 == 0 else (y3, y2)
                    f = s.at(self.order[k], x2, x3)
                    dq = (s.p + q) % s.ndp
                    self.send(None, lambda f=f, q=q, dq=dq: self.rc(self.src(f, dq), self.rd.at[q-1, f], (q-1)*4*na + f, (q-1)*4*na + f, (s.me, dq)))

    def add(self, f, srcs, dst=None):
        s = self.s
        for q in range(1, s.ndp):
            self.wait(self.rd.at[q-1, f], (q-1)*4*s.na + f)
        if self.load is not None: self.load(f).wait()
        own = self.mine(f)
        dst = own if dst is None else dst
        srcs = [self.rd.at[q-1, f] for q in range(1, s.ndp)] + srcs
        w = own.shape[-1]
        CH = next(c for c in (512, 384, 256, 128) if w % c == 0)
        def body(j, _):
            cs = pl.ds(pl.multiple_of(j*CH, 128), CH)
            v = own[:, cs].astype(F32)
            for r in srcs: v = v + r[:, cs].astype(F32)
            dst[:, cs] = v.astype(dst.dtype)
            return 0
        lax.fori_loop(0, w // CH, body, 0)

    def events(self):
        s = self.s; na = s.na
        out = []
        for x2 in (1, 0):
            for k in range(na):
                def go(x2=x2, k=k):
                    a = self.order[k]; f = lambda: s.at(a, x2, 1)
                    slot = lambda: a*2 + self.bit2 + (1 - 2*self.bit2)*x2
                    self.add(f(), [])
                    self.send(None, lambda: self.rc(self.mine(f()), self.r3.at[slot()], self.B3 + slot(), self.B3 + slot(), s.dev(s.a, 0, 1)))
                out.append((None, go))
        for k in range(na):
            def go(k=k):
                a = self.order[k]; f = lambda: s.at(a, 1, 0)
                slot = a*2 + 1 - self.bit2
                self.wait(self.r3.at[slot], self.B3 + slot)
                self.add(f(), [self.r3.at[slot]])
                self.send(None, lambda: self.rc(self.mine(f()), self.r2.at[a], self.B2 + a, self.B2 + a, s.dev(s.a, 1, 0)))
            out.append((None, go))
        for k in range(na - 1, 0, -1):
            for up in (True, False):
                a = s.a + k if up else s.a - k
                cond = a < na if up else a >= 0
                more = s.a > 0 if up else s.a < na - 1
                buf, B = (self.cu, self.BU) if up else (self.cd, self.BD)
                def go(a=a, cond=cond, more=more, buf=buf, B=B, up=up):
                    slot = a*2 + self.bit2
                    f = lambda: s.at(a)
                    self.wait(self.r3.at[slot], self.B3 + slot)
                    self.wait(self.r2.at[a], self.B2 + a)
                    base = [self.r3.at[slot], self.r2.at[a]]
                    @pl.when(more)
                    def _():
                        self.wait(buf.at[a], B + a)
                        self.add(f(), base + [buf.at[a]])
                    @pl.when(jnp.logical_not(more))
                    def _(): self.add(f(), base)
                    self.send(cond, lambda: self.rc(self.mine(f()), buf.at[a], B + a, B + a, s.dev(s.a + 1 if up else s.a - 1)))
                out.append((cond, go))
        def last():
            a = s.a; slot = a*2 + self.bit2
            self.wait(self.r3.at[slot], self.B3 + slot)
            self.wait(self.r2.at[a], self.B2 + a)
            base = [self.r3.at[slot], self.r2.at[a]]
            dst = self.out(s.p)
            @pl.when(a == 0)
            def _():
                self.wait(self.cd.at[a], self.BD + a)
                self.add(s.me, base + [self.cd.at[a]], dst)
            @pl.when(a == na - 1)
            def _():
                self.wait(self.cu.at[a], self.BU + a)
                self.add(s.me, base + [self.cu.at[a]], dst)
            @pl.when((a > 0) & (a < na - 1))
            def _():
                self.wait(self.cd.at[a], self.BD + a)
                self.wait(self.cu.at[a], self.BU + a)
                self.add(s.me, base + [self.cd.at[a], self.cu.at[a]], dst)
            for q in range(1, s.ndp):
                self.send(None, lambda q=q: self.rc(self.out(s.p), self.out(s.p), self.BO + q - 1, self.BO + q - 1, (s.me, (s.p + q) % s.ndp)))
        out.append((None, last))
        return out

    def finish(self):
        s = self.s
        for q in range(1, s.ndp):
            self.wait(self.out((s.p + s.ndp - q) % s.ndp), self.BO + q - 1)
        for cond, make in self.log:
            if cond is None: make().wait_send()
            else:
                @pl.when(cond)
                def _(): make().wait_send()

    @staticmethod
    def scratch(na, ndp, R, w):
        F = 4*na
        B = lambda *sh: pltpu.VMEM(sh + (R, w), BF16)
        NS = Reduce.slots(na, ndp)
        return [B(ndp - 1, F), B(2*na), B(na), B(na), B(na), pltpu.SemaphoreType.DMA((NS,)), pltpu.SemaphoreType.DMA((NS,))]

class SmallSum:
    def __init__(self, spot, buf, got, ss, rs):
        self.s, self.buf, self.got, self.ss, self.rs = spot, buf, got, ss, rs
        self.sent = []

    @staticmethod
    def scratch(na, ndp, shape):
        NX = ndp + 1 + na - 1
        return [pltpu.VMEM((4,) + shape, F32), pltpu.VMEM((NX,) + shape, F32), pltpu.SemaphoreType.DMA((NX,)), pltpu.SemaphoreType.DMA((NX,))]

    def go(self, i, j, dev):
        d = pltpu.make_async_remote_copy(src_ref=self.buf.at[i], dst_ref=self.got.at[j], send_sem=self.ss.at[j], recv_sem=self.rs.at[j], device_id=dev, device_id_type=MESH)
        d.start(); self.sent.append(d)

    def wait(self, j):
        pltpu.make_async_remote_copy(src_ref=self.got.at[j], dst_ref=self.got.at[j], send_sem=self.ss.at[j], recv_sem=self.rs.at[j], device_id=(self.s.me, self.s.p), device_id_type=MESH).wait_recv()

    def ordered(self, i, here, n, j0):
        def pick(m):
            v = self.buf[i]
            for q in range(1, n):
                v = jnp.where((here + n - q) % n == m, self.got[j0 + q - 1], v)
            return v
        v = pick(0)
        for m in range(1, n): v = v + pick(m)
        return v

    def start(self):
        s = self.s
        for q in range(1, s.ndp): self.go(0, q - 1, (s.me, (s.p + q) % s.ndp))

    def steps(self, out):
        s = self.s; X = s.ndp - 1
        def one():
            for q in range(1, s.ndp): self.wait(q - 1)
            self.buf[1] = self.ordered(0, s.p, s.ndp, 0)
            self.go(1, X, ((s.a*2 + s.b)*2 + 1 - s.c, s.p))
        def two():
            self.wait(X)
            self.buf[2] = self.buf[1] + self.got[X]
            self.go(2, X + 1, ((s.a*2 + 1 - s.b)*2 + s.c, s.p))
        def three():
            self.wait(X + 1)
            self.buf[3] = self.buf[2] + self.got[X + 1]
            for k in range(1, s.na): self.go(3, X + 1 + k, s.dev((s.a + k) % s.na))
        def four():
            for k in range(1, s.na): self.wait(X + 1 + k)
            out[...] = self.ordered(3, s.a, s.na, X + 2)
        return [one, two, three, four]

    def finish(self):
        for d in self.sent: d.wait_send()

def barrier_full(s):
    sem = pltpu.get_barrier_semaphore()
    def sig(dev): pl.semaphore_signal(sem, inc=1, device_id=dev, device_id_type=MESH)
    for k in range(1, s.na): sig(s.dev((s.a + k) % s.na))
    sig(s.dev(s.a, 1, 0)); sig(s.dev(s.a, 0, 1))
    for q in range(1, s.ndp): sig((s.me, (s.p + q) % s.ndp))
    pl.semaphore_wait(sem, s.na + s.ndp)

def backward_kernel(na, ndp, lens_ref, q_h, k_h, v_h, do_h, lse_ref, tok_h, dz_h, wa_h, gf_h, small_in,
                    dx_ref, of_ref, oq_ref, small_out,
                    q_ref, k_ref, v_ref, do_ref, tok_ref, wqkv, g_s, xt_s, dqt_s, wg, ownf, lsem, fsem, *sc):
    s = Spot(na, ndp)
    R = gf_h.shape[1]; T = tok_ref.shape[0]; S = T // LMAX
    PAIRS = HEADS // 2
    loads = []
    for i, (h, r) in enumerate(((q_h, q_ref), (k_h, k_ref), (v_h, v_ref), (do_h, do_ref))):
        loads.append(pltpu.make_async_copy(h, r, lsem.at[i]))
    late = [pltpu.make_async_copy(tok_h, tok_ref, lsem.at[4]), pltpu.make_async_copy(wa_h.at[:, :, 0:3*D], wqkv, lsem.at[5]), pltpu.make_async_copy(dz_h, dx_ref, lsem.at[6])]
    wf = gf_h.shape[2] // ndp; wq = wg.shape[2] // ndp
    def cols(q, w): return pl.ds(pl.multiple_of(q*w, 128), w)
    cf = lambda f: pltpu.make_async_copy(gf_h.at[f, :, cols(s.p, wf)], ownf.at[f], fsem.at[f])
    rf = Reduce(s, lambda f, q: gf_h.at[f, :, cols(q, wf)], lambda f: ownf.at[f], *sc[0:7], lambda q: of_ref.at[:, cols(q, wf)], cf)
    rq = Reduce(s, lambda f, q: wg.at[f, :, cols(q, wq)], lambda f: wg.at[f, :, cols(s.p, wq)], *sc[7:14], lambda q: oq_ref.at[:, cols(q, wq)])
    xs = SmallSum(s, *sc[14:18])
    barrier_full(s)
    rf.start()
    for l in loads + late: l.start()
    both = rf.events()
    ntask = S*PAIRS
    n3, n2 = 2*na, na
    plan = [[] for _ in range(ntask)]
    quick, half = max(1, ntask // 4), ntask // 2
    for i, e in enumerate(both[:n3 + n2]):
        t = i*quick // n3 if i < n3 else half + (i - n3)*(ntask - half) // n2
        plan[t].append(e)
    chain_f, last_f = both[n3 + n2:-1], both[-1]

    lane = lax.broadcasted_iota(jnp.int32, (LMAX, 128), 1)
    row = lax.broadcasted_iota(jnp.int32, (LMAX, 128), 0)
    one = jnp.ones((LMAX, 128), BF16); zero = jnp.zeros((LMAX, 128), BF16)
    for l in loads: l.wait()
    def task(t, _):
        sl = t // PAIRS; j = t % PAIRS
        rs = pl.ds(pl.multiple_of(sl * LMAX, LMAX), LMAX)
        ls = pl.ds(pl.multiple_of(j * 128, 128), 128)
        bar = jnp.where(row < lens_ref[sl], 0.0, -1e30).astype(BF16)
        q2 = q_ref[rs, ls]; k2 = k_ref[rs, ls]; v2 = v_ref[rs, ls]; do2 = do_ref[rs, ls]
        kt = k2.T
        raw, dps = [], []
        for e in range(2):
            other = 64 * (1 - e)
            mine = (lane >= 64) == (e == 1)
            ka = jnp.where(mine, k2, jnp.where(lane == other, bar, zero))
            va = jnp.where(mine, v2, zero)
            qa = jnp.where(lane == other, one, q2)
            raw.append(mm(ka, qa, NT)); dps.append(mm(va, do2, NT))
        dvs, dks = [], []
        for e in range(2):
            p = jnp.exp(raw[e] - lse_ref[pl.ds(sl * 16 + 2*j + e, 1), :])
            pd = p * dps[e]
            ds = (pd - p * jnp.sum(pd, axis=0, keepdims=True)).astype(BF16)
            dvs.append(mm(p.astype(BF16), do2)); dks.append(mm(ds, q2))
            dqt_s[64*e:64*e+64, :] = mm(kt[64*e:64*e+64], ds)
        g_s[rs, pl.ds(pl.multiple_of(2*D + j*128, 128), 128)] = jnp.where(lane >= 64, dvs[1], dvs[0]).astype(BF16)
        g_s[rs, pl.ds(pl.multiple_of(D + j*128, 128), 128)] = jnp.where(lane >= 64, dks[1], dks[0]).astype(BF16)
        g_s[rs, ls] = (dqt_s[...].T * 0.125).astype(BF16)
        for n in range(ntask):
            if plan[n]:
                @pl.when(t == n)
                def _():
                    for e in plan[n]: run_event(e)
        return 0
    lax.fori_loop(0, ntask, task, 0)
    late[0].wait()
    xt_s[...] = tok_ref[...].T
    if wg.shape[2] > 3*D: wg[:, :, 3*D:] = jnp.zeros(wg.shape[:2] + (wg.shape[2] - 3*D,), BF16)
    def wgr(r, _):
        cs = pl.ds(pl.multiple_of(r * 256, 256), 256)
        wg[:, :, cs] = mm(xt_s[...], g_s[:, cs]).reshape(4*na, R, 256).astype(BF16)
        return 0
    lax.fori_loop(0, 3*D // 256, wgr, 0)
    rq.start()
    xs.buf[0] = small_in[...]
    xs.buf[0, 0:1, :] = jnp.sum(g_s[:, 0:D].astype(F32), axis=0, keepdims=True)
    xs.buf[0, 1:2, :] = jnp.sum(g_s[:, 2*D:3*D].astype(F32), axis=0, keepdims=True)
    xs.start()
    eq = rq.events(); small = xs.steps(small_out)
    for e in eq[:n3]: run_event(e)
    late[1].wait(); late[2].wait()
    def rows(r):
        rr = slice(r*256, (r+1)*256)
        dx_ref[rr, :] += mm(g_s[rr, :], wqkv[...].reshape(D, 3*D), NT)
    steps = [lambda r=r: rows(r) for r in range(T // 256)]
    chain_q = eq[n3 + n2:-1]
    small[0]()
    for e in chain_f: run_event(e)
    small[1]()
    for f in steps[:1]: f()
    for e in eq[n3:n3 + n2]: run_event(e)
    small[2]()
    run_event(last_f)
    rest = steps[1:]
    gap = -(-len(chain_q) // (len(rest) + 1))
    for i in range(len(rest) + 1):
        for e in chain_q[i*gap:(i+1)*gap]: run_event(e)
        if i < len(rest): rest[i]()
    small[3]()
    run_event(eq[-1])
    rf.finish(); rq.finish(); xs.finish()

def backward(mesh_shape, lens, q, k, v, do, lse, tokens, dz, wa3, gf, small, cid):
    F, ndp = mesh_shape
    na = F // 4; R = gf.shape[1]; T = tokens.shape[0]
    S = jax.ShapeDtypeStruct
    V = pl.BlockSpec(memory_space=pltpu.VMEM); A = pl.BlockSpec(memory_space=pl.ANY)
    up = lambda n: -(-n // (128*ndp)) * 128*ndp
    CQ = up(3*D)
    B = lambda *sh: pltpu.VMEM(sh, BF16)
    return pl.pallas_call(
        functools.partial(backward_kernel, na, ndp),
        out_shape=[S((T, D), F32), S((R, gf.shape[2]), F32), S((R, CQ), F32), S(small.shape, F32)],
        in_specs=[pl.BlockSpec(memory_space=pltpu.SMEM), A, A, A, A, V, A, A, A, A, V],
        out_specs=[V]*4,
        scratch_shapes=[B(T, D)]*5 + [B(F, R, 3*D)] + [B(T, 3*D), B(D, T), pltpu.VMEM((128, LMAX), F32),
                        B(F, R, CQ), B(F, R, gf.shape[2]//ndp), pltpu.SemaphoreType.DMA((7,)), pltpu.SemaphoreType.DMA((F,))]
                       + Reduce.scratch(na, ndp, R, gf.shape[2]//ndp) + Reduce.scratch(na, ndp, R, CQ//ndp)
                       + SmallSum.scratch(na, ndp, small.shape),
        compiler_params=pltpu.CompilerParams(collective_id=cid, has_side_effects=True, vmem_limit_bytes=60 << 20),
        name="reduce_attend",
    )(lens, q, k, v, do, lse, tokens, dz, wa3, gf, small)


STEPS = 4

def adam(g, m, v, w, fix1, fix2, rate):
    m_new = 0.9 * m + 0.1 * g
    v_new = 0.98 * v + 0.02 * g * g
    w_new = w - rate * ((m_new * fix1) / (jnp.sqrt(v_new * fix2) + 1e-06) + 0.01 * w)
    return m_new, v_new, w_new

def update_kernel(step_ref, rate_ref, gq_ref, go_ref, gf_ref, small_ref, dx_ref,
                  aw, am, av, fw, fm, fv, vw, vm, vv, bw, bm, bv, dxo, *outs):
    i = pl.program_id(0)
    count = jnp.full((8, 128), step_ref[0], jnp.int32).astype(F32)
    fix1 = (1.0 / (1.0 - jnp.exp(count * -0.10536051565782628)))[0:1, 0:1]
    fix2 = (1.0 / (1.0 - jnp.exp(count * -0.020202707317519466)))[0:1, 0:1]
    rate = rate_ref[0]

    def put(g, m, v, w, o):
        a, b, c = adam(g, m[...], v[...], w[...], fix1, fix2, rate)
        o[0][...] = g; o[1][...] = a; o[2][...] = b; o[3][...] = c; o[4][...] = c.astype(BF16)

    dxo[...] = dx_ref[...]
    put(gf_ref[...], fm, fv, fw, outs[5:10])
    cut = 3*D // (4*D // STEPS)
    @pl.when(i < cut)
    def _(): put(gq_ref[...], am, av, aw, outs[0:5])
    @pl.when(i >= cut)
    def _(): put(go_ref[...], am, av, aw, outs[0:5])

    @pl.when(i == 0)
    def _():
        R = vw.shape[1]
        f = lax.axis_index("fsdp")
        g = pltpu.roll(small_ref[0:8, :], lax.rem(D - f*R, D), 1)[:, 0:R]
        put(g, vm, vv, vw, outs[10:15])
        at = f*4*R
        x = pltpu.roll(small_ref[8:16, :], lax.rem(D - lax.rem(at, D), D), 1)
        here = lax.broadcasted_iota(jnp.int32, (8, D), 0) == at // D
        put(jnp.sum(jnp.where(here, x, 0.0), axis=0, keepdims=True)[:, 0:4*R], bm, bv, bw, outs[15:20])

def update(adam_step, learn_rate, gq, gall, small, dx, attn, ffn_, vecs, bff):
    R = vecs[0].shape[1]; T = dx.shape[0]
    ca, cf = 4*D // STEPS, 2*FF // STEPS
    cut = 3*D // ca
    blk = lambda w, fn=lambda i: i: pl.BlockSpec((R, w), lambda i, fn=fn: (0, fn(i)))
    one = lambda a: pl.BlockSpec(a.shape, lambda i: (0, 0))
    SM = pl.BlockSpec(memory_space=pltpu.SMEM)
    row = pl.BlockSpec((T // STEPS, D), lambda i: (i, 0))
    S = jax.ShapeDtypeStruct
    five = lambda sh: [S(sh, F32)]*4 + [S(sh, BF16)]
    tiny = lambda sh: [pl.BlockSpec(sh, lambda i: (0, 0))]*5
    return pl.pallas_call(
        update_kernel,
        grid=(STEPS,),
        out_shape=[S((T, D), F32)] + five((R, 4*D)) + five((R, 2*FF)) + five((8, R)) + five((1, 4*R)),
        in_specs=[SM, SM, blk(ca, lambda i: jnp.minimum(i, cut - 1)), blk(ca, lambda i: 2*FF // ca + jnp.maximum(i - cut, 0)), blk(cf), one(small), row]
                 + [blk(ca)]*3 + [blk(cf)]*3 + [one(v) for v in vecs] + [one(b) for b in bff],
        out_specs=[row] + [blk(ca)]*5 + [blk(cf)]*5 + tiny((8, R)) + tiny((1, 4*R)),
        name="update",
    )(adam_step, learn_rate, gq, gall, gall, small, dx, *attn, *ffn_, *vecs, *bff)


def local(mesh_shape, tokens, cotangent, lengths, adam_step, learn_rate, attn_w, attn_m, attn_v, ffn_w, ffn_m, ffn_v,
          vecs, vecs_m, vecs_v, b_ff, bff_m, bff_v):
    shards, rows = mesh_shape[0], vecs.shape[0]
    T = tokens.shape[0]
    attn_low, ffn_low, vec8, bias, q, k, v, o, lse = forward(
        mesh_shape, attn_w, ffn_w, vecs.T, b_ff.reshape(1, 4 * rows), lengths, tokens, 1)
    attn_low = attn_low.reshape(D, 4 * D)
    ffn_low = ffn_low.reshape(D, 2 * FF)
    outputs, dz1, do, grads, small_ffn = ffn(o, tokens, cotangent, attn_low, ffn_low, vec8, bias, lengths)
    grads = jnp.pad(grads, ((0, 0), (0, -grads.shape[1] % (128 * mesh_shape[1]))))
    input_grad, summed, summed_qkv, summed_small = backward(
        mesh_shape, lengths, q, k, v, do, lse, tokens, dz1, attn_low.reshape(shards, rows, 4 * D),
        grads.reshape(shards, rows, grads.shape[1]), small_ffn, 2)
    line = lambda x: x.reshape(1, 4 * rows)
    new = update(adam_step, learn_rate, summed_qkv, summed, summed_small, input_grad, (attn_w, attn_m, attn_v),
                 (ffn_w, ffn_m, ffn_v), (vecs.T, vecs_m.T, vecs_v.T), (line(b_ff), line(bff_m), line(bff_v)))
    return (outputs, new[0], *new[1:11], *[x.T for x in new[11:16]], *[x.reshape(4 * rows) for x in new[16:21]])


def solution(mesh):
    both, rows, whole = P(("fsdp", "dp")), P("fsdp"), P()
    return jax.shard_map(
        functools.partial(local, (mesh.shape["fsdp"], mesh.shape["dp"])),
        mesh=mesh,
        in_specs=(both, both, both, whole, whole) + (rows,) * 12,
        out_specs=(both, both) + (rows,) * 20,
        check_vma=False,
    )
```

```python
import functools

import jax
import jax.numpy as jnp
from jax import lax
from jax.experimental import pallas as pl
from jax.experimental.pallas import tpu as pltpu
from jax.sharding import PartitionSpec as P

MESH = pl.DeviceIdType.MESH

D = 768; HEADS = 12; HEAD = 64; FF = 3072; LMAX = 512
NN = (((1,), (0,)), ((), ()))
NT = (((1,), (1,)), ((), ()))
TN = (((0,), (0,)), ((), ()))
F32 = jnp.float32; BF16 = jnp.bfloat16
QC = 256

def mm(a, b, dims=NN):
    return lax.dot_general(a, b, dims, preferred_element_type=F32)

def attend_fwd_kernel(lens_ref, tok_ref, wq_ref, wk_ref, wv_ref, vec_ref, q_ref, k_ref, v_ref, o_ref, lse_ref, ot_ref):
    n = lens_ref[pl.program_id(0)]
    x = tok_ref[...]
    q_ref[...] = ((mm(x, wq_ref[...]) + vec_ref[0:1, :]).astype(BF16) * 0.125).astype(BF16)
    k_ref[...] = mm(x, wk_ref[...]).astype(BF16)
    v_ref[...] = (mm(x, wv_ref[...]) + vec_ref[1:2, :]).astype(BF16)
    lane = lax.broadcasted_iota(jnp.int32, (LMAX, 128), 1)
    row = lax.broadcasted_iota(jnp.int32, (LMAX, 128), 0)
    bar = jnp.where(row < n, 0.0, -1e30).astype(BF16)
    one = jnp.ones((LMAX, 128), BF16); zero = jnp.zeros((LMAX, 128), BF16)

    def pair(j, _):
        ls = pl.ds(pl.multiple_of(j * 128, 128), 128)
        q2 = q_ref[:, ls]; k2 = k_ref[:, ls]
        vt = v_ref[:, ls].T
        for e in range(2):
            other = 64 * (1 - e)
            ka = jnp.where((lane >= 64) == (e == 1), k2, jnp.where(lane == other, bar, zero))
            qa = jnp.where(lane == other, one, q2)
            for c in range(LMAX // QC):
                s = mm(ka, qa[c*QC:(c+1)*QC], NT)
                top = jnp.max(s, axis=0, keepdims=True)
                p = jnp.exp(s - top)
                tot = jnp.sum(p, axis=0, keepdims=True)
                o = mm(vt[64*e:64*e+64], p.astype(BF16))
                ot_ref[64*e:64*e+64, c*QC:(c+1)*QC] = o / tot
                lse_ref[pl.ds(2*j + e, 1), c*QC:(c+1)*QC] = top + jnp.log(tot)
        o_ref[:, ls] = ot_ref[...].T.astype(BF16)
        return 0
    lax.fori_loop(0, HEADS // 2, pair, 0)

def attend_fwd(tokens, wa, vec8, lens):
    S = tokens.shape[0] // LMAX
    row = pl.BlockSpec((LMAX, D), lambda s, l: (s, 0))
    w = lambda i: pl.BlockSpec((D, D), lambda s, l, i=i: (0, i))
    return pl.pallas_call(
        attend_fwd_kernel,
        out_shape=[jax.ShapeDtypeStruct((S*LMAX, D), BF16)]*4 + [jax.ShapeDtypeStruct((S*16, LMAX), F32)],
        grid_spec=pltpu.PrefetchScalarGridSpec(num_scalar_prefetch=1, grid=(S,),
            in_specs=[row, w(0), w(1), w(2), pl.BlockSpec((8, D), lambda s, l: (0, 0))],
            out_specs=[row]*4 + [pl.BlockSpec((16, LMAX), lambda s, l: (s, 0))],
            scratch_shapes=[pltpu.VMEM((128, LMAX), F32)]),
        name="attend_fwd",
    )(lens, tokens, wa, wa, wa, vec8)

def attend_bwd_kernel(lens_ref, q_ref, k_ref, v_ref, do_ref, lse_ref, tok_ref, dz_ref, wq_ref, wk_ref, wv_ref, dx_ref, dw_ref, small_ref,
                      dq_s, dk_s, dv_s, xt_s, dqt_s, acck, accv, lse_s):
    S = tok_ref.shape[0] // LMAX
    lane = lax.broadcasted_iota(jnp.int32, (LMAX, 128), 1)
    row = lax.broadcasted_iota(jnp.int32, (LMAX, 128), 0)
    one = jnp.ones((LMAX, 128), BF16); zero = jnp.zeros((LMAX, 128), BF16)
    xt_s[...] = tok_ref[...].T

    def task(t, _):
        sl = t // (HEADS // 2); j = t % (HEADS // 2)
        rs = pl.ds(pl.multiple_of(sl * LMAX, LMAX), LMAX)
        ls = pl.ds(pl.multiple_of(j * 128, 128), 128)
        bar = jnp.where(row < lens_ref[sl], 0.0, -1e30).astype(BF16)
        q2 = q_ref[rs, ls]; k2 = k_ref[rs, ls]; v2 = v_ref[rs, ls]; do2 = do_ref[rs, ls]
        kt = k2.T
        for e in range(2):
            other = 64 * (1 - e)
            mine = (lane >= 64) == (e == 1)
            ka = jnp.where(mine, k2, jnp.where(lane == other, bar, zero))
            va = jnp.where(mine, v2, zero)
            qa = jnp.where(lane == other, one, q2)
            lse_row = lse_ref[pl.ds(sl * 16 + 2*j + e, 1), :]
            for c in range(LMAX // QC):
                cs = slice(c*QC, (c+1)*QC)
                s = mm(ka, qa[cs], NT)
                p = jnp.exp(s - lse_row[:, cs])
                dp = mm(va, do2[cs], NT)
                pd = p * dp
                dsum = jnp.sum(pd, axis=0, keepdims=True)
                ds = (pd - p * dsum).astype(BF16)
                dvc = mm(p.astype(BF16), do2[cs])
                dkc = mm(ds, q2[cs])
                if c == 0:
                    dva, dka = dvc, dkc
                else:
                    dva, dka = dva + dvc, dka + dkc
                dqt_s[64*e:64*e+64, cs] = mm(kt[64*e:64*e+64], ds)
            if e == 0:
                accv[...] = dva; acck[...] = dka
            else:
                dv_s[rs, ls] = jnp.where(mine, dva, accv[...]).astype(BF16)
                dk_s[rs, ls] = jnp.where(mine, dka, acck[...]).astype(BF16)
        dq_s[rs, ls] = (dqt_s[...].T * 0.125).astype(BF16)
        return 0
    lax.fori_loop(0, S * (HEADS // 2), task, 0)
    small_ref[...] = jnp.zeros_like(small_ref)
    small_ref[0:1, :] = jnp.sum(dq_s[...].astype(F32), axis=0, keepdims=True)
    small_ref[1:2, :] = jnp.sum(dv_s[...].astype(F32), axis=0, keepdims=True)
    def rows(r, _):
        rr = pl.ds(pl.multiple_of(r * 256, 256), 256)
        dx_ref[rr, :] = dz_ref[rr, :] + mm(dq_s[rr, :], wq_ref[...], NT) + mm(dk_s[rr, :], wk_ref[...], NT) + mm(dv_s[rr, :], wv_ref[...], NT)
        return 0
    lax.fori_loop(0, S * LMAX // 256, rows, 0)
    for i, g in enumerate((dq_s, dk_s, dv_s)):
        def wg(r, _, g=g, i=i):
            rr = pl.ds(pl.multiple_of(r * 256, 256), 256)
            dw_ref[rr, i*D:(i+1)*D] = mm(xt_s[rr, :], g[...]).astype(BF16)
            return 0
        lax.fori_loop(0, D // 256, wg, 0)

def attend_bwd(q, k, v, do, lse, tokens, dz, wa, lens):
    T = tokens.shape[0]
    V = pl.BlockSpec(memory_space=pltpu.VMEM)
    w = lambda i: pl.BlockSpec((D, D), lambda s, l, i=i: (0, i))
    full = lambda a: pl.BlockSpec(a.shape, lambda s, l: (0, 0))
    o = lambda sh: pl.BlockSpec(sh, lambda s, l: (0, 0))
    return pl.pallas_call(
        attend_bwd_kernel,
        out_shape=[jax.ShapeDtypeStruct((T, D), F32), jax.ShapeDtypeStruct((D, 3*D), BF16), jax.ShapeDtypeStruct((8, D), F32)],
        grid_spec=pltpu.PrefetchScalarGridSpec(num_scalar_prefetch=1, grid=(1,),
            in_specs=[full(q)]*4 + [full(lse), full(tokens), full(dz), w(0), w(1), w(2)],
            out_specs=[o((T, D)), o((D, 3*D)), o((8, D))],
            scratch_shapes=[pltpu.VMEM((T, D), BF16)]*3 + [pltpu.VMEM((D, T), BF16), pltpu.VMEM((128, LMAX), F32), pltpu.VMEM((LMAX, 128), F32), pltpu.VMEM((LMAX, 128), F32), pltpu.VMEM((8, 128), F32)]),
        name="attend_bwd",
    )(lens, q, k, v, do, lse, tokens, dz, wa, wa, wa)


M = 256
NB = 768


def gelu_pair(u):
    phi = 0.5 * (1.0 + lax.erf(u * 0.7071067811865476))
    e = jnp.exp(-0.5 * (u * u))
    return u * phi, phi + u * (e * 0.3989422804014327)

def norm_stats(z):
    mean = jnp.mean(z, axis=-1, keepdims=True)
    c = z - mean
    var = jnp.mean(c * c, axis=-1, keepdims=True)
    r = lax.rsqrt(var + 1e-5)
    return c * r, r

def norm_back(dxh, xh, r):
    return r * (dxh - jnp.mean(dxh, axis=-1, keepdims=True) - xh * jnp.mean(dxh * xh, axis=-1, keepdims=True))

def colsum(x):
    return jnp.sum(x, axis=0, keepdims=True)

def ffn_kernel(tiles, lens_ref, o_ref, tok_ref, cot_ref, wa_h, wf_h, vec_ref, b1_ref,
               out_ref, dz_ref, do_ref, gf_ref, small_ref,
               wo_ref, w1_ref, w2_ref, gp_s, ot_s, da_s, ht_s, dft_s, g_s, du_s, sem):
    t = pl.program_id(0); per = LMAX // M
    live = [(lens_ref[u // per] > (u % per) * M).astype(jnp.int32) for u in range(tiles)]
    count = sum(live)
    loads = [pltpu.make_async_copy(wa_h.at[:, 3*D:4*D], wo_ref, sem.at[0]), pltpu.make_async_copy(wf_h.at[:, 0:FF], w1_ref, sem.at[1]), pltpu.make_async_copy(wf_h.at[:, FF:2*FF], w2_ref, sem.at[2])]
    def arrived(i):
        @pl.when(t == 0)
        def _(): loads[i].wait()

    @pl.when(t == 0)
    def _():
        for l in loads: l.start()
        small_ref[...] = jnp.zeros_like(small_ref)

    n = lens_ref[jnp.minimum(t, tiles - 1) // per] - (t % per) * M

    @pl.when((t < tiles) & (n <= 0))
    def _():
        for r in (out_ref, dz_ref, do_ref):
            r[...] = jnp.zeros_like(r)

    @pl.when((t < tiles) & (n > 0))
    def _():
        pos = sum(live[u] * (u < t).astype(jnp.int32) for u in range(tiles))
        rs = pl.ds(pl.multiple_of(pos * M, M), M)
        v = lambda i: vec_ref[i:i+1, :]
        o = o_ref[...]
        arrived(0)
        z1 = tok_ref[...].astype(F32) + (mm(o, wo_ref[...]) + v(2))
        ot_s[:, rs] = o.T
        xh1, r1 = norm_stats(z1)
        h = xh1 * v(3) + v(4)
        hb = h.astype(BF16)
        ht_s[:, rs] = hb.T
        arrived(1)
        arrived(2)
        f = None
        CF = 512
        cuts = [slice(c, c + CF) for c in range(0, FF, CF)]
        u = mm(hb, w1_ref[:, cuts[0]]) + b1_ref[:, cuts[0]]
        for j, cs in enumerate(cuts):
            nxt = mm(hb, w1_ref[:, cuts[j+1]]) + b1_ref[:, cuts[j+1]] if j + 1 < len(cuts) else None
            g, gp = gelu_pair(u)
            gb = g.astype(BF16)
            g_s[rs, cs] = gb
            gp_s[:, cs] = gp
            part = mm(gb, w2_ref[:, cs], NT)
            f = part if f is None else f + part
            u = nxt
        z2 = h + (f + v(5))
        xh2, r2 = norm_stats(z2)
        keep = lax.broadcasted_iota(jnp.int32, (M, 1), 0) < n
        out_ref[...] = jnp.where(keep, xh2 * v(6) + v(7), 0.0).astype(BF16)
        dy = jnp.where(keep, cot_ref[...].astype(F32), 0.0)
        small_ref[7:8, :] += colsum(dy)
        small_ref[6:7, :] += colsum(dy * xh2)
        dz2 = norm_back(dy * v(6), xh2, r2)
        df = dz2.astype(BF16)
        dft_s[:, rs] = df.T
        small_ref[5:6, :] += colsum(df.astype(F32))
        du = (gp_s[...] * mm(df, w2_ref[...])).astype(BF16)
        du_s[rs, :] = du
        db1 = colsum(du.astype(F32))
        for i in range(4):
            small_ref[8+i:9+i, :] += db1[:, i*D:(i+1)*D]
        dh = dz2 + mm(du, w1_ref[...], NT)
        small_ref[4:5, :] += colsum(dh)
        small_ref[3:4, :] += colsum(dh * xh1)
        dz1 = norm_back(dh * v(3), xh1, r1)
        da = dz1.astype(BF16)
        small_ref[2:3, :] += colsum(da.astype(F32))
        dz_ref[...] = dz1
        da_s[rs, :] = da
        do_ref[...] = mm(da, wo_ref[...], NT).astype(BF16)

    i = t - tiles
    half = FF // NB
    for kk in range(1, tiles + 1):
        K = kk*M
        for lt, r, c0, n0, n1 in ((ht_s, du_s, 0, 0, half), (dft_s, g_s, half, half, 2*half), (ot_s, da_s, 2*half, 2*half, 2*half + 1)):
            @pl.when((count == kk) & (i >= n0) & (i < n1))
            def _(lt=lt, r=r, K=K, c0=c0):
                cs = pl.ds(pl.multiple_of((i - c0) * NB, NB), NB)
                gf_ref[...] = mm(lt[:, :K], r[:K, cs]).astype(BF16)

def ffn(o, tokens, cot, wa, wf, vec8, b1, lens):
    T = tokens.shape[0]; tiles = T // M; chunks = 2*FF // NB + 1
    row = pl.BlockSpec((M, D), lambda t, l: (jnp.minimum(t, tiles - 1), 0))
    one = lambda sh: pl.BlockSpec(sh, lambda t, l: (0, 0))
    A = pl.BlockSpec(memory_space=pl.ANY)
    S = jax.ShapeDtypeStruct
    B = lambda *sh: pltpu.VMEM(sh, BF16)
    return pl.pallas_call(
        functools.partial(ffn_kernel, tiles),
        out_shape=[S((T, D), BF16), S((T, D), F32), S((T, D), BF16), S((D, chunks*NB), BF16), S((16, D), F32)],
        grid_spec=pltpu.PrefetchScalarGridSpec(num_scalar_prefetch=1, grid=(tiles + chunks,),
            in_specs=[row, row, row, A, A, one((8, D)), one((1, FF))],
            out_specs=[row, row, row, pl.BlockSpec((D, NB), lambda t, l: (0, jnp.maximum(t - tiles, 0))), one((16, D))],
            scratch_shapes=[B(D, D), B(D, FF), B(D, FF), pltpu.VMEM((M, FF), F32), B(D, T), B(T, D), B(D, T), B(D, T), B(T, FF), B(T, FF), pltpu.SemaphoreType.DMA((3,))]),
        compiler_params=pltpu.CompilerParams(vmem_limit_bytes=60 << 20),
        name="ffn",
    )(lens, o, tokens, cot, wa, wf, vec8, b1)


RATE = 1.0

class Spot:
    def __init__(self, na, ndp):
        self.na, self.ndp = na, ndp
        self.me = lax.axis_index("fsdp"); self.p = lax.axis_index("dp")
        self.a = self.me // 4; self.b = (self.me // 2) % 2; self.c = self.me % 2
        self.par = self.p % 2
        self.b2 = self.b + (1 - 2*self.b)*(1 - self.par); self.c2 = self.c + (1 - 2*self.c)*self.par
        self.b3 = self.b + (1 - 2*self.b)*self.par; self.c3 = self.c + (1 - 2*self.c)*(1 - self.par)

    def at(self, a, flip2=0, flip3=0):
        if flip2 and flip3:
            b, c = 1 - self.b, 1 - self.c
        elif flip2:
            b, c = self.b2, self.c2
        elif flip3:
            b, c = self.b3, self.c3
        else:
            b, c = self.b, self.c
        return (a*2 + b)*2 + c

    def dev(self, a, flip2=0, flip3=0):
        return (self.at(a, flip2, flip3), self.p)

    def barrier(self):
        sem = pltpu.get_barrier_semaphore()
        up, down = self.a < self.na - 1, self.a > 0
        def sig(dev):
            pl.semaphore_signal(sem, inc=1, device_id=dev, device_id_type=MESH)
        @pl.when(up)
        def _(): sig(self.dev(self.a + 1))
        @pl.when(down)
        def _(): sig(self.dev(self.a - 1))
        sig(self.dev(self.a, 1, 0)); sig(self.dev(self.a, 0, 1))
        for q in range(1, self.ndp): sig((self.me, (self.p + q) % self.ndp))
        pl.semaphore_wait(sem, 1 + self.ndp + up.astype(jnp.int32) + down.astype(jnp.int32))

class Gather:
    def __init__(self, spot, own, view, ssem, rsem, dp_view=None):
        self.s, self.own, self.view, self.ss, self.rs, self.dp_view = spot, own, view, ssem, rsem, dp_view
        na = spot.na
        self.JU, self.JD = 0, na - 1
        self.J2 = 2*(na - 1); self.J3 = self.J2 + na; self.JP = self.J3 + 2*na
        self.log = []

    @staticmethod
    def slots(na, ndp):
        return 2*(na - 1) + na + 2*na + (ndp - 1)*4*na

    def copy(self, f, dev, j, r=None, src=None):
        v = self.view(f)
        return pltpu.make_async_remote_copy(src_ref=v if src is None else src, dst_ref=v, send_sem=self.ss.at[j],
                                            recv_sem=self.rs.at[j if r is None else r], device_id=dev, device_id_type=MESH)

    def send(self, cond, make):
        make().start()
        self.log.append((cond, make))

    def wait(self, f, j):
        self.copy(f, (self.s.me, self.s.p), j).wait_recv()

    def dp(self, cond, f):
        if self.dp_view is None: return
        s = self.s
        for q in range(1, s.ndp):
            self.send(cond, lambda q=q: self.copy(f(), (s.me, (s.p + q) % s.ndp), self.JP + (q-1)*4*s.na + f()))

    def start(self):
        s = self.s; na = s.na
        up, down = s.a < na - 1, s.a > 0
        @pl.when(up)
        def _(): self.send(up, lambda: self.copy(s.me, s.dev(s.a + 1), self.JU, src=self.own))
        @pl.when(down)
        def _(): self.send(down, lambda: self.copy(s.me, s.dev(s.a - 1), self.JD, src=self.own))
        self.send(None, lambda: self.copy(s.me, s.dev(s.a, 1, 0), self.J2 + s.a, src=self.own))
        self.send(None, lambda: self.copy(s.me, s.dev(s.a, 0, 1), self.J3 + s.a*2, src=self.own))

    def events(self):
        s = self.s; na = s.na
        def chain(up, k):
            a = s.a - 1 - k if up else s.a + 1 + k
            cond = a >= 0 if up else a < na
            fwd = s.a < na - 1 if up else s.a > 0
            both = cond & fwd
            j = (self.JU if up else self.JD) + k
            def go():
                self.wait(s.at(a), j)
                if k < na - 2:
                    @pl.when(fwd)
                    def _(): self.send(both, lambda: self.copy(s.at(a), s.dev(s.a + 1 if up else s.a - 1), j + 1))
                self.send(cond, lambda: self.copy(s.at(a), s.dev(s.a, 1, 0), self.J2 + a))
                self.send(cond, lambda: self.copy(s.at(a), s.dev(s.a, 0, 1), self.J3 + a*2))
                self.dp(cond, lambda: s.at(a))
            return cond, go
        def second(a, cond):
            def go():
                self.wait(s.at(a, 1, 0), self.J2 + a)
                self.send(cond, lambda: self.copy(s.at(a, 1, 0), s.dev(s.a, 0, 1), self.J3 + a*2 + 1))
                self.dp(cond, lambda: s.at(a, 1, 0))
            return cond, go
        def third(a, cond, x):
            def go():
                self.wait(s.at(a, x, 1), self.J3 + a*2 + x)
                self.dp(cond, lambda: s.at(a, x, 1))
            return cond, go
        levels = [[(s.a, None)]]
        for k in range(na - 1):
            levels.append([(s.a - 1 - k, s.a - 1 - k >= 0), (s.a + 1 + k, s.a + 1 + k < na)])
        out = []
        for k in range(na + 2):
            if k < na - 1: out += [chain(True, k), chain(False, k)]
            if k < na:
                out += [second(a, cd) for a, cd in levels[k]]
                out += [third(a, cd, 0) for a, cd in levels[k]]
            if 0 < k <= na:
                out += [third(a, cd, 1) for a, cd in levels[k-1]]
        return out

    def finish(self):
        s = self.s
        if self.dp_view is not None:
            for q in range(1, s.ndp):
                def body(f, _):
                    @pl.when(f != s.me)
                    def _():
                        j = self.JP + (q-1)*4*s.na + f
                        v = self.dp_view(f, (s.p + s.ndp - q) % s.ndp)
                        pltpu.make_async_remote_copy(src_ref=v, dst_ref=v, send_sem=self.ss.at[j], recv_sem=self.rs.at[j], device_id=(s.me, s.p), device_id_type=MESH).wait_recv()
                    return 0
                lax.fori_loop(0, 4*s.na, body, 0)
        self.drain()

    def drain(self):
        for cond, make in self.log:
            if cond is None:
                make().wait_send()
            else:
                @pl.when(cond)
                def _(): make().wait_send()

def run_event(ev):
    cond, go = ev
    if cond is None: go()
    else: pl.when(cond)(go)

def forward_kernel(na, ndp, wa_sh, wf_h, vecs, bff, lens_ref, tok_h,
                   wa_out, wf_out, vec8, bias, q_h, k_h, v_h, o_h, lse_ref,
                   wa_c, wf_c, ex, wqkv, ot_s, wf_sh, tok_ref, q_ref, k_ref, v_ref, o_ref, lsem, *sems):
    s = Spot(na, ndp)
    R = wa_sh.shape[0]
    loads = [pltpu.make_async_copy(wf_h, wf_sh, lsem.at[3]), pltpu.make_async_copy(tok_h, tok_ref, lsem.at[4])]
    for l in loads: l.start()
    ex[s.me, 0:8, 0:R] = vecs[...].astype(BF16).astype(F32)
    for j in range(4):
        ex[s.me, 8+j:9+j, 0:R] = bff[0:1, j*R:(j+1)*R].astype(BF16).astype(F32)
    wa_c[...] = wa_sh[...].astype(BF16)
    gs = []
    for i, (c, out) in enumerate(((wa_c, wa_out), (wf_c, wf_out))):
        w = c.shape[1] // ndp
        cols = lambda q, w=w: pl.ds(pl.multiple_of(q*w, 128), w)
        gs.append(Gather(s, c.at[:, cols(s.p)], lambda f, out=out, cols=cols: out.at[f, :, cols(s.p)], sems[2*i], sems[2*i+1],
                         lambda f, q, out=out, cols=cols: out.at[f, :, cols(q)]))
    gx = Gather(s, ex.at[s.me], lambda f: ex.at[f], sems[4], sems[5])
    ga, gf = gs
    s.barrier()
    gx.start(); ga.start()
    locs = [pltpu.make_async_copy(wa_c, wa_out.at[s.me], lsem.at[0])]
    locs[0].start()
    loads[0].wait()
    wf_c[...] = wf_sh[...].astype(BF16)
    locs.append(pltpu.make_async_copy(wf_c, wf_out.at[s.me], lsem.at[1]))
    locs[1].start()
    ea, exv, ef = ga.events(), gx.events(), gf.events()
    gf.start()
    for u, v in zip(ea, exv):
        run_event(v); run_event(u)
    for q in range(1, ndp):
        def body(f, _, q=q):
            @pl.when(f != s.me)
            def _():
                j = ga.JP + (q-1)*4*na + f
                v = ga.dp_view(f, (s.p + ndp - q) % ndp)
                pltpu.make_async_remote_copy(src_ref=v, dst_ref=v, send_sem=ga.ss.at[j], recv_sem=ga.rs.at[j], device_id=(s.me, s.p), device_id_type=MESH).wait_recv()
            return 0
        lax.fori_loop(0, 4*na, body, 0)
    locs[0].wait()
    load = pltpu.make_async_copy(wa_out.at[:, :, 0:3*D], wqkv, lsem.at[2])
    load.start()
    for f in range(4*na):
        vec8[:, f*R:(f+1)*R] = ex[f, 0:8, 0:R]
        for j in range(4):
            bias[0:1, (f*4+j)*R:(f*4+j+1)*R] = ex[f, 8+j:9+j, 0:R]
    load.wait()
    loads[1].wait()
    S = tok_ref.shape[0] // LMAX
    lane = lax.broadcasted_iota(jnp.int32, (LMAX, 128), 1)
    row = lax.broadcasted_iota(jnp.int32, (LMAX, 128), 0)
    one = jnp.ones((LMAX, 128), BF16); zero = jnp.zeros((LMAX, 128), BF16)
    PAIRS = HEADS // 2
    ntask = S*(3 + PAIRS)
    cut = [min(len(ef), int(RATE*t)) for t in range(ntask + 1)]
    def events_after(i, first, last):
        for t in range(first, last):
            evs = ef[cut[t]:cut[t+1]]
            if evs:
                @pl.when(i == t)
                def _():
                    for e in evs: run_event(e)
    w3 = wqkv.shape
    def proj(sl, which):
        rs = pl.ds(pl.multiple_of(sl*LMAX, LMAX), LMAX)
        x = tok_ref[rs, :]
        y = mm(x, wqkv[:, :, which*D:(which+1)*D].reshape(4*na*R, D))
        if which == 0: q_ref[rs, :] = ((y + vec8[0:1, :]).astype(BF16) * 0.125).astype(BF16)
        elif which == 1: k_ref[rs, :] = y.astype(BF16)
        else: v_ref[rs, :] = (y + vec8[1:2, :]).astype(BF16)
    def step1(i, _):
        for which in range(3):
            @pl.when(i % 3 == which)
            def _(): proj(i // 3, which)
        events_after(i, 0, 3*S)
        return 0
    lax.fori_loop(0, 3*S, step1, 0)
    stores = [pltpu.make_async_copy(r, h, lsem.at[5 + i]) for i, (r, h) in enumerate(((q_ref, q_h), (k_ref, k_h), (v_ref, v_h), (o_ref, o_h)))]
    for c in stores[:3]: c.start()
    def step2(i, _):
        sl = i // PAIRS; j = i % PAIRS
        rs = pl.ds(pl.multiple_of(sl*LMAX, LMAX), LMAX)
        ls = pl.ds(pl.multiple_of(j * 128, 128), 128)
        bar = jnp.where(row < lens_ref[sl], 0.0, -1e30).astype(BF16)
        q2 = q_ref[rs, ls]; k2 = k_ref[rs, ls]
        vt = v_ref[rs, ls].T
        raw = []
        for e in range(2):
            other = 64 * (1 - e)
            ka = jnp.where((lane >= 64) == (e == 1), k2, jnp.where(lane == other, bar, zero))
            qa = jnp.where(lane == other, one, q2)
            raw.append(mm(ka, qa, NT))
        for e in range(2):
            top = jnp.max(raw[e], axis=0, keepdims=True)
            p = jnp.exp(raw[e] - top)
            tot = jnp.sum(p, axis=0, keepdims=True)
            ot_s[64*e:64*e+64, :] = mm(vt[64*e:64*e+64], p.astype(BF16)) / tot
            lse_ref[pl.ds(sl*16 + 2*j + e, 1), :] = top + jnp.log(tot)
        o_ref[rs, ls] = ot_s[...].T.astype(BF16)
        events_after(i + 3*S, 3*S, ntask)
        return 0
    lax.fori_loop(0, S*PAIRS, step2, 0)
    stores[3].start()
    for e in ef[cut[ntask]:]: run_event(e)
    gf.finish(); gx.finish()
    for c in stores: c.wait()
    ga.drain()
    locs[1].wait()

def forward(mesh_shape, wa_sh, wf_sh, vecs, bff, lens, tokens, cid):
    F, ndp = mesh_shape
    na = F // 4; R = vecs.shape[1]; T = tokens.shape[0]
    NS = Gather.slots(na, ndp)
    S = jax.ShapeDtypeStruct
    V = pl.BlockSpec(memory_space=pltpu.VMEM); A = pl.BlockSpec(memory_space=pl.ANY)
    DMA = pltpu.SemaphoreType.DMA
    return pl.pallas_call(
        functools.partial(forward_kernel, na, ndp),
        out_shape=[S((F, R, 4*D), BF16), S((F, R, 2*FF), BF16), S((8, D), F32), S((1, FF), F32)] + [S((T, D), BF16)]*4 + [S((T//LMAX*16, LMAX), F32)],
        in_specs=[V, A, V, V, pl.BlockSpec(memory_space=pltpu.SMEM), A],
        out_specs=[A, A, V, V, A, A, A, A, V],
        scratch_shapes=[pltpu.VMEM((R, 4*D), BF16), pltpu.VMEM((R, 2*FF), BF16), pltpu.VMEM((F, 16, 128), F32), pltpu.VMEM((F, R, 3*D), BF16),
                        pltpu.VMEM((128, LMAX), F32), pltpu.VMEM((R, 2*FF), F32)] + [pltpu.VMEM((T, D), BF16)]*5 + [DMA((9,))] + [DMA((NS,))]*6,
        compiler_params=pltpu.CompilerParams(collective_id=cid, has_side_effects=True, vmem_limit_bytes=56 << 20),
        name="gather_attend",
    )(wa_sh, wf_sh, vecs, bff, lens, tokens)


def as_int(cond):
    return cond.astype(jnp.int32)

class Reduce:
    def __init__(self, spot, src, mine, rd, r3, r2, cu, cd, ss, rs, out, load=None):
        self.s = spot
        self.src, self.mine = src, mine
        self.rd, self.r3, self.r2, self.cu, self.cd = rd, r3, r2, cu, cd
        self.ss, self.rs, self.out, self.load = ss, rs, out, load
        s = spot; na = s.na; F = 4*na
        self.B3 = (s.ndp - 1)*F; self.B2 = self.B3 + 2*na; self.BU = self.B2 + na; self.BD = self.BU + na; self.BO = self.BD + na
        self.log = []
        z = s.a; lower = as_int(z < na // 2)
        self.order = []
        for k in range(na):
            c1 = as_int(k < na - 1 - z); c2 = as_int(k < z)
            lo = c1*(na - 1 - k) + (1 - c1)*(k - (na - 1 - z))
            hi = c2*k + (1 - c2)*(na - 1 - (k - z))
            self.order.append(lower*lo + (1 - lower)*hi)
        self.bit2 = s.b*(1 - s.par) + s.c*s.par

    @staticmethod
    def slots(na, ndp):
        return (ndp - 1)*4*na + 5*na + ndp - 1

    def rc(self, src, dst, j, r, dev):
        return pltpu.make_async_remote_copy(src_ref=src, dst_ref=dst, send_sem=self.ss.at[j], recv_sem=self.rs.at[r], device_id=dev, device_id_type=MESH)

    def send(self, cond, make):
        make().start()
        self.log.append((cond, make))

    def wait(self, dst, r):
        self.rc(dst, dst, r, r, (self.s.me, self.s.p)).wait_recv()

    def start(self):
        s = self.s; na = s.na
        if self.load is not None:
            for y3, y2 in ((1, 1), (1, 0), (0, 1), (0, 0)):
                for k in range(na): self.load(s.at(self.order[k], y2, y3)).start()
        for y3, y2 in ((1, 1), (1, 0), (0, 1), (0, 0)):
            for k in range(na):
                for q in range(1, s.ndp):
                    x2, x3 = (y2, y3) if q % 2 == 0 else (y3, y2)
                    f = s.at(self.order[k], x2, x3)
                    dq = (s.p + q) % s.ndp
                    self.send(None, lambda f=f, q=q, dq=dq: self.rc(self.src(f, dq), self.rd.at[q-1, f], (q-1)*4*na + f, (q-1)*4*na + f, (s.me, dq)))

    def add(self, f, srcs, dst=None):
        s = self.s
        for q in range(1, s.ndp):
            self.wait(self.rd.at[q-1, f], (q-1)*4*s.na + f)
        if self.load is not None: self.load(f).wait()
        own = self.mine(f)
        dst = own if dst is None else dst
        srcs = [self.rd.at[q-1, f] for q in range(1, s.ndp)] + srcs
        w = own.shape[-1]
        CH = next(c for c in (512, 384, 256, 128) if w % c == 0)
        def body(j, _):
            cs = pl.ds(pl.multiple_of(j*CH, 128), CH)
            v = own[:, cs].astype(F32)
            for r in srcs: v = v + r[:, cs].astype(F32)
            dst[:, cs] = v.astype(dst.dtype)
            return 0
        lax.fori_loop(0, w // CH, body, 0)

    def events(self):
        s = self.s; na = s.na
        out = []
        for x2 in (1, 0):
            for k in range(na):
                def go(x2=x2, k=k):
                    a = self.order[k]; f = lambda: s.at(a, x2, 1)
                    slot = lambda: a*2 + self.bit2 + (1 - 2*self.bit2)*x2
                    self.add(f(), [])
                    self.send(None, lambda: self.rc(self.mine(f()), self.r3.at[slot()], self.B3 + slot(), self.B3 + slot(), s.dev(s.a, 0, 1)))
                out.append((None, go))
        for k in range(na):
            def go(k=k):
                a = self.order[k]; f = lambda: s.at(a, 1, 0)
                slot = a*2 + 1 - self.bit2
                self.wait(self.r3.at[slot], self.B3 + slot)
                self.add(f(), [self.r3.at[slot]])
                self.send(None, lambda: self.rc(self.mine(f()), self.r2.at[a], self.B2 + a, self.B2 + a, s.dev(s.a, 1, 0)))
            out.append((None, go))
        for k in range(na - 1, 0, -1):
            for up in (True, False):
                a = s.a + k if up else s.a - k
                cond = a < na if up else a >= 0
                more = s.a > 0 if up else s.a < na - 1
                buf, B = (self.cu, self.BU) if up else (self.cd, self.BD)
                def go(a=a, cond=cond, more=more, buf=buf, B=B, up=up):
                    slot = a*2 + self.bit2
                    f = lambda: s.at(a)
                    self.wait(self.r3.at[slot], self.B3 + slot)
                    self.wait(self.r2.at[a], self.B2 + a)
                    base = [self.r3.at[slot], self.r2.at[a]]
                    @pl.when(more)
                    def _():
                        self.wait(buf.at[a], B + a)
                        self.add(f(), base + [buf.at[a]])
                    @pl.when(jnp.logical_not(more))
                    def _(): self.add(f(), base)
                    self.send(cond, lambda: self.rc(self.mine(f()), buf.at[a], B + a, B + a, s.dev(s.a + 1 if up else s.a - 1)))
                out.append((cond, go))
        def last():
            a = s.a; slot = a*2 + self.bit2
            self.wait(self.r3.at[slot], self.B3 + slot)
            self.wait(self.r2.at[a], self.B2 + a)
            base = [self.r3.at[slot], self.r2.at[a]]
            dst = self.out(s.p)
            @pl.when(a == 0)
            def _():
                self.wait(self.cd.at[a], self.BD + a)
                self.add(s.me, base + [self.cd.at[a]], dst)
            @pl.when(a == na - 1)
            def _():
                self.wait(self.cu.at[a], self.BU + a)
                self.add(s.me, base + [self.cu.at[a]], dst)
            @pl.when((a > 0) & (a < na - 1))
            def _():
                self.wait(self.cd.at[a], self.BD + a)
                self.wait(self.cu.at[a], self.BU + a)
                self.add(s.me, base + [self.cd.at[a], self.cu.at[a]], dst)
            for q in range(1, s.ndp):
                self.send(None, lambda q=q: self.rc(self.out(s.p), self.out(s.p), self.BO + q - 1, self.BO + q - 1, (s.me, (s.p + q) % s.ndp)))
        out.append((None, last))
        return out

    def finish(self):
        s = self.s
        for q in range(1, s.ndp):
            self.wait(self.out((s.p + s.ndp - q) % s.ndp), self.BO + q - 1)
        for cond, make in self.log:
            if cond is None: make().wait_send()
            else:
                @pl.when(cond)
                def _(): make().wait_send()

    @staticmethod
    def scratch(na, ndp, R, w):
        F = 4*na
        B = lambda *sh: pltpu.VMEM(sh + (R, w), BF16)
        NS = Reduce.slots(na, ndp)
        return [B(ndp - 1, F), B(2*na), B(na), B(na), B(na), pltpu.SemaphoreType.DMA((NS,)), pltpu.SemaphoreType.DMA((NS,))]

class SmallSum:
    def __init__(self, spot, buf, got, ss, rs):
        self.s, self.buf, self.got, self.ss, self.rs = spot, buf, got, ss, rs
        self.sent = []

    @staticmethod
    def scratch(na, ndp, shape):
        NX = ndp + 1 + na - 1
        return [pltpu.VMEM((4,) + shape, F32), pltpu.VMEM((NX,) + shape, F32), pltpu.SemaphoreType.DMA((NX,)), pltpu.SemaphoreType.DMA((NX,))]

    def go(self, i, j, dev):
        d = pltpu.make_async_remote_copy(src_ref=self.buf.at[i], dst_ref=self.got.at[j], send_sem=self.ss.at[j], recv_sem=self.rs.at[j], device_id=dev, device_id_type=MESH)
        d.start(); self.sent.append(d)

    def wait(self, j):
        pltpu.make_async_remote_copy(src_ref=self.got.at[j], dst_ref=self.got.at[j], send_sem=self.ss.at[j], recv_sem=self.rs.at[j], device_id=(self.s.me, self.s.p), device_id_type=MESH).wait_recv()

    def ordered(self, i, here, n, j0):
        def pick(m):
            v = self.buf[i]
            for q in range(1, n):
                v = jnp.where((here + n - q) % n == m, self.got[j0 + q - 1], v)
            return v
        v = pick(0)
        for m in range(1, n): v = v + pick(m)
        return v

    def start(self):
        s = self.s
        for q in range(1, s.ndp): self.go(0, q - 1, (s.me, (s.p + q) % s.ndp))

    def steps(self, out):
        s = self.s; X = s.ndp - 1
        def one():
            for q in range(1, s.ndp): self.wait(q - 1)
            self.buf[1] = self.ordered(0, s.p, s.ndp, 0)
            self.go(1, X, ((s.a*2 + s.b)*2 + 1 - s.c, s.p))
        def two():
            self.wait(X)
            self.buf[2] = self.buf[1] + self.got[X]
            self.go(2, X + 1, ((s.a*2 + 1 - s.b)*2 + s.c, s.p))
        def three():
            self.wait(X + 1)
            self.buf[3] = self.buf[2] + self.got[X + 1]
            for k in range(1, s.na): self.go(3, X + 1 + k, s.dev((s.a + k) % s.na))
        def four():
            for k in range(1, s.na): self.wait(X + 1 + k)
            out[...] = self.ordered(3, s.a, s.na, X + 2)
        return [one, two, three, four]

    def finish(self):
        for d in self.sent: d.wait_send()

def barrier_full(s):
    sem = pltpu.get_barrier_semaphore()
    def sig(dev): pl.semaphore_signal(sem, inc=1, device_id=dev, device_id_type=MESH)
    for k in range(1, s.na): sig(s.dev((s.a + k) % s.na))
    sig(s.dev(s.a, 1, 0)); sig(s.dev(s.a, 0, 1))
    for q in range(1, s.ndp): sig((s.me, (s.p + q) % s.ndp))
    pl.semaphore_wait(sem, s.na + s.ndp)

def backward_kernel(na, ndp, lens_ref, q_h, k_h, v_h, do_h, lse_ref, tok_h, dz_h, wa_h, gf_h, small_in,
                    dx_h, of_ref, oq_ref, small_out,
                    q_ref, k_ref, v_ref, do_ref, tok_ref, wqkv, g_s, xt_s, dqt_s, wg, ownf, dx_ref, lsem, fsem, *sc):
    s = Spot(na, ndp)
    R = gf_h.shape[1]; T = tok_ref.shape[0]; S = T // LMAX
    PAIRS = HEADS // 2
    loads = []
    for i, (h, r) in enumerate(((q_h, q_ref), (k_h, k_ref), (v_h, v_ref), (do_h, do_ref))):
        loads.append(pltpu.make_async_copy(h, r, lsem.at[i]))
    late = [pltpu.make_async_copy(tok_h, tok_ref, lsem.at[4]), pltpu.make_async_copy(wa_h.at[:, :, 0:3*D], wqkv, lsem.at[5]), pltpu.make_async_copy(dz_h, dx_ref, lsem.at[6])]
    wf = gf_h.shape[2] // ndp; wq = wg.shape[2] // ndp
    def cols(q, w): return pl.ds(pl.multiple_of(q*w, 128), w)
    cf = lambda f: pltpu.make_async_copy(gf_h.at[f, :, cols(s.p, wf)], ownf.at[f], fsem.at[f])
    rf = Reduce(s, lambda f, q: gf_h.at[f, :, cols(q, wf)], lambda f: ownf.at[f], *sc[0:7], lambda q: of_ref.at[:, cols(q, wf)], cf)
    rq = Reduce(s, lambda f, q: wg.at[f, :, cols(q, wq)], lambda f: wg.at[f, :, cols(s.p, wq)], *sc[7:14], lambda q: oq_ref.at[:, cols(q, wq)])
    xs = SmallSum(s, *sc[14:18])
    barrier_full(s)
    rf.start()
    for l in loads + late: l.start()
    both = rf.events()
    ntask = S*PAIRS
    n3, n2 = 2*na, na
    plan = [[] for _ in range(ntask)]
    quick, half = max(1, ntask // 4), ntask // 2
    for i, e in enumerate(both[:n3 + n2]):
        t = i*quick // n3 if i < n3 else half + (i - n3)*(ntask - half) // n2
        plan[t].append(e)
    chain_f, last_f = both[n3 + n2:-1], both[-1]

    lane = lax.broadcasted_iota(jnp.int32, (LMAX, 128), 1)
    row = lax.broadcasted_iota(jnp.int32, (LMAX, 128), 0)
    one = jnp.ones((LMAX, 128), BF16); zero = jnp.zeros((LMAX, 128), BF16)
    for l in loads: l.wait()
    def task(t, _):
        sl = t // PAIRS; j = t % PAIRS
        rs = pl.ds(pl.multiple_of(sl * LMAX, LMAX), LMAX)
        ls = pl.ds(pl.multiple_of(j * 128, 128), 128)
        bar = jnp.where(row < lens_ref[sl], 0.0, -1e30).astype(BF16)
        q2 = q_ref[rs, ls]; k2 = k_ref[rs, ls]; v2 = v_ref[rs, ls]; do2 = do_ref[rs, ls]
        kt = k2.T
        raw, dps = [], []
        for e in range(2):
            other = 64 * (1 - e)
            mine = (lane >= 64) == (e == 1)
            ka = jnp.where(mine, k2, jnp.where(lane == other, bar, zero))
            va = jnp.where(mine, v2, zero)
            qa = jnp.where(lane == other, one, q2)
            raw.append(mm(ka, qa, NT)); dps.append(mm(va, do2, NT))
        dvs, dks = [], []
        for e in range(2):
            p = jnp.exp(raw[e] - lse_ref[pl.ds(sl * 16 + 2*j + e, 1), :])
            pd = p * dps[e]
            ds = (pd - p * jnp.sum(pd, axis=0, keepdims=True)).astype(BF16)
            dvs.append(mm(p.astype(BF16), do2)); dks.append(mm(ds, q2))
            dqt_s[64*e:64*e+64, :] = mm(kt[64*e:64*e+64], ds)
        g_s[rs, pl.ds(pl.multiple_of(2*D + j*128, 128), 128)] = jnp.where(lane >= 64, dvs[1], dvs[0]).astype(BF16)
        g_s[rs, pl.ds(pl.multiple_of(D + j*128, 128), 128)] = jnp.where(lane >= 64, dks[1], dks[0]).astype(BF16)
        g_s[rs, ls] = (dqt_s[...].T * 0.125).astype(BF16)
        for n in range(ntask):
            if plan[n]:
                @pl.when(t == n)
                def _():
                    for e in plan[n]: run_event(e)
        return 0
    lax.fori_loop(0, ntask, task, 0)
    late[0].wait()
    xt_s[...] = tok_ref[...].T
    if wg.shape[2] > 3*D: wg[:, :, 3*D:] = jnp.zeros(wg.shape[:2] + (wg.shape[2] - 3*D,), BF16)
    def wgr(r, _):
        cs = pl.ds(pl.multiple_of(r * 256, 256), 256)
        wg[:, :, cs] = mm(xt_s[...], g_s[:, cs]).reshape(4*na, R, 256).astype(BF16)
        return 0
    lax.fori_loop(0, 3*D // 256, wgr, 0)
    rq.start()
    xs.buf[0] = small_in[...]
    xs.buf[0, 0:1, :] = jnp.sum(g_s[:, 0:D].astype(F32), axis=0, keepdims=True)
    xs.buf[0, 1:2, :] = jnp.sum(g_s[:, 2*D:3*D].astype(F32), axis=0, keepdims=True)
    xs.start()
    eq = rq.events(); small = xs.steps(small_out)
    for e in eq[:n3]: run_event(e)
    late[1].wait(); late[2].wait()
    def rows(r):
        rr = slice(r*256, (r+1)*256)
        dx_ref[rr, :] += mm(g_s[rr, :], wqkv[...].reshape(D, 3*D), NT)
    steps = [lambda r=r: rows(r) for r in range(T // 256)]
    chain_q = eq[n3 + n2:-1]
    dx_out = pltpu.make_async_copy(dx_ref, dx_h, lsem.at[7])
    small[0]()
    for e in chain_f: run_event(e)
    small[1]()
    for f in steps[:1]: f()
    for e in eq[n3:n3 + n2]: run_event(e)
    small[2]()
    run_event(last_f)
    rest = steps[1:]
    gap = -(-len(chain_q) // (len(rest) + 1))
    for i in range(len(rest) + 1):
        for e in chain_q[i*gap:(i+1)*gap]: run_event(e)
        if i < len(rest): rest[i]()
        if i == len(rest) - 1: dx_out.start()
    small[3]()
    run_event(eq[-1])
    dx_out.wait()
    rf.finish(); rq.finish(); xs.finish()

def backward(mesh_shape, lens, q, k, v, do, lse, tokens, dz, wa3, gf, small, cid):
    F, ndp = mesh_shape
    na = F // 4; R = gf.shape[1]; T = tokens.shape[0]
    S = jax.ShapeDtypeStruct
    V = pl.BlockSpec(memory_space=pltpu.VMEM); A = pl.BlockSpec(memory_space=pl.ANY)
    up = lambda n: -(-n // (128*ndp)) * 128*ndp
    CQ = up(3*D)
    B = lambda *sh: pltpu.VMEM(sh, BF16)
    return pl.pallas_call(
        functools.partial(backward_kernel, na, ndp),
        out_shape=[S((T, D), F32), S((R, gf.shape[2]), F32), S((R, CQ), F32), S(small.shape, F32)],
        in_specs=[pl.BlockSpec(memory_space=pltpu.SMEM), A, A, A, A, V, A, A, A, A, V],
        out_specs=[A, V, V, V],
        scratch_shapes=[B(T, D)]*5 + [B(F, R, 3*D)] + [B(T, 3*D), B(D, T), pltpu.VMEM((128, LMAX), F32),
                        B(F, R, CQ), B(F, R, gf.shape[2]//ndp), pltpu.VMEM((T, D), F32), pltpu.SemaphoreType.DMA((8,)), pltpu.SemaphoreType.DMA((F,))]
                       + Reduce.scratch(na, ndp, R, gf.shape[2]//ndp) + Reduce.scratch(na, ndp, R, CQ//ndp)
                       + SmallSum.scratch(na, ndp, small.shape),
        compiler_params=pltpu.CompilerParams(collective_id=cid, has_side_effects=True, vmem_limit_bytes=60 << 20),
        name="reduce_attend",
    )(lens, q, k, v, do, lse, tokens, dz, wa3, gf, small)


STEPS = 4

def adam(g, m, v, w, fix1, fix2, rate):
    m_new = 0.9 * m + 0.1 * g
    v_new = 0.98 * v + 0.02 * g * g
    w_new = w - rate * ((m_new * fix1) / (jnp.sqrt(v_new * fix2) + 1e-06) + 0.01 * w)
    return m_new, v_new, w_new

def update_kernel(step_ref, rate_ref, gq_ref, go_ref, gf_ref, small_ref, dx_ref,
                  aw, am, av, fw, fm, fv, vw, vm, vv, bw, bm, bv, dxo, *outs):
    i = pl.program_id(0)
    count = jnp.full((8, 128), step_ref[0], jnp.int32).astype(F32)
    fix1 = (1.0 / (1.0 - jnp.exp(count * -0.10536051565782628)))[0:1, 0:1]
    fix2 = (1.0 / (1.0 - jnp.exp(count * -0.020202707317519466)))[0:1, 0:1]
    rate = rate_ref[0]

    def put(g, m, v, w, o):
        a, b, c = adam(g, m[...], v[...], w[...], fix1, fix2, rate)
        o[0][...] = g; o[1][...] = a; o[2][...] = b; o[3][...] = c; o[4][...] = c.astype(BF16)

    dxo[...] = dx_ref[...]
    put(gf_ref[...], fm, fv, fw, outs[5:10])
    cut = 3*D // (4*D // STEPS)
    @pl.when(i < cut)
    def _(): put(gq_ref[...], am, av, aw, outs[0:5])
    @pl.when(i >= cut)
    def _(): put(go_ref[...], am, av, aw, outs[0:5])

    @pl.when(i == 0)
    def _():
        R = vw.shape[1]
        f = lax.axis_index("fsdp")
        g = pltpu.roll(small_ref[0:8, :], lax.rem(D - f*R, D), 1)[:, 0:R]
        put(g, vm, vv, vw, outs[10:15])
        at = f*4*R
        x = pltpu.roll(small_ref[8:16, :], lax.rem(D - lax.rem(at, D), D), 1)
        here = lax.broadcasted_iota(jnp.int32, (8, D), 0) == at // D
        put(jnp.sum(jnp.where(here, x, 0.0), axis=0, keepdims=True)[:, 0:4*R], bm, bv, bw, outs[15:20])

def update(adam_step, learn_rate, gq, gall, small, dx, attn, ffn_, vecs, bff):
    R = vecs[0].shape[1]; T = dx.shape[0]
    ca, cf = 4*D // STEPS, 2*FF // STEPS
    cut = 3*D // ca
    blk = lambda w, fn=lambda i: i: pl.BlockSpec((R, w), lambda i, fn=fn: (0, fn(i)))
    one = lambda a: pl.BlockSpec(a.shape, lambda i: (0, 0))
    SM = pl.BlockSpec(memory_space=pltpu.SMEM)
    row = pl.BlockSpec((T // STEPS, D), lambda i: (i, 0))
    S = jax.ShapeDtypeStruct
    five = lambda sh: [S(sh, F32)]*4 + [S(sh, BF16)]
    tiny = lambda sh: [pl.BlockSpec(sh, lambda i: (0, 0))]*5
    return pl.pallas_call(
        update_kernel,
        grid=(STEPS,),
        out_shape=[S((T, D), F32)] + five((R, 4*D)) + five((R, 2*FF)) + five((8, R)) + five((1, 4*R)),
        in_specs=[SM, SM, blk(ca, lambda i: jnp.minimum(i, cut - 1)), blk(ca, lambda i: 2*FF // ca + jnp.maximum(i - cut, 0)), blk(cf), one(small), row]
                 + [blk(ca)]*3 + [blk(cf)]*3 + [one(v) for v in vecs] + [one(b) for b in bff],
        out_specs=[row] + [blk(ca)]*5 + [blk(cf)]*5 + tiny((8, R)) + tiny((1, 4*R)),
        name="update",
    )(adam_step, learn_rate, gq, gall, gall, small, dx, *attn, *ffn_, *vecs, *bff)


def local(mesh_shape, tokens, cotangent, lengths, adam_step, learn_rate, attn_w, attn_m, attn_v, ffn_w, ffn_m, ffn_v,
          vecs, vecs_m, vecs_v, b_ff, bff_m, bff_v):
    shards, rows = mesh_shape[0], vecs.shape[0]
    T = tokens.shape[0]
    attn_low, ffn_low, vec8, bias, q, k, v, o, lse = forward(
        mesh_shape, attn_w, ffn_w, vecs.T, b_ff.reshape(1, 4 * rows), lengths, tokens, 1)
    attn_low = attn_low.reshape(D, 4 * D)
    ffn_low = ffn_low.reshape(D, 2 * FF)
    outputs, dz1, do, grads, small_ffn = ffn(o, tokens, cotangent, attn_low, ffn_low, vec8, bias, lengths)
    grads = jnp.pad(grads, ((0, 0), (0, -grads.shape[1] % (128 * mesh_shape[1]))))
    input_grad, summed, summed_qkv, summed_small = backward(
        mesh_shape, lengths, q, k, v, do, lse, tokens, dz1, attn_low.reshape(shards, rows, 4 * D),
        grads.reshape(shards, rows, grads.shape[1]), small_ffn, 2)
    line = lambda x: x.reshape(1, 4 * rows)
    new = update(adam_step, learn_rate, summed_qkv, summed, summed_small, input_grad, (attn_w, attn_m, attn_v),
                 (ffn_w, ffn_m, ffn_v), (vecs.T, vecs_m.T, vecs_v.T), (line(b_ff), line(bff_m), line(bff_v)))
    return (outputs, new[0], *new[1:11], *[x.T for x in new[11:16]], *[x.reshape(4 * rows) for x in new[16:21]])


def solution(mesh):
    both, rows, whole = P(("fsdp", "dp")), P("fsdp"), P()
    return jax.shard_map(
        functools.partial(local, (mesh.shape["fsdp"], mesh.shape["dp"])),
        mesh=mesh,
        in_specs=(both, both, both, whole, whole) + (rows,) * 12,
        out_specs=(both, both) + (rows,) * 20,
        check_vma=False,
    )
```

```python
import functools

import jax
import jax.numpy as jnp
from jax import lax
from jax.experimental import pallas as pl
from jax.experimental.pallas import tpu as pltpu
from jax.sharding import PartitionSpec as P

MESH = pl.DeviceIdType.MESH

D = 768; HEADS = 12; HEAD = 64; FF = 3072; LMAX = 512
NN = (((1,), (0,)), ((), ()))
NT = (((1,), (1,)), ((), ()))
TN = (((0,), (0,)), ((), ()))
F32 = jnp.float32; BF16 = jnp.bfloat16
QC = 256

def mm(a, b, dims=NN):
    return lax.dot_general(a, b, dims, preferred_element_type=F32)

def attend_fwd_kernel(lens_ref, tok_ref, wq_ref, wk_ref, wv_ref, vec_ref, q_ref, k_ref, v_ref, o_ref, lse_ref, ot_ref):
    n = lens_ref[pl.program_id(0)]
    x = tok_ref[...]
    q_ref[...] = ((mm(x, wq_ref[...]) + vec_ref[0:1, :]).astype(BF16) * 0.125).astype(BF16)
    k_ref[...] = mm(x, wk_ref[...]).astype(BF16)
    v_ref[...] = (mm(x, wv_ref[...]) + vec_ref[1:2, :]).astype(BF16)
    lane = lax.broadcasted_iota(jnp.int32, (LMAX, 128), 1)
    row = lax.broadcasted_iota(jnp.int32, (LMAX, 128), 0)
    bar = jnp.where(row < n, 0.0, -1e30).astype(BF16)
    one = jnp.ones((LMAX, 128), BF16); zero = jnp.zeros((LMAX, 128), BF16)

    def pair(j, _):
        ls = pl.ds(pl.multiple_of(j * 128, 128), 128)
        q2 = q_ref[:, ls]; k2 = k_ref[:, ls]
        vt = v_ref[:, ls].T
        for e in range(2):
            other = 64 * (1 - e)
            ka = jnp.where((lane >= 64) == (e == 1), k2, jnp.where(lane == other, bar, zero))
            qa = jnp.where(lane == other, one, q2)
            for c in range(LMAX // QC):
                s = mm(ka, qa[c*QC:(c+1)*QC], NT)
                top = jnp.max(s, axis=0, keepdims=True)
                p = jnp.exp(s - top)
                tot = jnp.sum(p, axis=0, keepdims=True)
                o = mm(vt[64*e:64*e+64], p.astype(BF16))
                ot_ref[64*e:64*e+64, c*QC:(c+1)*QC] = o / tot
                lse_ref[pl.ds(2*j + e, 1), c*QC:(c+1)*QC] = top + jnp.log(tot)
        o_ref[:, ls] = ot_ref[...].T.astype(BF16)
        return 0
    lax.fori_loop(0, HEADS // 2, pair, 0)

def attend_fwd(tokens, wa, vec8, lens):
    S = tokens.shape[0] // LMAX
    row = pl.BlockSpec((LMAX, D), lambda s, l: (s, 0))
    w = lambda i: pl.BlockSpec((D, D), lambda s, l, i=i: (0, i))
    return pl.pallas_call(
        attend_fwd_kernel,
        out_shape=[jax.ShapeDtypeStruct((S*LMAX, D), BF16)]*4 + [jax.ShapeDtypeStruct((S*16, LMAX), F32)],
        grid_spec=pltpu.PrefetchScalarGridSpec(num_scalar_prefetch=1, grid=(S,),
            in_specs=[row, w(0), w(1), w(2), pl.BlockSpec((8, D), lambda s, l: (0, 0))],
            out_specs=[row]*4 + [pl.BlockSpec((16, LMAX), lambda s, l: (s, 0))],
            scratch_shapes=[pltpu.VMEM((128, LMAX), F32)]),
        name="attend_fwd",
    )(lens, tokens, wa, wa, wa, vec8)

def attend_bwd_kernel(lens_ref, q_ref, k_ref, v_ref, do_ref, lse_ref, tok_ref, dz_ref, wq_ref, wk_ref, wv_ref, dx_ref, dw_ref, small_ref,
                      dq_s, dk_s, dv_s, xt_s, dqt_s, acck, accv, lse_s):
    S = tok_ref.shape[0] // LMAX
    lane = lax.broadcasted_iota(jnp.int32, (LMAX, 128), 1)
    row = lax.broadcasted_iota(jnp.int32, (LMAX, 128), 0)
    one = jnp.ones((LMAX, 128), BF16); zero = jnp.zeros((LMAX, 128), BF16)
    xt_s[...] = tok_ref[...].T

    def task(t, _):
        sl = t // (HEADS // 2); j = t % (HEADS // 2)
        rs = pl.ds(pl.multiple_of(sl * LMAX, LMAX), LMAX)
        ls = pl.ds(pl.multiple_of(j * 128, 128), 128)
        bar = jnp.where(row < lens_ref[sl], 0.0, -1e30).astype(BF16)
        q2 = q_ref[rs, ls]; k2 = k_ref[rs, ls]; v2 = v_ref[rs, ls]; do2 = do_ref[rs, ls]
        kt = k2.T
        for e in range(2):
            other = 64 * (1 - e)
            mine = (lane >= 64) == (e == 1)
            ka = jnp.where(mine, k2, jnp.where(lane == other, bar, zero))
            va = jnp.where(mine, v2, zero)
            qa = jnp.where(lane == other, one, q2)
            lse_row = lse_ref[pl.ds(sl * 16 + 2*j + e, 1), :]
            for c in range(LMAX // QC):
                cs = slice(c*QC, (c+1)*QC)
                s = mm(ka, qa[cs], NT)
                p = jnp.exp(s - lse_row[:, cs])
                dp = mm(va, do2[cs], NT)
                pd = p * dp
                dsum = jnp.sum(pd, axis=0, keepdims=True)
                ds = (pd - p * dsum).astype(BF16)
                dvc = mm(p.astype(BF16), do2[cs])
                dkc = mm(ds, q2[cs])
                if c == 0:
                    dva, dka = dvc, dkc
                else:
                    dva, dka = dva + dvc, dka + dkc
                dqt_s[64*e:64*e+64, cs] = mm(kt[64*e:64*e+64], ds)
            if e == 0:
                accv[...] = dva; acck[...] = dka
            else:
                dv_s[rs, ls] = jnp.where(mine, dva, accv[...]).astype(BF16)
                dk_s[rs, ls] = jnp.where(mine, dka, acck[...]).astype(BF16)
        dq_s[rs, ls] = (dqt_s[...].T * 0.125).astype(BF16)
        return 0
    lax.fori_loop(0, S * (HEADS // 2), task, 0)
    small_ref[...] = jnp.zeros_like(small_ref)
    small_ref[0:1, :] = jnp.sum(dq_s[...].astype(F32), axis=0, keepdims=True)
    small_ref[1:2, :] = jnp.sum(dv_s[...].astype(F32), axis=0, keepdims=True)
    def rows(r, _):
        rr = pl.ds(pl.multiple_of(r * 256, 256), 256)
        dx_ref[rr, :] = dz_ref[rr, :] + mm(dq_s[rr, :], wq_ref[...], NT) + mm(dk_s[rr, :], wk_ref[...], NT) + mm(dv_s[rr, :], wv_ref[...], NT)
        return 0
    lax.fori_loop(0, S * LMAX // 256, rows, 0)
    for i, g in enumerate((dq_s, dk_s, dv_s)):
        def wg(r, _, g=g, i=i):
            rr = pl.ds(pl.multiple_of(r * 256, 256), 256)
            dw_ref[rr, i*D:(i+1)*D] = mm(xt_s[rr, :], g[...]).astype(BF16)
            return 0
        lax.fori_loop(0, D // 256, wg, 0)

def attend_bwd(q, k, v, do, lse, tokens, dz, wa, lens):
    T = tokens.shape[0]
    V = pl.BlockSpec(memory_space=pltpu.VMEM)
    w = lambda i: pl.BlockSpec((D, D), lambda s, l, i=i: (0, i))
    full = lambda a: pl.BlockSpec(a.shape, lambda s, l: (0, 0))
    o = lambda sh: pl.BlockSpec(sh, lambda s, l: (0, 0))
    return pl.pallas_call(
        attend_bwd_kernel,
        out_shape=[jax.ShapeDtypeStruct((T, D), F32), jax.ShapeDtypeStruct((D, 3*D), BF16), jax.ShapeDtypeStruct((8, D), F32)],
        grid_spec=pltpu.PrefetchScalarGridSpec(num_scalar_prefetch=1, grid=(1,),
            in_specs=[full(q)]*4 + [full(lse), full(tokens), full(dz), w(0), w(1), w(2)],
            out_specs=[o((T, D)), o((D, 3*D)), o((8, D))],
            scratch_shapes=[pltpu.VMEM((T, D), BF16)]*3 + [pltpu.VMEM((D, T), BF16), pltpu.VMEM((128, LMAX), F32), pltpu.VMEM((LMAX, 128), F32), pltpu.VMEM((LMAX, 128), F32), pltpu.VMEM((8, 128), F32)]),
        name="attend_bwd",
    )(lens, q, k, v, do, lse, tokens, dz, wa, wa, wa)


M = 256
NB = 768


def gelu_pair(u):
    phi = 0.5 * (1.0 + lax.erf(u * 0.7071067811865476))
    e = jnp.exp(-0.5 * (u * u))
    return u * phi, phi + u * (e * 0.3989422804014327)

def norm_stats(z):
    mean = jnp.mean(z, axis=-1, keepdims=True)
    c = z - mean
    var = jnp.mean(c * c, axis=-1, keepdims=True)
    r = lax.rsqrt(var + 1e-5)
    return c * r, r

def norm_back(dxh, xh, r):
    return r * (dxh - jnp.mean(dxh, axis=-1, keepdims=True) - xh * jnp.mean(dxh * xh, axis=-1, keepdims=True))

def colsum(x):
    return jnp.sum(x, axis=0, keepdims=True)

def ffn_kernel(tiles, lens_ref, o_ref, tok_ref, cot_ref, wa_h, wf_h, vec_ref, b1_ref,
               out_ref, dz_ref, do_ref, gf_ref, small_ref,
               wo_ref, w1_ref, w2_ref, gp_s, ot_s, da_s, ht_s, dft_s, g_s, du_s, sem):
    t = pl.program_id(0); per = LMAX // M
    live = [(lens_ref[u // per] > (u % per) * M).astype(jnp.int32) for u in range(tiles)]
    count = sum(live)
    loads = [pltpu.make_async_copy(wa_h.at[:, 3*D:4*D], wo_ref, sem.at[0]), pltpu.make_async_copy(wf_h.at[:, 0:FF], w1_ref, sem.at[1]), pltpu.make_async_copy(wf_h.at[:, FF:2*FF], w2_ref, sem.at[2])]
    def arrived(i):
        @pl.when(t == 0)
        def _(): loads[i].wait()

    @pl.when(t == 0)
    def _():
        for l in loads: l.start()
        small_ref[...] = jnp.zeros_like(small_ref)

    n = lens_ref[jnp.minimum(t, tiles - 1) // per] - (t % per) * M

    @pl.when((t < tiles) & (n <= 0))
    def _():
        for r in (out_ref, dz_ref, do_ref):
            r[...] = jnp.zeros_like(r)

    @pl.when((t < tiles) & (n > 0))
    def _():
        pos = sum(live[u] * (u < t).astype(jnp.int32) for u in range(tiles))
        rs = pl.ds(pl.multiple_of(pos * M, M), M)
        v = lambda i: vec_ref[i:i+1, :]
        o = o_ref[...]
        arrived(0)
        z1 = tok_ref[...].astype(F32) + (mm(o, wo_ref[...]) + v(2))
        ot_s[:, rs] = o.T
        xh1, r1 = norm_stats(z1)
        h = xh1 * v(3) + v(4)
        hb = h.astype(BF16)
        ht_s[:, rs] = hb.T
        arrived(1)
        arrived(2)
        f = None
        CF = 512
        cuts = [slice(c, c + CF) for c in range(0, FF, CF)]
        u = mm(hb, w1_ref[:, cuts[0]]) + b1_ref[:, cuts[0]]
        for j, cs in enumerate(cuts):
            nxt = mm(hb, w1_ref[:, cuts[j+1]]) + b1_ref[:, cuts[j+1]] if j + 1 < len(cuts) else None
            g, gp = gelu_pair(u)
            gb = g.astype(BF16)
            g_s[rs, cs] = gb
            gp_s[:, cs] = gp
            part = mm(gb, w2_ref[:, cs], NT)
            f = part if f is None else f + part
            u = nxt
        z2 = h + (f + v(5))
        xh2, r2 = norm_stats(z2)
        keep = lax.broadcasted_iota(jnp.int32, (M, 1), 0) < n
        out_ref[...] = jnp.where(keep, xh2 * v(6) + v(7), 0.0).astype(BF16)
        dy = jnp.where(keep, cot_ref[...].astype(F32), 0.0)
        small_ref[7:8, :] += colsum(dy)
        small_ref[6:7, :] += colsum(dy * xh2)
        dz2 = norm_back(dy * v(6), xh2, r2)
        df = dz2.astype(BF16)
        dft_s[:, rs] = df.T
        small_ref[5:6, :] += colsum(df.astype(F32))
        du = (gp_s[...] * mm(df, w2_ref[...])).astype(BF16)
        du_s[rs, :] = du
        db1 = colsum(du.astype(F32))
        for i in range(4):
            small_ref[8+i:9+i, :] += db1[:, i*D:(i+1)*D]
        dh = dz2 + mm(du, w1_ref[...], NT)
        small_ref[4:5, :] += colsum(dh)
        small_ref[3:4, :] += colsum(dh * xh1)
        dz1 = norm_back(dh * v(3), xh1, r1)
        da = dz1.astype(BF16)
        small_ref[2:3, :] += colsum(da.astype(F32))
        dz_ref[...] = dz1
        da_s[rs, :] = da
        do_ref[...] = mm(da, wo_ref[...], NT).astype(BF16)

    i = t - tiles
    half = FF // NB
    for kk in range(1, tiles + 1):
        K = kk*M
        for lt, r, c0, n0, n1 in ((ht_s, du_s, 0, 0, half), (dft_s, g_s, half, half, 2*half), (ot_s, da_s, 2*half, 2*half, 2*half + 1)):
            @pl.when((count == kk) & (i >= n0) & (i < n1))
            def _(lt=lt, r=r, K=K, c0=c0):
                cs = pl.ds(pl.multiple_of((i - c0) * NB, NB), NB)
                gf_ref[...] = mm(lt[:, :K], r[:K, cs]).astype(BF16)

def ffn(o, tokens, cot, wa, wf, vec8, b1, lens):
    T = tokens.shape[0]; tiles = T // M; chunks = 2*FF // NB + 1
    row = pl.BlockSpec((M, D), lambda t, l: (jnp.minimum(t, tiles - 1), 0))
    one = lambda sh: pl.BlockSpec(sh, lambda t, l: (0, 0))
    A = pl.BlockSpec(memory_space=pl.ANY)
    S = jax.ShapeDtypeStruct
    B = lambda *sh: pltpu.VMEM(sh, BF16)
    return pl.pallas_call(
        functools.partial(ffn_kernel, tiles),
        out_shape=[S((T, D), BF16), S((T, D), F32), S((T, D), BF16), S((D, chunks*NB), BF16), S((16, D), F32)],
        grid_spec=pltpu.PrefetchScalarGridSpec(num_scalar_prefetch=1, grid=(tiles + chunks,),
            in_specs=[row, row, row, A, A, one((8, D)), one((1, FF))],
            out_specs=[row, row, row, pl.BlockSpec((D, NB), lambda t, l: (0, jnp.maximum(t - tiles, 0))), one((16, D))],
            scratch_shapes=[B(D, D), B(D, FF), B(D, FF), pltpu.VMEM((M, FF), F32), B(D, T), B(T, D), B(D, T), B(D, T), B(T, FF), B(T, FF), pltpu.SemaphoreType.DMA((3,))]),
        compiler_params=pltpu.CompilerParams(vmem_limit_bytes=60 << 20),
        name="ffn",
    )(lens, o, tokens, cot, wa, wf, vec8, b1)


RATE = 1.0

class Spot:
    def __init__(self, na, ndp):
        self.na, self.ndp = na, ndp
        self.me = lax.axis_index("fsdp"); self.p = lax.axis_index("dp")
        self.a = self.me // 4; self.b = (self.me // 2) % 2; self.c = self.me % 2
        self.par = self.p % 2
        self.b2 = self.b + (1 - 2*self.b)*(1 - self.par); self.c2 = self.c + (1 - 2*self.c)*self.par
        self.b3 = self.b + (1 - 2*self.b)*self.par; self.c3 = self.c + (1 - 2*self.c)*(1 - self.par)

    def at(self, a, flip2=0, flip3=0):
        if flip2 and flip3:
            b, c = 1 - self.b, 1 - self.c
        elif flip2:
            b, c = self.b2, self.c2
        elif flip3:
            b, c = self.b3, self.c3
        else:
            b, c = self.b, self.c
        return (a*2 + b)*2 + c

    def dev(self, a, flip2=0, flip3=0):
        return (self.at(a, flip2, flip3), self.p)

    def barrier(self):
        sem = pltpu.get_barrier_semaphore()
        up, down = self.a < self.na - 1, self.a > 0
        def sig(dev):
            pl.semaphore_signal(sem, inc=1, device_id=dev, device_id_type=MESH)
        @pl.when(up)
        def _(): sig(self.dev(self.a + 1))
        @pl.when(down)
        def _(): sig(self.dev(self.a - 1))
        sig(self.dev(self.a, 1, 0)); sig(self.dev(self.a, 0, 1))
        for q in range(1, self.ndp): sig((self.me, (self.p + q) % self.ndp))
        pl.semaphore_wait(sem, 1 + self.ndp + up.astype(jnp.int32) + down.astype(jnp.int32))

class Gather:
    def __init__(self, spot, own, view, ssem, rsem, dp_view=None):
        self.s, self.own, self.view, self.ss, self.rs, self.dp_view = spot, own, view, ssem, rsem, dp_view
        na = spot.na
        self.JU, self.JD = 0, na - 1
        self.J2 = 2*(na - 1); self.J3 = self.J2 + na; self.JP = self.J3 + 2*na
        self.log = []

    @staticmethod
    def slots(na, ndp):
        return 2*(na - 1) + na + 2*na + (ndp - 1)*4*na

    def copy(self, f, dev, j, r=None, src=None):
        v = self.view(f)
        return pltpu.make_async_remote_copy(src_ref=v if src is None else src, dst_ref=v, send_sem=self.ss.at[j],
                                            recv_sem=self.rs.at[j if r is None else r], device_id=dev, device_id_type=MESH)

    def send(self, cond, make):
        make().start()
        self.log.append((cond, make))

    def wait(self, f, j):
        self.copy(f, (self.s.me, self.s.p), j).wait_recv()

    def dp(self, cond, f):
        if self.dp_view is None: return
        s = self.s
        for q in range(1, s.ndp):
            self.send(cond, lambda q=q: self.copy(f(), (s.me, (s.p + q) % s.ndp), self.JP + (q-1)*4*s.na + f()))

    def start(self):
        s = self.s; na = s.na
        up, down = s.a < na - 1, s.a > 0
        @pl.when(up)
        def _(): self.send(up, lambda: self.copy(s.me, s.dev(s.a + 1), self.JU, src=self.own))
        @pl.when(down)
        def _(): self.send(down, lambda: self.copy(s.me, s.dev(s.a - 1), self.JD, src=self.own))
        self.send(None, lambda: self.copy(s.me, s.dev(s.a, 1, 0), self.J2 + s.a, src=self.own))
        self.send(None, lambda: self.copy(s.me, s.dev(s.a, 0, 1), self.J3 + s.a*2, src=self.own))

    def events(self):
        s = self.s; na = s.na
        def chain(up, k):
            a = s.a - 1 - k if up else s.a + 1 + k
            cond = a >= 0 if up else a < na
            fwd = s.a < na - 1 if up else s.a > 0
            both = cond & fwd
            j = (self.JU if up else self.JD) + k
            def go():
                self.wait(s.at(a), j)
                if k < na - 2:
                    @pl.when(fwd)
                    def _(): self.send(both, lambda: self.copy(s.at(a), s.dev(s.a + 1 if up else s.a - 1), j + 1))
                self.send(cond, lambda: self.copy(s.at(a), s.dev(s.a, 1, 0), self.J2 + a))
                self.send(cond, lambda: self.copy(s.at(a), s.dev(s.a, 0, 1), self.J3 + a*2))
                self.dp(cond, lambda: s.at(a))
            return cond, go
        def second(a, cond):
            def go():
                self.wait(s.at(a, 1, 0), self.J2 + a)
                self.send(cond, lambda: self.copy(s.at(a, 1, 0), s.dev(s.a, 0, 1), self.J3 + a*2 + 1))
                self.dp(cond, lambda: s.at(a, 1, 0))
            return cond, go
        def third(a, cond, x):
            def go():
                self.wait(s.at(a, x, 1), self.J3 + a*2 + x)
                self.dp(cond, lambda: s.at(a, x, 1))
            return cond, go
        levels = [[(s.a, None)]]
        for k in range(na - 1):
            levels.append([(s.a - 1 - k, s.a - 1 - k >= 0), (s.a + 1 + k, s.a + 1 + k < na)])
        out = []
        for k in range(na + 2):
            if k < na - 1: out += [chain(True, k), chain(False, k)]
            if k < na:
                out += [second(a, cd) for a, cd in levels[k]]
                out += [third(a, cd, 0) for a, cd in levels[k]]
            if 0 < k <= na:
                out += [third(a, cd, 1) for a, cd in levels[k-1]]
        return out

    def finish(self):
        s = self.s
        if self.dp_view is not None:
            for q in range(1, s.ndp):
                def body(f, _):
                    @pl.when(f != s.me)
                    def _():
                        j = self.JP + (q-1)*4*s.na + f
                        v = self.dp_view(f, (s.p + s.ndp - q) % s.ndp)
                        pltpu.make_async_remote_copy(src_ref=v, dst_ref=v, send_sem=self.ss.at[j], recv_sem=self.rs.at[j], device_id=(s.me, s.p), device_id_type=MESH).wait_recv()
                    return 0
                lax.fori_loop(0, 4*s.na, body, 0)
        self.drain()

    def drain(self):
        for cond, make in self.log:
            if cond is None:
                make().wait_send()
            else:
                @pl.when(cond)
                def _(): make().wait_send()

def run_event(ev):
    cond, go = ev
    if cond is None: go()
    else: pl.when(cond)(go)

def forward_kernel(na, ndp, wa_sh, wf_h, vecs, bff, lens_ref, tok_h,
                   wa_out, wf_out, vec8, bias, q_h, k_h, v_h, o_h, lse_ref,
                   wa_c, wf_c, ex, wqkv, ot_s, wf_sh, tok_ref, q_ref, k_ref, v_ref, o_ref, lsem, *sems):
    s = Spot(na, ndp)
    R = wa_sh.shape[0]
    loads = [pltpu.make_async_copy(wf_h, wf_sh, lsem.at[3]), pltpu.make_async_copy(tok_h, tok_ref, lsem.at[4])]
    for l in loads: l.start()
    ex[s.me, 0:8, 0:R] = vecs[...].astype(BF16).astype(F32)
    for j in range(4):
        ex[s.me, 8+j:9+j, 0:R] = bff[0:1, j*R:(j+1)*R].astype(BF16).astype(F32)
    wa_c[...] = wa_sh[...].astype(BF16)
    gs = []
    for i, (c, out) in enumerate(((wa_c, wa_out), (wf_c, wf_out))):
        w = c.shape[1] // ndp
        cols = lambda q, w=w: pl.ds(pl.multiple_of(q*w, 128), w)
        gs.append(Gather(s, c.at[:, cols(s.p)], lambda f, out=out, cols=cols: out.at[f, :, cols(s.p)], sems[2*i], sems[2*i+1],
                         lambda f, q, out=out, cols=cols: out.at[f, :, cols(q)]))
    gx = Gather(s, ex.at[s.me], lambda f: ex.at[f], sems[4], sems[5])
    ga, gf = gs
    s.barrier()
    gx.start(); ga.start()
    locs = [pltpu.make_async_copy(wa_c, wa_out.at[s.me], lsem.at[0])]
    locs[0].start()
    loads[0].wait()
    wf_c[...] = wf_sh[...].astype(BF16)
    locs.append(pltpu.make_async_copy(wf_c, wf_out.at[s.me], lsem.at[1]))
    locs[1].start()
    ea, exv, ef = ga.events(), gx.events(), gf.events()
    gf.start()
    for u, v in zip(ea, exv):
        run_event(v); run_event(u)
    for q in range(1, ndp):
        def body(f, _, q=q):
            @pl.when(f != s.me)
            def _():
                j = ga.JP + (q-1)*4*na + f
                v = ga.dp_view(f, (s.p + ndp - q) % ndp)
                pltpu.make_async_remote_copy(src_ref=v, dst_ref=v, send_sem=ga.ss.at[j], recv_sem=ga.rs.at[j], device_id=(s.me, s.p), device_id_type=MESH).wait_recv()
            return 0
        lax.fori_loop(0, 4*na, body, 0)
    locs[0].wait()
    load = pltpu.make_async_copy(wa_out.at[:, :, 0:3*D], wqkv, lsem.at[2])
    load.start()
    for f in range(4*na):
        vec8[:, f*R:(f+1)*R] = ex[f, 0:8, 0:R]
        for j in range(4):
            bias[0:1, (f*4+j)*R:(f*4+j+1)*R] = ex[f, 8+j:9+j, 0:R]
    load.wait()
    loads[1].wait()
    S = tok_ref.shape[0] // LMAX
    lane = lax.broadcasted_iota(jnp.int32, (LMAX, 128), 1)
    row = lax.broadcasted_iota(jnp.int32, (LMAX, 128), 0)
    one = jnp.ones((LMAX, 128), BF16); zero = jnp.zeros((LMAX, 128), BF16)
    PAIRS = HEADS // 2
    ntask = S*(3 + PAIRS)
    cut = [min(len(ef), int(RATE*t)) for t in range(ntask + 1)]
    def events_after(i, first, last):
        for t in range(first, last):
            evs = ef[cut[t]:cut[t+1]]
            if evs:
                @pl.when(i == t)
                def _():
                    for e in evs: run_event(e)
    w3 = wqkv.shape
    def proj(sl, which):
        rs = pl.ds(pl.multiple_of(sl*LMAX, LMAX), LMAX)
        x = tok_ref[rs, :]
        y = mm(x, wqkv[:, :, which*D:(which+1)*D].reshape(4*na*R, D))
        if which == 0: q_ref[rs, :] = ((y + vec8[0:1, :]).astype(BF16) * 0.125).astype(BF16)
        elif which == 1: k_ref[rs, :] = y.astype(BF16)
        else: v_ref[rs, :] = (y + vec8[1:2, :]).astype(BF16)
    def step1(i, _):
        for which in range(3):
            @pl.when(i % 3 == which)
            def _(): proj(i // 3, which)
        events_after(i, 0, 3*S)
        return 0
    lax.fori_loop(0, 3*S, step1, 0)
    stores = [pltpu.make_async_copy(r, h, lsem.at[5 + i]) for i, (r, h) in enumerate(((q_ref, q_h), (k_ref, k_h), (v_ref, v_h), (o_ref, o_h)))]
    for c in stores[:3]: c.start()
    def step2(i, _):
        sl = i // PAIRS; j = i % PAIRS
        rs = pl.ds(pl.multiple_of(sl*LMAX, LMAX), LMAX)
        ls = pl.ds(pl.multiple_of(j * 128, 128), 128)
        bar = jnp.where(row < lens_ref[sl], 0.0, -1e30).astype(BF16)
        q2 = q_ref[rs, ls]; k2 = k_ref[rs, ls]
        vt = v_ref[rs, ls].T
        raw = []
        for e in range(2):
            other = 64 * (1 - e)
            ka = jnp.where((lane >= 64) == (e == 1), k2, jnp.where(lane == other, bar, zero))
            qa = jnp.where(lane == other, one, q2)
            raw.append(mm(ka, qa, NT))
        for e in range(2):
            top = jnp.max(raw[e], axis=0, keepdims=True)
            p = jnp.exp(raw[e] - top)
            tot = jnp.sum(p, axis=0, keepdims=True)
            ot_s[64*e:64*e+64, :] = mm(vt[64*e:64*e+64], p.astype(BF16)) / tot
            lse_ref[pl.ds(sl*16 + 2*j + e, 1), :] = top + jnp.log(tot)
        o_ref[rs, ls] = ot_s[...].T.astype(BF16)
        events_after(i + 3*S, 3*S, ntask)
        return 0
    lax.fori_loop(0, S*PAIRS, step2, 0)
    stores[3].start()
    for e in ef[cut[ntask]:]: run_event(e)
    gf.finish(); gx.finish()
    for c in stores: c.wait()
    ga.drain()
    locs[1].wait()

def forward(mesh_shape, wa_sh, wf_sh, vecs, bff, lens, tokens, cid):
    F, ndp = mesh_shape
    na = F // 4; R = vecs.shape[1]; T = tokens.shape[0]
    NS = Gather.slots(na, ndp)
    S = jax.ShapeDtypeStruct
    V = pl.BlockSpec(memory_space=pltpu.VMEM); A = pl.BlockSpec(memory_space=pl.ANY)
    DMA = pltpu.SemaphoreType.DMA
    return pl.pallas_call(
        functools.partial(forward_kernel, na, ndp),
        out_shape=[S((F, R, 4*D), BF16), S((F, R, 2*FF), BF16), S((8, D), F32), S((1, FF), F32)] + [S((T, D), BF16)]*4 + [S((T//LMAX*16, LMAX), F32)],
        in_specs=[V, A, V, V, pl.BlockSpec(memory_space=pltpu.SMEM), A],
        out_specs=[A, A, V, V, A, A, A, A, V],
        scratch_shapes=[pltpu.VMEM((R, 4*D), BF16), pltpu.VMEM((R, 2*FF), BF16), pltpu.VMEM((F, 16, 128), F32), pltpu.VMEM((F, R, 3*D), BF16),
                        pltpu.VMEM((128, LMAX), F32), pltpu.VMEM((R, 2*FF), F32)] + [pltpu.VMEM((T, D), BF16)]*5 + [DMA((9,))] + [DMA((NS,))]*6,
        compiler_params=pltpu.CompilerParams(collective_id=cid, has_side_effects=True, vmem_limit_bytes=56 << 20),
        name="gather_attend",
    )(wa_sh, wf_sh, vecs, bff, lens, tokens)


def as_int(cond):
    return cond.astype(jnp.int32)

class Reduce:
    def __init__(self, spot, src, mine, rd, r3, r2, cu, cd, ss, rs, out, load=None):
        self.s = spot
        self.src, self.mine = src, mine
        self.rd, self.r3, self.r2, self.cu, self.cd = rd, r3, r2, cu, cd
        self.ss, self.rs, self.out, self.load = ss, rs, out, load
        s = spot; na = s.na; F = 4*na
        self.B3 = (s.ndp - 1)*F; self.B2 = self.B3 + 2*na; self.BU = self.B2 + na; self.BD = self.BU + na; self.BO = self.BD + na
        self.log = []
        z = s.a; lower = as_int(z < na // 2)
        self.order = []
        for k in range(na):
            c1 = as_int(k < na - 1 - z); c2 = as_int(k < z)
            lo = c1*(na - 1 - k) + (1 - c1)*(k - (na - 1 - z))
            hi = c2*k + (1 - c2)*(na - 1 - (k - z))
            self.order.append(lower*lo + (1 - lower)*hi)
        self.bit2 = s.b*(1 - s.par) + s.c*s.par

    @staticmethod
    def slots(na, ndp):
        return (ndp - 1)*4*na + 5*na + ndp - 1

    def rc(self, src, dst, j, r, dev):
        return pltpu.make_async_remote_copy(src_ref=src, dst_ref=dst, send_sem=self.ss.at[j], recv_sem=self.rs.at[r], device_id=dev, device_id_type=MESH)

    def send(self, cond, make):
        make().start()
        self.log.append((cond, make))

    def wait(self, dst, r):
        self.rc(dst, dst, r, r, (self.s.me, self.s.p)).wait_recv()

    def start(self):
        s = self.s; na = s.na
        if self.load is not None:
            for y3, y2 in ((1, 1), (1, 0), (0, 1), (0, 0)):
                for k in range(na): self.load(s.at(self.order[k], y2, y3)).start()
        for y3, y2 in ((1, 1), (1, 0), (0, 1), (0, 0)):
            for k in range(na):
                for q in range(1, s.ndp):
                    x2, x3 = (y2, y3) if q % 2 == 0 else (y3, y2)
                    f = s.at(self.order[k], x2, x3)
                    dq = (s.p + q) % s.ndp
                    self.send(None, lambda f=f, q=q, dq=dq: self.rc(self.src(f, dq), self.rd.at[q-1, f], (q-1)*4*na + f, (q-1)*4*na + f, (s.me, dq)))

    def add(self, f, srcs, dst=None):
        s = self.s
        for q in range(1, s.ndp):
            self.wait(self.rd.at[q-1, f], (q-1)*4*s.na + f)
        if self.load is not None: self.load(f).wait()
        own = self.mine(f)
        dst = own if dst is None else dst
        srcs = [self.rd.at[q-1, f] for q in range(1, s.ndp)] + srcs
        w = own.shape[-1]
        CH = next(c for c in (512, 384, 256, 128) if w % c == 0)
        def body(j, _):
            cs = pl.ds(pl.multiple_of(j*CH, 128), CH)
            v = own[:, cs].astype(F32)
            for r in srcs: v = v + r[:, cs].astype(F32)
            dst[:, cs] = v.astype(dst.dtype)
            return 0
        lax.fori_loop(0, w // CH, body, 0)

    def events(self):
        s = self.s; na = s.na
        out = []
        for x2 in (1, 0):
            for k in range(na):
                def go(x2=x2, k=k):
                    a = self.order[k]; f = lambda: s.at(a, x2, 1)
                    slot = lambda: a*2 + self.bit2 + (1 - 2*self.bit2)*x2
                    self.add(f(), [])
                    self.send(None, lambda: self.rc(self.mine(f()), self.r3.at[slot()], self.B3 + slot(), self.B3 + slot(), s.dev(s.a, 0, 1)))
                out.append((None, go))
        for k in range(na):
            def go(k=k):
                a = self.order[k]; f = lambda: s.at(a, 1, 0)
                slot = a*2 + 1 - self.bit2
                self.wait(self.r3.at[slot], self.B3 + slot)
                self.add(f(), [self.r3.at[slot]])
                self.send(None, lambda: self.rc(self.mine(f()), self.r2.at[a], self.B2 + a, self.B2 + a, s.dev(s.a, 1, 0)))
            out.append((None, go))
        for k in range(na - 1, 0, -1):
            for up in (True, False):
                a = s.a + k if up else s.a - k
                cond = a < na if up else a >= 0
                more = s.a > 0 if up else s.a < na - 1
                buf, B = (self.cu, self.BU) if up else (self.cd, self.BD)
                def go(a=a, cond=cond, more=more, buf=buf, B=B, up=up):
                    slot = a*2 + self.bit2
                    f = lambda: s.at(a)
                    self.wait(self.r3.at[slot], self.B3 + slot)
                    self.wait(self.r2.at[a], self.B2 + a)
                    base = [self.r3.at[slot], self.r2.at[a]]
                    @pl.when(more)
                    def _():
                        self.wait(buf.at[a], B + a)
                        self.add(f(), base + [buf.at[a]])
                    @pl.when(jnp.logical_not(more))
                    def _(): self.add(f(), base)
                    self.send(cond, lambda: self.rc(self.mine(f()), buf.at[a], B + a, B + a, s.dev(s.a + 1 if up else s.a - 1)))
                out.append((cond, go))
        def last():
            a = s.a; slot = a*2 + self.bit2
            self.wait(self.r3.at[slot], self.B3 + slot)
            self.wait(self.r2.at[a], self.B2 + a)
            base = [self.r3.at[slot], self.r2.at[a]]
            dst = self.out(s.p)
            @pl.when(a == 0)
            def _():
                self.wait(self.cd.at[a], self.BD + a)
                self.add(s.me, base + [self.cd.at[a]], dst)
            @pl.when(a == na - 1)
            def _():
                self.wait(self.cu.at[a], self.BU + a)
                self.add(s.me, base + [self.cu.at[a]], dst)
            @pl.when((a > 0) & (a < na - 1))
            def _():
                self.wait(self.cd.at[a], self.BD + a)
                self.wait(self.cu.at[a], self.BU + a)
                self.add(s.me, base + [self.cd.at[a], self.cu.at[a]], dst)
            for q in range(1, s.ndp):
                self.send(None, lambda q=q: self.rc(self.out(s.p), self.out(s.p), self.BO + q - 1, self.BO + q - 1, (s.me, (s.p + q) % s.ndp)))
        out.append((None, last))
        return out

    def finish(self):
        s = self.s
        for q in range(1, s.ndp):
            self.wait(self.out((s.p + s.ndp - q) % s.ndp), self.BO + q - 1)
        for cond, make in self.log:
            if cond is None: make().wait_send()
            else:
                @pl.when(cond)
                def _(): make().wait_send()

    @staticmethod
    def scratch(na, ndp, R, w):
        F = 4*na
        B = lambda *sh: pltpu.VMEM(sh + (R, w), BF16)
        NS = Reduce.slots(na, ndp)
        return [B(ndp - 1, F), B(2*na), B(na), B(na), B(na), pltpu.SemaphoreType.DMA((NS,)), pltpu.SemaphoreType.DMA((NS,))]

class SmallSum:
    def __init__(self, spot, buf, got, ss, rs):
        self.s, self.buf, self.got, self.ss, self.rs = spot, buf, got, ss, rs
        self.sent = []

    @staticmethod
    def scratch(na, ndp, shape):
        NX = ndp + 1 + na - 1
        return [pltpu.VMEM((4,) + shape, F32), pltpu.VMEM((NX,) + shape, F32), pltpu.SemaphoreType.DMA((NX,)), pltpu.SemaphoreType.DMA((NX,))]

    def go(self, i, j, dev):
        d = pltpu.make_async_remote_copy(src_ref=self.buf.at[i], dst_ref=self.got.at[j], send_sem=self.ss.at[j], recv_sem=self.rs.at[j], device_id=dev, device_id_type=MESH)
        d.start(); self.sent.append(d)

    def wait(self, j):
        pltpu.make_async_remote_copy(src_ref=self.got.at[j], dst_ref=self.got.at[j], send_sem=self.ss.at[j], recv_sem=self.rs.at[j], device_id=(self.s.me, self.s.p), device_id_type=MESH).wait_recv()

    def ordered(self, i, here, n, j0):
        def pick(m):
            v = self.buf[i]
            for q in range(1, n):
                v = jnp.where((here + n - q) % n == m, self.got[j0 + q - 1], v)
            return v
        v = pick(0)
        for m in range(1, n): v = v + pick(m)
        return v

    def start(self):
        s = self.s
        for q in range(1, s.ndp): self.go(0, q - 1, (s.me, (s.p + q) % s.ndp))

    def steps(self, out):
        s = self.s; X = s.ndp - 1
        def one():
            for q in range(1, s.ndp): self.wait(q - 1)
            self.buf[1] = self.ordered(0, s.p, s.ndp, 0)
            self.go(1, X, ((s.a*2 + s.b)*2 + 1 - s.c, s.p))
        def two():
            self.wait(X)
            self.buf[2] = self.buf[1] + self.got[X]
            self.go(2, X + 1, ((s.a*2 + 1 - s.b)*2 + s.c, s.p))
        def three():
            self.wait(X + 1)
            self.buf[3] = self.buf[2] + self.got[X + 1]
            for k in range(1, s.na): self.go(3, X + 1 + k, s.dev((s.a + k) % s.na))
        def four():
            for k in range(1, s.na): self.wait(X + 1 + k)
            out[...] = self.ordered(3, s.a, s.na, X + 2)
        return [one, two, three, four]

    def finish(self):
        for d in self.sent: d.wait_send()

def barrier_full(s):
    sem = pltpu.get_barrier_semaphore()
    def sig(dev): pl.semaphore_signal(sem, inc=1, device_id=dev, device_id_type=MESH)
    for k in range(1, s.na): sig(s.dev((s.a + k) % s.na))
    sig(s.dev(s.a, 1, 0)); sig(s.dev(s.a, 0, 1))
    for q in range(1, s.ndp): sig((s.me, (s.p + q) % s.ndp))
    pl.semaphore_wait(sem, s.na + s.ndp)

def backward_kernel(na, ndp, lens_ref, q_h, k_h, v_h, do_h, lse_ref, tok_h, dz_h, wa_h, gf_h, small_in,
                    dx_h, of_ref, oq_ref, small_out,
                    q_ref, k_ref, v_ref, do_ref, tok_ref, wqkv, g_s, xt_s, dqt_s, wg, ownf, dx_ref, lsem, fsem, *sc):
    s = Spot(na, ndp)
    R = gf_h.shape[1]; T = tok_ref.shape[0]; S = T // LMAX
    PAIRS = HEADS // 2
    loads = []
    for i, (h, r) in enumerate(((q_h, q_ref), (k_h, k_ref), (v_h, v_ref), (do_h, do_ref))):
        loads.append(pltpu.make_async_copy(h, r, lsem.at[i]))
    late = [pltpu.make_async_copy(tok_h, tok_ref, lsem.at[4]), pltpu.make_async_copy(wa_h.at[:, :, 0:3*D], wqkv, lsem.at[5]), pltpu.make_async_copy(dz_h, dx_ref, lsem.at[6])]
    wf = gf_h.shape[2] // ndp; wq = wg.shape[2] // ndp
    def cols(q, w): return pl.ds(pl.multiple_of(q*w, 128), w)
    cf = lambda f: pltpu.make_async_copy(gf_h.at[f, :, cols(s.p, wf)], ownf.at[f], fsem.at[f])
    rf = Reduce(s, lambda f, q: gf_h.at[f, :, cols(q, wf)], lambda f: ownf.at[f], *sc[0:7], lambda q: of_ref.at[:, cols(q, wf)], cf)
    rq = Reduce(s, lambda f, q: wg.at[f, :, cols(q, wq)], lambda f: wg.at[f, :, cols(s.p, wq)], *sc[7:14], lambda q: oq_ref.at[:, cols(q, wq)])
    xs = SmallSum(s, *sc[14:18])
    barrier_full(s)
    rf.start()
    for l in loads + late: l.start()
    both = rf.events()
    ntask = S*PAIRS
    n3, n2 = 2*na, na
    plan = [[] for _ in range(ntask)]
    quick, half = max(1, ntask // 4), ntask // 2
    for i, e in enumerate(both[:n3 + n2]):
        t = i*quick // n3 if i < n3 else half + (i - n3)*(ntask - half) // n2
        plan[t].append(e)
    chain_f, last_f = both[n3 + n2:-1], both[-1]

    lane = lax.broadcasted_iota(jnp.int32, (LMAX, 128), 1)
    row = lax.broadcasted_iota(jnp.int32, (LMAX, 128), 0)
    one = jnp.ones((LMAX, 128), BF16); zero = jnp.zeros((LMAX, 128), BF16)
    for l in loads: l.wait()
    def task(t, _):
        sl = t // PAIRS; j = t % PAIRS
        rs = pl.ds(pl.multiple_of(sl * LMAX, LMAX), LMAX)
        ls = pl.ds(pl.multiple_of(j * 128, 128), 128)
        bar = jnp.where(row < lens_ref[sl], 0.0, -1e30).astype(BF16)
        q2 = q_ref[rs, ls]; k2 = k_ref[rs, ls]; v2 = v_ref[rs, ls]; do2 = do_ref[rs, ls]
        kt = k2.T
        raw, dps = [], []
        for e in range(2):
            other = 64 * (1 - e)
            mine = (lane >= 64) == (e == 1)
            ka = jnp.where(mine, k2, jnp.where(lane == other, bar, zero))
            va = jnp.where(mine, v2, zero)
            qa = jnp.where(lane == other, one, q2)
            raw.append(mm(ka, qa, NT)); dps.append(mm(va, do2, NT))
        dvs, dks = [], []
        for e in range(2):
            p = jnp.exp(raw[e] - lse_ref[pl.ds(sl * 16 + 2*j + e, 1), :])
            pd = p * dps[e]
            ds = (pd - p * jnp.sum(pd, axis=0, keepdims=True)).astype(BF16)
            dvs.append(mm(p.astype(BF16), do2)); dks.append(mm(ds, q2))
            dqt_s[64*e:64*e+64, :] = mm(kt[64*e:64*e+64], ds)
        g_s[rs, pl.ds(pl.multiple_of(2*D + j*128, 128), 128)] = jnp.where(lane >= 64, dvs[1], dvs[0]).astype(BF16)
        g_s[rs, pl.ds(pl.multiple_of(D + j*128, 128), 128)] = jnp.where(lane >= 64, dks[1], dks[0]).astype(BF16)
        g_s[rs, ls] = (dqt_s[...].T * 0.125).astype(BF16)
        for n in range(ntask):
            if plan[n]:
                @pl.when(t == n)
                def _():
                    for e in plan[n]: run_event(e)
        return 0
    lax.fori_loop(0, ntask, task, 0)
    late[0].wait()
    xt_s[...] = tok_ref[...].T
    if wg.shape[2] > 3*D: wg[:, :, 3*D:] = jnp.zeros(wg.shape[:2] + (wg.shape[2] - 3*D,), BF16)
    def wgr(r, _):
        cs = pl.ds(pl.multiple_of(r * 256, 256), 256)
        wg[:, :, cs] = mm(xt_s[...], g_s[:, cs]).reshape(4*na, R, 256).astype(BF16)
        return 0
    lax.fori_loop(0, 3*D // 256, wgr, 0)
    rq.start()
    xs.buf[0] = small_in[...]
    xs.buf[0, 0:1, :] = jnp.sum(g_s[:, 0:D].astype(F32), axis=0, keepdims=True)
    xs.buf[0, 1:2, :] = jnp.sum(g_s[:, 2*D:3*D].astype(F32), axis=0, keepdims=True)
    xs.start()
    eq = rq.events(); small = xs.steps(small_out)
    for e in eq[:n3]: run_event(e)
    late[1].wait(); late[2].wait()
    def rows(r):
        rr = slice(r*256, (r+1)*256)
        dx_ref[rr, :] += mm(g_s[rr, :], wqkv[...].reshape(D, 3*D), NT)
    steps = [lambda r=r: rows(r) for r in range(T // 256)]
    chain_q = eq[n3 + n2:-1]
    dx_out = pltpu.make_async_copy(dx_ref, dx_h, lsem.at[7])
    small[0]()
    for e in chain_f: run_event(e)
    run_event(last_f)
    small[1]()
    for f in steps[:1]: f()
    for e in eq[n3:n3 + n2]: run_event(e)
    small[2]()
    rest = steps[1:]
    gap = -(-len(chain_q) // (len(rest) + 1))
    for i in range(len(rest) + 1):
        for e in chain_q[i*gap:(i+1)*gap]: run_event(e)
        if i < len(rest): rest[i]()
        if i == len(rest) - 1: dx_out.start()
    small[3]()
    run_event(eq[-1])
    dx_out.wait()
    rf.finish(); rq.finish(); xs.finish()

def backward(mesh_shape, lens, q, k, v, do, lse, tokens, dz, wa3, gf, small, cid):
    F, ndp = mesh_shape
    na = F // 4; R = gf.shape[1]; T = tokens.shape[0]
    S = jax.ShapeDtypeStruct
    V = pl.BlockSpec(memory_space=pltpu.VMEM); A = pl.BlockSpec(memory_space=pl.ANY)
    up = lambda n: -(-n // (128*ndp)) * 128*ndp
    CQ = up(3*D)
    B = lambda *sh: pltpu.VMEM(sh, BF16)
    return pl.pallas_call(
        functools.partial(backward_kernel, na, ndp),
        out_shape=[S((T, D), F32), S((R, gf.shape[2]), F32), S((R, CQ), F32), S(small.shape, F32)],
        in_specs=[pl.BlockSpec(memory_space=pltpu.SMEM), A, A, A, A, V, A, A, A, A, V],
        out_specs=[A, V, V, V],
        scratch_shapes=[B(T, D)]*5 + [B(F, R, 3*D)] + [B(T, 3*D), B(D, T), pltpu.VMEM((128, LMAX), F32),
                        B(F, R, CQ), B(F, R, gf.shape[2]//ndp), pltpu.VMEM((T, D), F32), pltpu.SemaphoreType.DMA((8,)), pltpu.SemaphoreType.DMA((F,))]
                       + Reduce.scratch(na, ndp, R, gf.shape[2]//ndp) + Reduce.scratch(na, ndp, R, CQ//ndp)
                       + SmallSum.scratch(na, ndp, small.shape),
        compiler_params=pltpu.CompilerParams(collective_id=cid, has_side_effects=True, vmem_limit_bytes=60 << 20),
        name="reduce_attend",
    )(lens, q, k, v, do, lse, tokens, dz, wa3, gf, small)


STEPS = 4

def adam(g, m, v, w, fix1, fix2, rate):
    m_new = 0.9 * m + 0.1 * g
    v_new = 0.98 * v + 0.02 * g * g
    w_new = w - rate * ((m_new * fix1) / (jnp.sqrt(v_new * fix2) + 1e-06) + 0.01 * w)
    return m_new, v_new, w_new

def update_kernel(step_ref, rate_ref, gq_ref, go_ref, gf_ref, small_ref, dx_ref,
                  aw, am, av, fw, fm, fv, vw, vm, vv, bw, bm, bv, dxo, *outs):
    i = pl.program_id(0)
    count = jnp.full((8, 128), step_ref[0], jnp.int32).astype(F32)
    fix1 = (1.0 / (1.0 - jnp.exp(count * -0.10536051565782628)))[0:1, 0:1]
    fix2 = (1.0 / (1.0 - jnp.exp(count * -0.020202707317519466)))[0:1, 0:1]
    rate = rate_ref[0]

    def put(g, m, v, w, o):
        a, b, c = adam(g, m[...], v[...], w[...], fix1, fix2, rate)
        o[0][...] = g; o[1][...] = a; o[2][...] = b; o[3][...] = c; o[4][...] = c.astype(BF16)

    dxo[...] = dx_ref[...]
    put(gf_ref[...], fm, fv, fw, outs[5:10])
    cut = 3*D // (4*D // STEPS)
    @pl.when(i < cut)
    def _(): put(gq_ref[...], am, av, aw, outs[0:5])
    @pl.when(i >= cut)
    def _(): put(go_ref[...], am, av, aw, outs[0:5])

    @pl.when(i == 0)
    def _():
        R = vw.shape[1]
        f = lax.axis_index("fsdp")
        g = pltpu.roll(small_ref[0:8, :], lax.rem(D - f*R, D), 1)[:, 0:R]
        put(g, vm, vv, vw, outs[10:15])
        at = f*4*R
        x = pltpu.roll(small_ref[8:16, :], lax.rem(D - lax.rem(at, D), D), 1)
        here = lax.broadcasted_iota(jnp.int32, (8, D), 0) == at // D
        put(jnp.sum(jnp.where(here, x, 0.0), axis=0, keepdims=True)[:, 0:4*R], bm, bv, bw, outs[15:20])

def update(adam_step, learn_rate, gq, gall, small, dx, attn, ffn_, vecs, bff):
    R = vecs[0].shape[1]; T = dx.shape[0]
    ca, cf = 4*D // STEPS, 2*FF // STEPS
    cut = 3*D // ca
    blk = lambda w, fn=lambda i: i: pl.BlockSpec((R, w), lambda i, fn=fn: (0, fn(i)))
    one = lambda a: pl.BlockSpec(a.shape, lambda i: (0, 0))
    SM = pl.BlockSpec(memory_space=pltpu.SMEM)
    row = pl.BlockSpec((T // STEPS, D), lambda i: (i, 0))
    S = jax.ShapeDtypeStruct
    five = lambda sh: [S(sh, F32)]*4 + [S(sh, BF16)]
    tiny = lambda sh: [pl.BlockSpec(sh, lambda i: (0, 0))]*5
    return pl.pallas_call(
        update_kernel,
        grid=(STEPS,),
        out_shape=[S((T, D), F32)] + five((R, 4*D)) + five((R, 2*FF)) + five((8, R)) + five((1, 4*R)),
        in_specs=[SM, SM, blk(ca, lambda i: jnp.minimum(i, cut - 1)), blk(ca, lambda i: 2*FF // ca + jnp.maximum(i - cut, 0)), blk(cf), one(small), row]
                 + [blk(ca)]*3 + [blk(cf)]*3 + [one(v) for v in vecs] + [one(b) for b in bff],
        out_specs=[row] + [blk(ca)]*5 + [blk(cf)]*5 + tiny((8, R)) + tiny((1, 4*R)),
        name="update",
    )(adam_step, learn_rate, gq, gall, gall, small, dx, *attn, *ffn_, *vecs, *bff)


def local(mesh_shape, tokens, cotangent, lengths, adam_step, learn_rate, attn_w, attn_m, attn_v, ffn_w, ffn_m, ffn_v,
          vecs, vecs_m, vecs_v, b_ff, bff_m, bff_v):
    shards, rows = mesh_shape[0], vecs.shape[0]
    T = tokens.shape[0]
    attn_low, ffn_low, vec8, bias, q, k, v, o, lse = forward(
        mesh_shape, attn_w, ffn_w, vecs.T, b_ff.reshape(1, 4 * rows), lengths, tokens, 1)
    attn_low = attn_low.reshape(D, 4 * D)
    ffn_low = ffn_low.reshape(D, 2 * FF)
    outputs, dz1, do, grads, small_ffn = ffn(o, tokens, cotangent, attn_low, ffn_low, vec8, bias, lengths)
    grads = jnp.pad(grads, ((0, 0), (0, -grads.shape[1] % (128 * mesh_shape[1]))))
    input_grad, summed, summed_qkv, summed_small = backward(
        mesh_shape, lengths, q, k, v, do, lse, tokens, dz1, attn_low.reshape(shards, rows, 4 * D),
        grads.reshape(shards, rows, grads.shape[1]), small_ffn, 2)
    line = lambda x: x.reshape(1, 4 * rows)
    new = update(adam_step, learn_rate, summed_qkv, summed, summed_small, input_grad, (attn_w, attn_m, attn_v),
                 (ffn_w, ffn_m, ffn_v), (vecs.T, vecs_m.T, vecs_v.T), (line(b_ff), line(bff_m), line(bff_v)))
    return (outputs, new[0], *new[1:11], *[x.T for x in new[11:16]], *[x.reshape(4 * rows) for x in new[16:21]])


def solution(mesh):
    both, rows, whole = P(("fsdp", "dp")), P("fsdp"), P()
    return jax.shard_map(
        functools.partial(local, (mesh.shape["fsdp"], mesh.shape["dp"])),
        mesh=mesh,
        in_specs=(both, both, both, whole, whole) + (rows,) * 12,
        out_specs=(both, both) + (rows,) * 20,
        check_vma=False,
    )
```
